128 devices in a mesh: lon: 16 (over z_hi, y, core), lat: 8 (over x, z_lo).
Axes of the slice: x: 4, y: 4, z: 4 (z_hi: 2, z_lo: 2; z = z_hi * 2 + z_lo), core: 2. Of those that a mesh axis runs over, the one named last changes fastest.
Arguments:
- temp: float32 [4, 512, 12288], P(None, 'lat', 'lon'), may hold values from -6 to 6
- salt: float32 [4, 512, 12288], P(None, 'lat', 'lon'), may hold values from -6 to 6
- uvel: float32 [4, 512, 12288], P(None, 'lat', 'lon'), may hold values from -6 to 6
- vvel: float32 [4, 512, 12288], P(None, 'lat', 'lon'), may hold values from -6 to 6
- thick: float32 [4, 512, 12288], P(None, 'lat', 'lon'), may hold values from 0.5 to 2
- land: int32 [4, 512, 12288], P(None, 'lat', 'lon'), may hold values 0 or 1
- east_width: float32 [512, 12288], P('lat', 'lon'), may hold values from 0.5 to 2
- north_width: float32 [512, 12288], P('lat', 'lon'), may hold values from 0.5 to 2
- coriolis: float32 [512, 12288], P('lat', 'lon'), may hold values from 0.5 to 1.5
Outputs:
- temp_next: float32 [4, 512, 12288], P(None, 'lat', 'lon')
- salt_next: float32 [4, 512, 12288], P(None, 'lat', 'lon')
- uvel_next: float32 [4, 512, 12288], P(None, 'lat', 'lon')
- vvel_next: float32 [4, 512, 12288], P(None, 'lat', 'lon')
The draws below stay inside these ranges and needn't reach their ends.
All inputs are finite; a program needn't handle non-finite values. No bound on the sum of `land` on one device may be relied on, other than what follows from the above.
Results may differ from the reference program's by a relative error of at most 0.00002.
Values sent between devices are 32-bit elements; how exact they have to be, the bound alone decides.
No kernel may reach another device: no remote copies, remote signals or barrier semaphores. Data moves between devices by JAX's collectives and lax.ppermute only.
A program may use at most 128 MiB of HBM per device.

```python
import math
import jax
import jax.numpy as jnp

LEV = 4
NLAT = 512
NLON = 12288


def place_ends(values, own_key, smallest, largest):
    place = [jax.random.randint(jax.random.fold_in(own_key, axis), (), 0, length) for axis, length in enumerate(values.shape)]
    main_axis = values.shape.index(max(values.shape))
    beside = place[:main_axis] + [(place[main_axis] + 1) % values.shape[main_axis]] + place[main_axis + 1:]
    return values.at[tuple(place)].set(smallest).at[tuple(beside)].set(largest)


def block_levels(own_key, dims, pieces, smallest, top_value):
    def one(axis_at, blocks):
        heights = jax.random.uniform(jax.random.fold_in(jax.random.fold_in(own_key, 6), axis_at), (blocks,), jnp.float32, smallest / len(pieces), top_value / len(pieces))
        return jnp.repeat(jnp.exp(heights), dims[axis_at] // blocks).reshape((-1,) + (1,) * (len(dims) - axis_at - 1))

    gain = one(*pieces[0])
    for cut in pieces[1:]:
        gain = gain * one(*cut)
    return gain


def scatter_about(rng, dims, spread, bound, split=(), dtype=jnp.bfloat16):
    drawn = spread * jax.random.normal(rng, dims, jnp.float32)
    if split:
        drawn = drawn * block_levels(rng, dims, split, -0.22, 0.18)
    return jnp.clip(drawn, -bound, bound).astype(dtype)


def setup_inputs(seed: int = 0) -> dict:
    key_of = jax.random.split(jax.random.key(seed), 10)
    return {
        "temp": scatter_about(key_of[0], (LEV, NLAT, NLON), 1.0, 6.0, ((1, 8), (2, 16)), jnp.float32),
        "salt": scatter_about(key_of[1], (LEV, NLAT, NLON), 1.0, 6.0, ((1, 8), (2, 16)), jnp.float32),
        "uvel": scatter_about(key_of[2], (LEV, NLAT, NLON), 1.0, 6.0, ((1, 8), (2, 16)), jnp.float32),
        "vvel": scatter_about(key_of[3], (LEV, NLAT, NLON), 1.0, 6.0, ((1, 8), (2, 16)), jnp.float32),
        "thick": jnp.clip(jnp.exp(math.log(2.0) - 1.3862944 * jax.random.uniform(key_of[4], (LEV, NLAT, NLON), jnp.float32) ** block_levels(key_of[4], (LEV, NLAT, NLON), ((1, 8), (2, 16)), -0.2, 0.2)), 0.5, 2.0),
        "land": place_ends((jax.random.randint(key_of[5], (LEV, NLAT, NLON), 0, 4) < 3).astype(jnp.int32), jax.random.fold_in(key_of[5], 1), 0, 1),
        "east_width": jnp.clip(jnp.exp(math.log(2.0) - 1.3862944 * jax.random.uniform(key_of[6], (NLAT, NLON), jnp.float32) ** block_levels(key_of[6], (NLAT, NLON), ((0, 8), (1, 16)), -0.2, 0.2)), 0.5, 2.0),
        "north_width": jnp.clip(jnp.exp(math.log(2.0) - 1.3862944 * jax.random.uniform(key_of[7], (NLAT, NLON), jnp.float32) ** block_levels(key_of[7], (NLAT, NLON), ((0, 8), (1, 16)), -0.2, 0.2)), 0.5, 2.0),
        "coriolis": jnp.clip(0.5 + 1.0 * jax.random.uniform(key_of[8], (NLAT, NLON), jnp.float32) ** block_levels(key_of[8], (NLAT, NLON), ((0, 8), (1, 16)), -0.2, 0.2), 0.5, 1.5),
    }


time_step = 0.2
biharm_coef = 0.02
alpha_temp = 0.2
beta_salt = 0.8
thin_floor = 0.25


def laplace(field, east_coef, north_coef, volume):
    east_diff = east_coef * (field[..., 1:] - field[..., :-1])
    north_diff = north_coef * (field[..., 1:, :] - field[..., :-1, :])
    return (east_diff[..., 1:-1, 1:] - east_diff[..., 1:-1, :-1] + north_diff[..., 1:, 1:-1] - north_diff[..., :-1, 1:-1]) / volume


def advance_level(fields, depth_ext, east_ext, north_ext, overhead, wet_cells, coriolis, east_width, north_width):
    lon_thick = jnp.minimum(depth_ext[:, :-1], depth_ext[:, 1:])
    lat_thick = jnp.minimum(depth_ext[:-1], depth_ext[1:])
    east_coef = lon_thick * (north_ext[:, :-1] + north_ext[:, 1:]) / (east_ext[:, :-1] + east_ext[:, 1:])
    north_coef = lat_thick * (east_ext[:-1] + east_ext[1:]) / (north_ext[:-1] + north_ext[1:])
    volume = east_ext * north_ext * jnp.maximum(depth_ext, thin_floor)
    cycle_lap = laplace(fields, east_coef, north_coef, volume[1:-1, 1:-1])
    biharmonic = laplace(cycle_lap, east_coef[1:-1, 1:-1], north_coef[1:-1, 1:-1], volume[2:-2, 2:-2])
    transport_east = lon_thick * (north_ext[:, :-1] + north_ext[:, 1:]) * (fields[2][:, :-1] + fields[2][:, 1:]) / 4.0
    transport_north = lat_thick * (east_ext[:-1] + east_ext[1:]) * (fields[3][:-1] + fields[3][1:]) / 4.0
    tracers = fields[:2]
    flux_east = transport_east * (tracers[..., :-1] + tracers[..., 1:]) / 2.0
    flux_north = transport_north * (tracers[..., :-1, :] + tracers[..., 1:, :]) / 2.0
    advect = (flux_east[..., 2:-2, 2:-1] - flux_east[..., 2:-2, 1:-2] + flux_north[..., 2:-1, 2:-2] - flux_north[..., 1:-2, 2:-2]) / volume[2:-2, 2:-2]
    buoyancy = (beta_salt * fields[1] - alpha_temp * fields[0]) * depth_ext
    pressure = overhead + 0.5 * buoyancy
    overhead = overhead + buoyancy
    grad_east = (pressure[2:-2, 3:-1] - pressure[2:-2, 1:-3]) / (2.0 * east_width)
    grad_north = (pressure[3:-1, 2:-2] - pressure[1:-3, 2:-2]) / (2.0 * north_width)
    interior = fields[:, 2:-2, 2:-2]
    temp_out = wet_cells * (interior[0] - time_step * advect[0] - biharm_coef * biharmonic[0])
    salt_out = wet_cells * (interior[1] - time_step * advect[1] - biharm_coef * biharmonic[1])
    uvel_out = wet_cells * (interior[2] + time_step * (coriolis * interior[3] - grad_east) - biharm_coef * biharmonic[2])
    vvel_out = wet_cells * (interior[3] + time_step * (-coriolis * interior[2] - grad_north) - biharm_coef * biharmonic[3])
    return (temp_out, salt_out, uvel_out, vvel_out), overhead


def extend_global(stacked, sign_list):
    mirror = stacked[:, -3:, ::-1] * sign_list[:, None, None]
    ghost_rows = jnp.stack([mirror[:, 1], mirror[:, 0]], axis=1)
    rim_fill = jnp.array([0.0, 0.0, 0.0, 0.0, 0.0, 1.0, 1.0], jnp.float32)
    south_rim = jnp.zeros((stacked.shape[0], 2, stacked.shape[2]), jnp.float32) + rim_fill[:, None, None]
    tall_stack = jnp.concatenate([south_rim, stacked, ghost_rows], axis=1)
    return jnp.concatenate([tall_stack[..., -2:], tall_stack, tall_stack[..., :2]], axis=2)


def reference(temp, salt, uvel, vvel, thick, land, east_width, north_width, coriolis):
    depth = land.astype(jnp.float32) * thick
    sign_list = jnp.array([1.0, 1.0, -1.0, -1.0, 1.0, 1.0, 1.0], jnp.float32)
    overhead = jnp.zeros((temp.shape[1] + 4, temp.shape[2] + 4), jnp.float32)
    results = []
    for level_index in range(temp.shape[0]):
        stacked = jnp.stack([temp[level_index], salt[level_index], uvel[level_index], vvel[level_index], depth[level_index], east_width, north_width])
        extended = extend_global(stacked, sign_list)
        outputs, overhead = advance_level(extended[:4], extended[4], extended[5], extended[6], overhead, land[level_index].astype(jnp.float32), coriolis, east_width, north_width)
        results.append(outputs)
    return (jnp.stack([r[0] for r in results]), jnp.stack([r[1] for r in results]), jnp.stack([r[2] for r in results]), jnp.stack([r[3] for r in results]))
```

```python
import jax
import jax.numpy as jnp
from jax import lax
from jax.experimental import pallas as pl
from jax.experimental.pallas import tpu as pltpu
from jax.sharding import PartitionSpec as P

time_step = 0.2
biharm_coef = 0.02
alpha_temp = 0.2
beta_salt = 0.8
thin_floor = 0.25

LEVELS = 4
ROWS = 64
COLS = 768
TILE = 128
WIDE = COLS + TILE
TALL = ROWS + 16
FIELDS = 22
F32 = jnp.float32
PARAMS = pltpu.CompilerParams(vmem_limit_bytes=56 * 1024 * 1024)
AXES = ("lon", "lat")


def place(lat, lon, lats, lons):
    return (lon % lons) * lats + lat


def both(pairs):
    return [p for a, b in pairs for p in ((a, b), (b, a))]


def lat_pairs(lats, lons, bit):
    pairs = [
        (place(i, j, lats, lons), place(i + 1, j, lats, lons))
        for i in range(bit, lats - 1, 2)
        for j in range(lons)
    ]
    if bit:
        pairs += [
            (place(lats - 1, j, lats, lons), place(lats - 1, lons - 1 - j, lats, lons))
            for j in range(lons // 2)
        ]
    return both(pairs)


def lon_pairs(lats, lons, bit):
    return both(
        [
            (place(i, j, lats, lons), place(i, j + 1, lats, lons))
            for i in range(lats)
            for j in range(bit, lons, 2)
        ]
    )


def rows_kernel(*refs):
    low, high, (near_ref, far_ref), stage = refs[:8], refs[8:16], refs[16:18], refs[18]
    lat = lax.axis_index("lat")
    odd = lat % 2 == 1
    top = lat == lax.axis_size("lat") - 1

    def gather(group, take, dst):
        for kind in range(5):
            for level in range(LEVELS):
                if kind < 4:
                    cells = group[kind][level]
                else:
                    cells = group[4][level] * group[5][level].astype(F32)
                for k, row in enumerate(take):
                    dst[k, kind * LEVELS + level : kind * LEVELS + level + 1, :] = cells[row : row + 1]
        for k, row in enumerate(take):
            dst[k, 20:21, :] = group[6][row : row + 1, :]
            dst[k, 21:22, :] = group[7][row : row + 1, :]

    @pl.when(odd)
    def _():
        gather(low, (0, 1), near_ref)

        @pl.when(jnp.logical_not(top))
        def _():
            gather(high, (6, 7), far_ref)

        @pl.when(top)
        def _():
            gather(high, (6, 5), stage)
            kind_row = lax.broadcasted_iota(jnp.int32, (24, TILE), 0)
            turned = jnp.logical_and(kind_row >= 2 * LEVELS, kind_row < 4 * LEVELS)
            sign = jnp.where(turned, -1.0, 1.0).astype(F32)
            flip = TILE - 1 - lax.broadcasted_iota(jnp.int32, (24, TILE), 1)
            for k in range(2):
                for t in range(COLS // TILE):
                    src = stage[k, :, COLS - TILE * (t + 1) : COLS - TILE * t]
                    rev = jnp.take_along_axis(src, flip, axis=1, mode="promise_in_bounds")
                    far_ref[k, :, TILE * t : TILE * (t + 1)] = rev * sign

    @pl.when(jnp.logical_not(odd))
    def _():
        gather(high, (6, 7), near_ref)
        gather(low, (0, 1), far_ref)


def pack_rows(arrays):
    def spec(a, at):
        if a.ndim == 3:
            return pl.BlockSpec((LEVELS, 8, COLS), lambda i: (0, at, 0))
        return pl.BlockSpec((8, COLS), lambda i: (at, 0))

    whole = pl.BlockSpec((2, 24, COLS), lambda i: (0, 0, 0))
    shape = jax.ShapeDtypeStruct((2, 24, COLS), F32)
    return pl.pallas_call(
        rows_kernel,
        grid=(1,),
        in_specs=[spec(a, 0) for a in arrays] + [spec(a, ROWS // 8 - 1) for a in arrays],
        out_specs=[whole, whole],
        out_shape=[shape, shape],
        scratch_shapes=[pltpu.VMEM((2, 24, COLS), F32)],
        compiler_params=PARAMS,
        name="pack_rows",
    )(*arrays, *arrays)


def ghost_rows(near, far, odd, at_south):
    south = jnp.where(odd, near, far)
    north = jnp.where(odd, far, near)
    kind_row = lax.broadcasted_iota(jnp.int32, south.shape, south.ndim - 2)
    south = jnp.where(jnp.logical_and(at_south, kind_row >= 20), 1.0, south)
    return south, north


def columns_kernel(*refs):
    west, east, near_ref, far_ref, out_ref = refs[:8], refs[8:16], refs[16], refs[17], refs[18]
    lat = lax.axis_index("lat")
    lane = lax.broadcasted_iota(jnp.int32, (ROWS, TILE), 1)
    packed = jnp.zeros((ROWS, TILE), F32)

    def edge(group, kind, level):
        if kind < 4:
            return group[kind][level]
        if kind == 4:
            return group[4][level] * group[5][level].astype(F32)
        return group[6 + level][...]

    for f in range(FIELDS):
        kind, level = divmod(f, LEVELS)
        cells = jnp.where(lane < TILE // 2, edge(west, kind, level), edge(east, kind, level))
        if f:
            cells = pltpu.roll(cells, 4 * f, 1)
        mine = ((lane + 2) & (TILE - 1)) >> 2 == f
        packed = jnp.where(mine, cells, packed)
    out_ref[0:ROWS, :] = packed

    small = lax.broadcasted_iota(jnp.int32, (24, TILE), 1)
    kind_row = lax.broadcasted_iota(jnp.int32, (24, TILE), 0)
    mine = ((small + 2) & (TILE - 1)) >> 2 == kind_row
    for side in range(2):
        for k in range(2):
            parts = []
            for cut in (slice(0, TILE), slice(COLS - TILE, COLS)):
                parts.append(
                    ghost_rows(near_ref[k, :, cut], far_ref[k, :, cut], lat % 2 == 1, lat == 0)[1 - side]
                )
            cells = jnp.where(small < TILE // 2, parts[0], parts[1])
            cells = pltpu.roll(cells, 0, 1, stride=4, stride_axis=0)
            row = jnp.sum(jnp.where(mine, cells, 0.0), axis=0, keepdims=True)
            at = ROWS + 2 * side + k
            out_ref[at : at + 1, :] = row
    out_ref[ROWS + 4 : ROWS + 8, :] = jnp.zeros((4, TILE), F32)


def pack_columns(arrays, near, far):
    def spec(a, at):
        if a.ndim == 3:
            return pl.BlockSpec((LEVELS, ROWS, TILE), lambda i: (0, 0, at))
        return pl.BlockSpec((ROWS, TILE), lambda i: (0, at))

    whole = pl.BlockSpec((2, 24, COLS), lambda i: (0, 0, 0))
    return pl.pallas_call(
        columns_kernel,
        grid=(1,),
        in_specs=[spec(a, 0) for a in arrays]
        + [spec(a, COLS // TILE - 1) for a in arrays]
        + [whole, whole],
        out_specs=pl.BlockSpec((ROWS + 8, TILE), lambda i: (0, 0)),
        out_shape=jax.ShapeDtypeStruct((ROWS + 8, TILE), F32),
        compiler_params=PARAMS,
        name="pack_columns",
    )(*arrays, *arrays, near, far)


def to_east(x):
    return pltpu.roll(x, x.shape[1] - 1, 1)


def to_west(x, by=1):
    return pltpu.roll(x, by, 1)


def step_kernel(
    temp, salt, uvel, vvel, thick, land, ewid, nwid, cori, near, far, lon_even, lon_odd,
    temp_out, salt_out, uvel_out, vvel_out,
    ext, wid, side, ratio_e, ratio_n, span_e, span_n, inv_area,
    coef_e, coef_n, inv_vol, move_n, flux_t, flux_s, lap, pres, slope, over, over_e,
):
    level = pl.program_id(0)
    lat, lon = lax.axis_index("lat"), lax.axis_index("lon")
    lat_odd, lon_is_odd = lat % 2 == 1, lon % 2 == 1

    def fill(dst, f, load):
        shift = (TILE - 4 * f) % TILE if isinstance(f, int) else (TILE - 4 * f) & (TILE - 1)
        for c in range(ROWS // 8):
            dst[8 + 8 * c : 16 + 8 * c, 0:COLS] = load(8 * c)
            dst[8 + 8 * c : 16 + 8 * c, COLS:WIDE] = pltpu.roll(side[8 * c : 8 * c + 8, :], shift, 1)
        south, north = [], []
        for k in range(2):
            a = near[k, pl.ds(f, 1), :]
            b = far[k, pl.ds(f, 1), :]
            s = jnp.where(lat_odd, a, b)
            if isinstance(f, int) and f >= 20:
                s = jnp.where(lat == 0, 1.0, s)
            south.append(s)
            north.append(jnp.where(lat_odd, b, a))
        corner = pltpu.roll(side[ROWS : ROWS + 8, :], shift, 1)
        dst[72:74, 0:COLS] = jnp.concatenate(north, axis=0)
        dst[6:8, 0:COLS] = jnp.concatenate(south, axis=0)
        dst[72:74, COLS:WIDE] = corner[0:2]
        dst[6:8, COLS:WIDE] = corner[2:4]

    @pl.when(level == 0)
    def _():
        lane = lax.broadcasted_iota(jnp.int32, (ROWS + 8, TILE), 1)
        a, b = lon_even[...], lon_odd[...]
        from_east = jnp.where(lon_is_odd, b, a)
        from_west = jnp.where(lon_is_odd, a, b)
        side[...] = jnp.where((lane & 3) < 2, from_east, from_west)
        fill(wid.at[0], 20, lambda r: ewid[r : r + 8, :])
        fill(wid.at[1], 21, lambda r: nwid[r : r + 8, :])
        for c in range(10):
            r = 6 + 8 * c if c < 9 else 71
            e, n = wid[0, r : r + 8, :], wid[1, r : r + 8, :]
            ee, ne = to_east(e), to_east(n)
            en, nn = wid[0, r + 1 : r + 9, :], wid[1, r + 1 : r + 9, :]
            ratio_e[r : r + 8, :] = (n + ne) / (e + ee)
            ratio_n[r : r + 8, :] = (e + en) / (n + nn)
            span_e[r : r + 8, :] = (1.25 * time_step / 0.2 * 0.02 / biharm_coef) * (n + ne)
            span_n[r : r + 8, :] = (1.25 * time_step / 0.2 * 0.02 / biharm_coef) * (e + en)
            inv_area[r : r + 8, :] = 1.0 / (e * n)
            over[r : r + 8, :] = jnp.zeros((8, WIDE), F32)
            over_e[r : r + 8, :] = jnp.zeros((8, WIDE), F32)

    fill(ext.at[0], level, lambda r: temp[0, r : r + 8, :])
    fill(ext.at[1], LEVELS + level, lambda r: salt[0, r : r + 8, :])
    fill(ext.at[2], 2 * LEVELS + level, lambda r: uvel[0, r : r + 8, :])
    fill(ext.at[3], 3 * LEVELS + level, lambda r: vvel[0, r : r + 8, :])
    fill(ext.at[4], 4 * LEVELS + level, lambda r: thick[0, r : r + 8, :] * land[0, r : r + 8, :].astype(F32))

    for c in range(9):
        r = 7 + 8 * c
        here, above, below = slice(r, r + 8), slice(r + 1, r + 9), slice(r - 1, r + 7)
        d, dn, ds = ext[4, here, :], ext[4, above, :], ext[4, below, :]
        de = to_east(d)
        lon_thick = jnp.minimum(d, de)
        lat_thick = jnp.minimum(d, dn)
        ce = lon_thick * ratio_e[here, :]
        cn = lat_thick * ratio_n[here, :]
        cs = jnp.minimum(ds, d) * ratio_n[below, :]
        iv = inv_area[here, :] / jnp.maximum(d, thin_floor)
        coef_e[here, :] = ce
        coef_n[here, :] = cn
        inv_vol[here, :] = iv
        east = []
        for f in range(4):
            q, qn, qs = ext[f, here, :], ext[f, above, :], ext[f, below, :]
            qe = to_east(q)
            fe = ce * (qe - q)
            lap[f, here, :] = (fe - to_west(fe) + cn * (qn - q) - cs * (q - qs)) * iv
            if f < 3:
                east.append(qe)
            if f == 2:
                te = lon_thick * span_e[here, :] * (q + qe)
                flux_t[here, :] = te * (ext[0, here, :] + east[0])
                flux_s[here, :] = te * (ext[1, here, :] + east[1])
                be = (beta_salt * east[1] - alpha_temp * east[0]) * de
                pe = over_e[here, :] + 0.5 * be
                over_e[here, :] = over_e[here, :] + be
                slope[here, :] = pe - to_west(pe, 2)
            if f == 3:
                move_n[here, :] = lat_thick * span_n[here, :] * (q + qn)
        b = (beta_salt * ext[1, here, :] - alpha_temp * ext[0, here, :]) * d
        pres[here, :] = over[here, :] + 0.5 * b
        over[here, :] = over[here, :] + b

    for c in range(ROWS // 8):
        r = 8 + 8 * c
        here, above, below = slice(r, r + 8), slice(r + 1, r + 9), slice(r - 1, r + 7)
        own = slice(8 * c, 8 * c + 8)
        ce, cn, cs = coef_e[here, :], coef_n[here, 0:COLS], coef_n[below, 0:COLS]
        iv = biharm_coef * inv_vol[here, 0:COLS]
        wet = land[0, own, :].astype(F32)

        def tendency(f, extra=None):
            m = lap[f, here, :]
            fe = ce * (to_east(m) - m)
            if extra is not None:
                fe = fe + extra[here, :]
            zonal = (fe - to_west(fe))[:, 0:COLS]
            m = m[:, 0:COLS]
            return zonal + cn * (lap[f, above, 0:COLS] - m) - cs * (m - lap[f, below, 0:COLS])

        gn, gs = move_n[here, 0:COLS], move_n[below, 0:COLS]
        for f, extra, out in ((0, flux_t, temp_out), (1, flux_s, salt_out)):
            q, qn, qs = ext[f, here, 0:COLS], ext[f, above, 0:COLS], ext[f, below, 0:COLS]
            total = tendency(f, extra) + gn * (q + qn) - gs * (qs + q)
            out[0, own, :] = wet * (q - total * iv)
        u, v = ext[2, here, 0:COLS], ext[3, here, 0:COLS]
        turn = time_step * cori[own, :]
        ge = slope[here, 0:COLS] * (0.5 * time_step) / ewid[own, :]
        gn = (pres[above, 0:COLS] - pres[below, 0:COLS]) * (0.5 * time_step) / nwid[own, :]
        uvel_out[0, own, :] = wet * (u + turn * v - ge - tendency(2) * iv)
        vvel_out[0, own, :] = wet * (v - turn * u - gn - tendency(3) * iv)


def advance(arrays, coriolis, near, far, lon_even, lon_odd):
    by_level = pl.BlockSpec((1, ROWS, COLS), lambda i: (i, 0, 0))
    flat = pl.BlockSpec((ROWS, COLS), lambda i: (0, 0))
    rows = pl.BlockSpec((2, 24, COLS), lambda i: (0, 0, 0))
    cols = pl.BlockSpec((ROWS + 8, TILE), lambda i: (0, 0))
    plane = pltpu.VMEM((TALL, WIDE), F32)
    return pl.pallas_call(
        step_kernel,
        grid=(LEVELS,),
        in_specs=[by_level] * 6 + [flat] * 3 + [rows] * 2 + [cols] * 2,
        out_specs=[by_level] * 4,
        out_shape=[jax.ShapeDtypeStruct((LEVELS, ROWS, COLS), F32)] * 4,
        scratch_shapes=[
            pltpu.VMEM((5, TALL, WIDE), F32),
            pltpu.VMEM((2, TALL, WIDE), F32),
            pltpu.VMEM((ROWS + 8, TILE), F32),
        ]
        + [plane] * 5
        + [plane] * 6
        + [pltpu.VMEM((4, TALL, WIDE), F32)]
        + [plane] * 4,
        compiler_params=PARAMS,
        name="advance",
    )(*arrays, coriolis, near, far, lon_even, lon_odd)


def shards(temp, salt, uvel, vvel, thick, land, east_width, north_width, coriolis):
    lats, lons = lax.axis_size("lat"), lax.axis_size("lon")
    arrays = (temp, salt, uvel, vvel, thick, land, east_width, north_width)
    near, far = pack_rows(arrays)
    near = lax.ppermute(near, AXES, lat_pairs(lats, lons, 0))
    far = lax.ppermute(far, AXES, lat_pairs(lats, lons, 1))
    packed = pack_columns(arrays, near, far)
    lon_even = lax.ppermute(packed, AXES, lon_pairs(lats, lons, 0))
    lon_odd = lax.ppermute(packed, AXES, lon_pairs(lats, lons, 1))
    return tuple(advance(arrays, coriolis, near, far, lon_even, lon_odd))


def solution(mesh):
    deep, flat = P(None, "lat", "lon"), P("lat", "lon")
    return jax.shard_map(
        shards,
        mesh=mesh,
        in_specs=(deep,) * 6 + (flat,) * 3,
        out_specs=(deep,) * 4,
        check_vma=False,
    )
```

```python
import jax
import jax.numpy as jnp
from jax import lax
from jax.experimental import pallas as pl
from jax.experimental.pallas import tpu as pltpu
from jax.sharding import PartitionSpec as P

time_step = 0.2
biharm_coef = 0.02
alpha_temp = 0.2
beta_salt = 0.8
thin_floor = 0.25
flux_scale = time_step / 8.0 / biharm_coef

LEVELS = 4
ROWS = 64
COLS = 768
TILE = 128
WIDE = COLS + TILE
MAIN = 16
TALL = ROWS + 2 * MAIN
FIELDS = 22
F32 = jnp.float32
PARAMS = pltpu.CompilerParams(vmem_limit_bytes=12 * 1024 * 1024)
BIG = pltpu.CompilerParams(vmem_limit_bytes=24 * 1024 * 1024)
AXES = ("lon", "lat")


def place(lat, lon, lats, lons):
    return (lon % lons) * lats + lat


def both(pairs):
    return [p for a, b in pairs for p in ((a, b), (b, a))]


def lat_pairs(lats, lons, bit):
    pairs = [
        (place(i, j, lats, lons), place(i + 1, j, lats, lons))
        for i in range(bit, lats - 1, 2)
        for j in range(lons)
    ]
    if bit:
        pairs += [
            (place(lats - 1, j, lats, lons), place(lats - 1, lons - 1 - j, lats, lons))
            for j in range(lons // 2)
        ]
    return both(pairs)


def lon_pairs(lats, lons, bit):
    return both(
        [
            (place(i, j, lats, lons), place(i, j + 1, lats, lons))
            for i in range(lats)
            for j in range(bit, lons, 2)
        ]
    )


def onto_chip(x):
    return pltpu.with_memory_space_constraint(x, pltpu.VMEM)


def off_chip(x):
    return pltpu.with_memory_space_constraint(x, pltpu.HBM)


def rows_kernel(*refs):
    low, high, (near_ref, far_ref), stage = refs[:8], refs[8:16], refs[16:18], refs[18]
    lat = lax.axis_index("lat")
    odd = lat % 2 == 1
    top = lat == lax.axis_size("lat") - 1

    def gather(group, take, dst):
        for kind in range(5):
            for level in range(LEVELS):
                if kind < 4:
                    cells = group[kind][level]
                else:
                    cells = group[4][level] * group[5][level].astype(F32)
                for k, row in enumerate(take):
                    dst[k, kind * LEVELS + level : kind * LEVELS + level + 1, :] = cells[row : row + 1]
        for k, row in enumerate(take):
            dst[k, 20:21, :] = group[6][row : row + 1, :]
            dst[k, 21:22, :] = group[7][row : row + 1, :]

    @pl.when(odd)
    def _():
        gather(low, (0, 1), near_ref)

        @pl.when(jnp.logical_not(top))
        def _():
            gather(high, (6, 7), far_ref)

        @pl.when(top)
        def _():
            gather(high, (6, 5), stage)
            kind_row = lax.broadcasted_iota(jnp.int32, (24, TILE), 0)
            turned = jnp.logical_and(kind_row >= 2 * LEVELS, kind_row < 4 * LEVELS)
            sign = jnp.where(turned, -1.0, 1.0).astype(F32)
            flip = TILE - 1 - lax.broadcasted_iota(jnp.int32, (24, TILE), 1)
            for k in range(2):
                for t in range(COLS // TILE):
                    src = stage[k, :, COLS - TILE * (t + 1) : COLS - TILE * t]
                    rev = jnp.take_along_axis(src, flip, axis=1, mode="promise_in_bounds")
                    far_ref[k, :, TILE * t : TILE * (t + 1)] = rev * sign

    @pl.when(jnp.logical_not(odd))
    def _():
        gather(high, (6, 7), near_ref)
        gather(low, (0, 1), far_ref)


def pack_rows(arrays):
    def spec(a, at):
        if a.ndim == 3:
            return pl.BlockSpec((LEVELS, 8, COLS), lambda i: (0, at, 0))
        return pl.BlockSpec((8, COLS), lambda i: (at, 0))

    whole = pl.BlockSpec((2, 24, COLS), lambda i: (0, 0, 0))
    shape = pltpu.VMEM((2, 24, COLS), F32)
    return pl.pallas_call(
        rows_kernel,
        grid=(1,),
        in_specs=[spec(a, 0) for a in arrays] + [spec(a, ROWS // 8 - 1) for a in arrays],
        out_specs=[pl.BlockSpec(memory_space=pltpu.VMEM)] * 2,
        out_shape=[shape, shape],
        scratch_shapes=[pltpu.VMEM((2, 24, COLS), F32)],
        compiler_params=PARAMS,
        name="pack_rows",
    )(*[off_chip(x) for x in (*arrays, *arrays)])


def ghost_rows(near, far, odd, at_south):
    south = jnp.where(odd, near, far)
    north = jnp.where(odd, far, near)
    kind_row = lax.broadcasted_iota(jnp.int32, south.shape, south.ndim - 2)
    south = jnp.where(jnp.logical_and(at_south, kind_row >= 20), 1.0, south)
    return south, north


def columns_kernel(*refs):
    west, east, near_ref, far_ref, out_ref = refs[:8], refs[8:16], refs[16], refs[17], refs[18]
    lat = lax.axis_index("lat")
    lane = lax.broadcasted_iota(jnp.int32, (ROWS, TILE), 1)
    packed = jnp.zeros((ROWS, TILE), F32)

    def edge(group, kind, level):
        if kind < 4:
            return group[kind][level]
        if kind == 4:
            return group[4][level] * group[5][level].astype(F32)
        return group[6 + level][...]

    for f in range(FIELDS):
        kind, level = divmod(f, LEVELS)
        cells = jnp.where(lane < TILE // 2, edge(west, kind, level), edge(east, kind, level))
        if f:
            cells = pltpu.roll(cells, 4 * f, 1)
        mine = ((lane + 2) & (TILE - 1)) >> 2 == f
        packed = jnp.where(mine, cells, packed)
    out_ref[0:ROWS, :] = packed

    small = lax.broadcasted_iota(jnp.int32, (24, TILE), 1)
    kind_row = lax.broadcasted_iota(jnp.int32, (24, TILE), 0)
    mine = ((small + 2) & (TILE - 1)) >> 2 == kind_row
    for side in range(2):
        for k in range(2):
            parts = []
            for cut in (slice(0, TILE), slice(COLS - TILE, COLS)):
                parts.append(
                    ghost_rows(near_ref[k, :, cut], far_ref[k, :, cut], lat % 2 == 1, lat == 0)[1 - side]
                )
            cells = jnp.where(small < TILE // 2, parts[0], parts[1])
            cells = pltpu.roll(cells, 0, 1, stride=4, stride_axis=0)
            row = jnp.sum(jnp.where(mine, cells, 0.0), axis=0, keepdims=True)
            at = ROWS + 2 * side + k
            out_ref[at : at + 1, :] = row
    out_ref[ROWS + 4 : ROWS + 8, :] = jnp.zeros((4, TILE), F32)


def pack_columns(arrays, near, far):
    def spec(a, at):
        if a.ndim == 3:
            return pl.BlockSpec((LEVELS, ROWS, TILE), lambda i: (0, 0, at))
        return pl.BlockSpec((ROWS, TILE), lambda i: (0, at))

    whole = pl.BlockSpec((2, 24, COLS), lambda i: (0, 0, 0))
    return pl.pallas_call(
        columns_kernel,
        grid=(1,),
        in_specs=[spec(a, 0) for a in arrays]
        + [spec(a, COLS // TILE - 1) for a in arrays]
        + [pl.BlockSpec(memory_space=pltpu.VMEM)] * 2,
        out_specs=pl.BlockSpec(memory_space=pltpu.VMEM),
        out_shape=pltpu.VMEM((ROWS + 8, TILE), F32),
        compiler_params=PARAMS,
        name="pack_columns",
    )(*[onto_chip(x) for x in (*arrays, *arrays, near, far)])


def north_of(here, above):
    sub = lax.broadcasted_iota(jnp.int32, here.shape, 0)
    return pltpu.roll(jnp.where(sub == 0, above, here), 7, 0)


def south_of(here, below):
    sub = lax.broadcasted_iota(jnp.int32, here.shape, 0)
    return pltpu.roll(jnp.where(sub == 7, below, here), 1, 0)


def step_kernel(
    temp, salt, uvel, vvel, thick, land, ewid, nwid, cori, near, far, lon_even, lon_odd,
    temp_out, salt_out, uvel_out, vvel_out,
    ext, wid, side, ratio_e, ratio_n, span_e, span_n, inv_area,
    coef_e, coef_n, inv_vol, move_n, flux_t, flux_s, lap, pres, slope, over, over_e,
):
    level = pl.program_id(0)
    lat, lon = lax.axis_index("lat"), lax.axis_index("lon")
    lat_odd, lon_is_odd = lat % 2 == 1, lon % 2 == 1
    lane = lax.broadcasted_iota(jnp.int32, (8, TILE), 1)
    first, last = lane == 0, lane == TILE - 1

    def tile(t):
        return slice(TILE * t, TILE * t + TILE)

    def turn_e(x):
        return pltpu.roll(x, TILE - 1, 1)

    def turn_w(x):
        return pltpu.roll(x, 1, 1)

    def fill(dst, f, load):
        shift = (TILE - 4 * f) & (TILE - 1)

        for r in range(0, ROWS, 8):
            dst[MAIN + r : MAIN + r + 8, 0:COLS] = load(r)
            dst[MAIN + r : MAIN + r + 8, COLS:WIDE] = pltpu.roll(side[r : r + 8, :], shift, 1)
        south, north = [], []
        for k in range(2):
            a = near[k, pl.ds(f, 1), :]
            b = far[k, pl.ds(f, 1), :]
            s = jnp.where(lat_odd, a, b)
            if isinstance(f, int) and f >= 20:
                s = jnp.where(lat == 0, 1.0, s)
            south.append(s)
            north.append(jnp.where(lat_odd, b, a))
        corner = pltpu.roll(side[ROWS : ROWS + 8, :], shift, 1)
        top, low = MAIN + ROWS, MAIN - 2
        dst[top : top + 2, 0:COLS] = jnp.concatenate(north, axis=0)
        dst[low : low + 2, 0:COLS] = jnp.concatenate(south, axis=0)
        dst[top : top + 2, COLS:WIDE] = corner[0:2]
        dst[low : low + 2, COLS:WIDE] = corner[2:4]

    @pl.when(level == 0)
    def _():
        wide_lane = lax.broadcasted_iota(jnp.int32, (ROWS + 8, TILE), 1)
        a, b = lon_even[...], lon_odd[...]
        from_east = jnp.where(lon_is_odd, b, a)
        from_west = jnp.where(lon_is_odd, a, b)
        side[...] = jnp.where((wide_lane & 3) < 2, from_east, from_west)
        fill(wid.at[0], 20, lambda r: ewid[r : r + 8, :])
        fill(wid.at[1], 21, lambda r: nwid[r : r + 8, :])

        def chunk(c, _):
            r = pl.multiple_of(8 * c + 8, 8)
            here, above = pl.ds(r, 8), pl.ds(r + 8, 8)
            for t in range(7):
                e, n = wid[0, here, tile(t)], wid[1, here, tile(t)]
                u = (t + 1) % 7
                ee = jnp.where(last, turn_e(wid[0, here, tile(u)]), turn_e(e))
                ne = jnp.where(last, turn_e(wid[1, here, tile(u)]), turn_e(n))
                en = north_of(e, wid[0, above, tile(t)])
                nn = north_of(n, wid[1, above, tile(t)])
                ratio_e[here, tile(t)] = (n + ne) / (e + ee)
                ratio_n[here, tile(t)] = (e + en) / (n + nn)
                span_e[here, tile(t)] = flux_scale * (n + ne)
                span_n[here, tile(t)] = flux_scale * (e + en)
                inv_area[here, tile(t)] = 1.0 / (e * n)
                over[here, tile(t)] = jnp.zeros((8, TILE), F32)
                over_e[here, tile(t)] = jnp.zeros((8, TILE), F32)
            return 0

        lax.fori_loop(0, ROWS // 8 + 2, chunk, 0)

    fill(ext.at[0], level, lambda r: temp[level, r : r + 8, :])
    fill(ext.at[1], LEVELS + level, lambda r: salt[level, r : r + 8, :])
    fill(ext.at[2], 2 * LEVELS + level, lambda r: uvel[level, r : r + 8, :])
    fill(ext.at[3], 3 * LEVELS + level, lambda r: vvel[level, r : r + 8, :])
    fill(ext.at[4], 4 * LEVELS + level, lambda r: thick[level, r : r + 8, :] * land[level, r : r + 8, :].astype(F32))

    def laps(c, _):
        r = pl.multiple_of(8 * c + 8, 8)
        here, above, below = pl.ds(r, 8), pl.ds(r + 8, 8), pl.ds(r - 8, 8)

        def zonal(t, turned):
            d, rd = turned[4]
            de_next = ext[4, here, tile((t + 1) % 7)]
            ahead = [(ext[f, here, tile((t + 1) % 7)],) for f in range(4)] + [(de_next,)]
            ahead = [(x[0], turn_e(x[0])) for x in ahead]
            de = jnp.where(last, ahead[4][1], rd)
            lon_thick = jnp.minimum(d, de)
            ce = lon_thick * ratio_e[here, tile(t)]
            east = [jnp.where(last, ahead[f][1], turned[f][1]) for f in range(4)]
            flux = [ce * (east[f] - turned[f][0]) for f in range(4)]
            te = lon_thick * span_e[here, tile(t)] * (turned[2][0] + east[2])
            be = (beta_salt * east[1] - alpha_temp * east[0]) * de
            return ahead, ce, flux, te, be, east

        start = [(x, turn_e(x)) for x in (ext[f, here, tile(6)] for f in range(5))]
        at_zero, _, flux6, _, be6, _ = zonal(6, start)
        pe6 = over_e[here, tile(6)] + 0.5 * be6
        wrap_flux = [turn_w(x) for x in flux6]
        wrap_pe = pltpu.roll(pe6, 2, 1)
        behind, behind_pe, turned = wrap_flux, wrap_pe, at_zero
        for t in range(7):
            ahead, ce, flux, te, be, east = zonal(t, turned)
            if t < 6:
                turned_flux = [turn_w(x) for x in flux]
            else:
                turned_flux = wrap_flux
            coef_e[here, tile(t)] = ce
            d = turned[4][0]
            dn = north_of(d, ext[4, above, tile(t)])
            ds = south_of(d, ext[4, below, tile(t)])
            lat_thick = jnp.minimum(d, dn)
            rn = ratio_n[here, tile(t)]
            cn = lat_thick * rn
            cs = jnp.minimum(ds, d) * south_of(rn, ratio_n[below, tile(t)])
            iv = inv_area[here, tile(t)] / jnp.maximum(d, thin_floor)
            coef_n[here, tile(t)] = cn
            inv_vol[here, tile(t)] = iv
            for f in range(4):
                q = turned[f][0]
                qn = north_of(q, ext[f, above, tile(t)])
                qs = south_of(q, ext[f, below, tile(t)])
                west = jnp.where(first, behind[f], turned_flux[f])
                lap[f, here, tile(t)] = (flux[f] - west + cn * (qn - q) - cs * (q - qs)) * iv
                if f == 3:
                    move_n[here, tile(t)] = lat_thick * span_n[here, tile(t)] * (q + qn)
            q0, q1 = turned[0][0], turned[1][0]
            flux_t[here, tile(t)] = te * (q0 + east[0])
            flux_s[here, tile(t)] = te * (q1 + east[1])
            b = (beta_salt * q1 - alpha_temp * q0) * d
            before = over[here, tile(t)]
            pres[here, tile(t)] = before + 0.5 * b
            over[here, tile(t)] = before + b
            before = over_e[here, tile(t)]
            over_e[here, tile(t)] = before + be
            if t < 6:
                pe = before + 0.5 * be
                turned_pe = pltpu.roll(pe, 2, 1)
                slope[here, tile(t)] = pe - jnp.where(lane < 2, behind_pe, turned_pe)
                behind_pe = turned_pe
            behind, turned = turned_flux, ahead
        return 0

    lax.fori_loop(0, ROWS // 8 + 2, laps, 0)

    def finish(c, _):
        r = pl.multiple_of(MAIN + 8 * c, 8)
        here, above, below = pl.ds(r, 8), pl.ds(r + 8, 8), pl.ds(r - 8, 8)
        own = pl.ds(pl.multiple_of(8 * c, 8), 8)

        def zonal(t, turned):
            ahead = [lap[f, here, tile((t + 1) % 7)] for f in range(4)]
            ahead = [(x, turn_e(x)) for x in ahead]
            ce = coef_e[here, tile(t)]
            flux = [ce * (jnp.where(last, ahead[f][1], turned[f][1]) - turned[f][0]) for f in range(4)]
            flux[0] = flux[0] + flux_t[here, tile(t)]
            flux[1] = flux[1] + flux_s[here, tile(t)]
            return ahead, flux

        start = [(x, turn_e(x)) for x in (lap[f, here, tile(6)] for f in range(4))]
        turned, flux6 = zonal(6, start)
        behind = [turn_w(x) for x in flux6]
        outs = (temp_out, salt_out, uvel_out, vvel_out)
        for t in range(6):
            ahead, flux = zonal(t, turned)
            turned_flux = [turn_w(x) for x in flux]
            cn = coef_n[here, tile(t)]
            cs = south_of(cn, coef_n[below, tile(t)])
            iv = biharm_coef * inv_vol[here, tile(t)]
            gn = move_n[here, tile(t)]
            gs = south_of(gn, move_n[below, tile(t)])
            wet = land[level, own, tile(t)].astype(F32)
            u, v = ext[2, here, tile(t)], ext[3, here, tile(t)]
            turning = time_step * cori[own, tile(t)]
            for f in range(4):
                m = turned[f][0]
                mn = north_of(m, lap[f, above, tile(t)])
                ms = south_of(m, lap[f, below, tile(t)])
                west = jnp.where(first, behind[f], turned_flux[f])
                total = flux[f] - west + cn * (mn - m) - cs * (m - ms)
                if f < 2:
                    q = ext[f, here, tile(t)]
                    qn = north_of(q, ext[f, above, tile(t)])
                    qs = south_of(q, ext[f, below, tile(t)])
                    total = total + gn * (q + qn) - gs * (qs + q)
                    outs[f][0, own, tile(t)] = wet * (q - total * iv)
                elif f == 2:
                    ge = slope[here, tile(t)] * (0.5 * time_step) / ewid[own, tile(t)]
                    outs[f][0, own, tile(t)] = wet * (u + turning * v - ge - total * iv)
                else:
                    p = pres[here, tile(t)]
                    pn = north_of(p, pres[above, tile(t)])
                    ps = south_of(p, pres[below, tile(t)])
                    gp = (pn - ps) * (0.5 * time_step) / nwid[own, tile(t)]
                    outs[f][0, own, tile(t)] = wet * (v - turning * u - gp - total * iv)
            behind, turned = turned_flux, ahead
        return 0

    lax.fori_loop(0, ROWS // 8, finish, 0)


def advance(arrays, coriolis, near, far, lon_even, lon_odd):
    by_level = pl.BlockSpec((1, ROWS, COLS), lambda i: (i, 0, 0))
    onchip = pl.BlockSpec(memory_space=pltpu.VMEM)
    plane = pltpu.VMEM((TALL, WIDE), F32)
    return pl.pallas_call(
        step_kernel,
        grid=(LEVELS,),
        in_specs=[onchip] * 13,
        out_specs=[by_level] * 4,
        out_shape=[jax.ShapeDtypeStruct((LEVELS, ROWS, COLS), F32)] * 4,
        scratch_shapes=[
            pltpu.VMEM((5, TALL, WIDE), F32),
            pltpu.VMEM((2, TALL, WIDE), F32),
            pltpu.VMEM((ROWS + 8, TILE), F32),
        ]
        + [plane] * 5
        + [plane] * 6
        + [pltpu.VMEM((4, TALL, WIDE), F32)]
        + [plane] * 4,
        compiler_params=BIG,
        name="advance",
    )(*[onto_chip(x) for x in (*arrays, coriolis, near, far, lon_even, lon_odd)])


def shards(temp, salt, uvel, vvel, thick, land, east_width, north_width, coriolis):
    lats, lons = lax.axis_size("lat"), lax.axis_size("lon")
    arrays = (temp, salt, uvel, vvel, thick, land, east_width, north_width)
    near, far = pack_rows(arrays)
    near = lax.ppermute(near, AXES, lat_pairs(lats, lons, 0))
    far = lax.ppermute(far, AXES, lat_pairs(lats, lons, 1))
    packed = pack_columns(arrays, near, far)
    lon_even = lax.ppermute(packed, AXES, lon_pairs(lats, lons, 0))
    lon_odd = lax.ppermute(packed, AXES, lon_pairs(lats, lons, 1))
    return tuple(advance(arrays, coriolis, near, far, lon_even, lon_odd))


def solution(mesh):
    deep, flat = P(None, "lat", "lon"), P("lat", "lon")
    return jax.shard_map(
        shards,
        mesh=mesh,
        in_specs=(deep,) * 6 + (flat,) * 3,
        out_specs=(deep,) * 4,
        check_vma=False,
    )
```

```python
import jax
import jax.numpy as jnp
from jax import lax
from jax.experimental import pallas as pl
from jax.experimental.pallas import tpu as pltpu
from jax.sharding import PartitionSpec as P

time_step = 0.2
biharm_coef = 0.02
alpha_temp = 0.2
beta_salt = 0.8
thin_floor = 0.25
flux_scale = time_step / 8.0 / biharm_coef

LEVELS = 4
ROWS = 64
COLS = 768
TILE = 128
TILES = COLS // TILE
CHUNKS = ROWS // 8
TALL = ROWS + 16
FIELDS = 22
SHOWN = FIELDS + LEVELS + 1
F32 = jnp.float32
PARAMS = pltpu.CompilerParams(vmem_limit_bytes=12 * 1024 * 1024)
AXES = ("lon", "lat")
VMEM = pl.BlockSpec(memory_space=pltpu.VMEM)


def place(lat, lon, lats, lons):
    return (lon % lons) * lats + lat


def both(pairs):
    return [p for a, b in pairs for p in ((a, b), (b, a))]


def lat_pairs(lats, lons, bit):
    pairs = [
        (place(i, j, lats, lons), place(i + 1, j, lats, lons))
        for i in range(bit, lats - 1, 2)
        for j in range(lons)
    ]
    if bit:
        pairs += [
            (place(lats - 1, j, lats, lons), place(lats - 1, lons - 1 - j, lats, lons))
            for j in range(lons // 2)
        ]
    return both(pairs)


def lon_pairs(lats, lons, bit):
    return both(
        [
            (place(i, j, lats, lons), place(i, j + 1, lats, lons))
            for i in range(lats)
            for j in range(bit, lons, 2)
        ]
    )


def onto_chip(x):
    return pltpu.with_memory_space_constraint(x, pltpu.VMEM)


def off_chip(x):
    return pltpu.with_memory_space_constraint(x, pltpu.HBM)


def rows_kernel(*refs):
    low, high, (near_ref, far_ref), stage = refs[:8], refs[8:16], refs[16:18], refs[18]
    lat = lax.axis_index("lat")
    odd = lat % 2 == 1
    top = lat == lax.axis_size("lat") - 1

    def gather(group, take, dst):
        for kind in range(5):
            for level in range(LEVELS):
                if kind < 4:
                    cells = group[kind][level]
                else:
                    cells = group[4][level] * group[5][level].astype(F32)
                for k, row in enumerate(take):
                    dst[k, kind * LEVELS + level : kind * LEVELS + level + 1, :] = cells[row : row + 1]
        for k, row in enumerate(take):
            dst[k, 20:21, :] = group[6][row : row + 1, :]
            dst[k, 21:22, :] = group[7][row : row + 1, :]

    @pl.when(odd)
    def _():
        gather(low, (0, 1), near_ref)

        @pl.when(jnp.logical_not(top))
        def _():
            gather(high, (6, 7), far_ref)

        @pl.when(top)
        def _():
            gather(high, (6, 5), stage)
            kind_row = lax.broadcasted_iota(jnp.int32, (24, TILE), 0)
            turned = jnp.logical_and(kind_row >= 2 * LEVELS, kind_row < 4 * LEVELS)
            sign = jnp.where(turned, -1.0, 1.0).astype(F32)
            flip = TILE - 1 - lax.broadcasted_iota(jnp.int32, (24, TILE), 1)
            for k in range(2):
                for t in range(COLS // TILE):
                    src = stage[k, :, COLS - TILE * (t + 1) : COLS - TILE * t]
                    rev = jnp.take_along_axis(src, flip, axis=1, mode="promise_in_bounds")
                    far_ref[k, :, TILE * t : TILE * (t + 1)] = rev * sign

    @pl.when(jnp.logical_not(odd))
    def _():
        gather(high, (6, 7), near_ref)
        gather(low, (0, 1), far_ref)


def pack_rows(arrays):
    def spec(a, at):
        if a.ndim == 3:
            return pl.BlockSpec((LEVELS, 8, COLS), lambda i: (0, at, 0))
        return pl.BlockSpec((8, COLS), lambda i: (at, 0))

    whole = pl.BlockSpec((2, 24, COLS), lambda i: (0, 0, 0))
    shape = pltpu.VMEM((2, 24, COLS), F32)
    return pl.pallas_call(
        rows_kernel,
        grid=(1,),
        in_specs=[spec(a, 0) for a in arrays] + [spec(a, ROWS // 8 - 1) for a in arrays],
        out_specs=[pl.BlockSpec(memory_space=pltpu.VMEM)] * 2,
        out_shape=[shape, shape],
        scratch_shapes=[pltpu.VMEM((2, 24, COLS), F32)],
        compiler_params=PARAMS,
        name="pack_rows",
    )(*[off_chip(x) for x in (*arrays, *arrays)])


def packed_field():
    def of(shape):
        lane = lax.broadcasted_iota(jnp.int32, shape, len(shape) - 1)
        return ((lane + 2) & (TILE - 1)) >> 1

    return of


def windows_kernel(temp, salt, uvel, vvel, thick, land, ewid, nwid, cori, win, packed):
    lane = lax.broadcasted_iota(jnp.int32, (ROWS, TILE), 1)
    field = packed_field()((ROWS, TILE))
    total = jnp.zeros((ROWS, TILE), F32)

    def edge(f, cut):
        kind, level = divmod(f, LEVELS)
        if kind < 4:
            return (temp, salt, uvel, vvel)[kind][level, :, cut]
        if kind == 4:
            return thick[level, :, cut] * land[level, :, cut].astype(F32)
        if f < FIELDS:
            return (ewid, nwid)[f - 20][:, cut]
        if f < FIELDS + LEVELS:
            return land[f - FIELDS, :, cut].astype(F32)
        return cori[:, cut]

    for f in range(SHOWN):
        low, high = edge(f, slice(0, TILE)), edge(f, slice(COLS - TILE, COLS))
        cells = jnp.where(lane < TILE // 4, low, pltpu.roll(high, TILE // 2, 1))
        win[f] = cells
        if f < FIELDS:
            mine = jnp.logical_or(field == f, field == f + 33)
            total = jnp.where(mine, pltpu.roll(cells, (TILE // 2 + 2 * f) % TILE, 1), total)
    packed[...] = total


def windows(arrays, coriolis):
    return pl.pallas_call(
        windows_kernel,
        in_specs=[VMEM] * 9,
        out_specs=[VMEM] * 2,
        out_shape=[pltpu.VMEM((SHOWN, ROWS, TILE), F32), pltpu.VMEM((ROWS, TILE), F32)],
        compiler_params=PARAMS,
        name="windows",
    )(*[onto_chip(x) for x in (*arrays, coriolis)])


def columns_kernel(packed, near, far, out, ghosts, corner):
    lat = lax.axis_index("lat")
    odd = lat % 2 == 1
    out[0:ROWS, :] = packed[...]
    row = lax.broadcasted_iota(jnp.int32, (24, COLS), 0)
    fill = jnp.logical_and(lat == 0, row >= 20)
    lane = lax.broadcasted_iota(jnp.int32, (24, TILE), 1)
    field = packed_field()((24, TILE))
    small_row = lax.broadcasted_iota(jnp.int32, (24, TILE), 0)
    mine = jnp.logical_or(field == small_row, field == small_row + 33)
    for k in range(2):
        a, b = near[k], far[k]
        for side in range(2):
            if side == 0:
                cells = jnp.where(odd, b, a)
            else:
                cells = jnp.where(fill, 1.0, jnp.where(odd, a, b))
            at = 2 * side + k
            ghosts[at] = cells
            shown = jnp.where(lane < TILE // 4, cells[:, 0:TILE], pltpu.roll(cells[:, COLS - TILE : COLS], TILE // 2, 1))
            corner[at] = shown
            spread = pltpu.roll(shown, TILE // 2, 1, stride=2, stride_axis=0)
            out[ROWS + at : ROWS + at + 1, :] = jnp.sum(jnp.where(mine, spread, 0.0), axis=0, keepdims=True)
    out[ROWS + 4 : ROWS + 8, :] = jnp.zeros((4, TILE), F32)


def pack_columns(packed, near, far):
    return pl.pallas_call(
        columns_kernel,
        in_specs=[VMEM] * 3,
        out_specs=[VMEM] * 3,
        out_shape=[
            pltpu.VMEM((ROWS + 8, TILE), F32),
            pltpu.VMEM((4, 24, COLS), F32),
            pltpu.VMEM((4, 24, TILE), F32),
        ],
        compiler_params=PARAMS,
        name="pack_columns",
    )(*[onto_chip(x) for x in (packed, near, far)])


def north_of(here, above):
    sub = lax.broadcasted_iota(jnp.int32, here.shape, 0)
    return pltpu.roll(jnp.where(sub == 0, above, here), 7, 0)


def south_of(here, below):
    sub = lax.broadcasted_iota(jnp.int32, here.shape, 0)
    return pltpu.roll(jnp.where(sub == 7, below, here), 1, 0)


def inner_kernel(
    temp, salt, uvel, vvel, thick, land, ewid, nwid, cori,
    temp_out, salt_out, uvel_out, vvel_out,
    deep, ratio_e, ratio_n, span_e, span_n, inv_area, half_e, half_n,
    coef_e, coef_n, inv_vol, move_n, flux_t, flux_s, lap, pres, slope, over, over_e,
):
    level = pl.program_id(0)
    lane = lax.broadcasted_iota(jnp.int32, (8, TILE), 1)
    first, last = lane == 0, lane == TILE - 1
    data = (temp, salt, uvel, vvel)

    def tile(t):
        return slice(TILE * t, TILE * t + TILE)

    def turn_e(x):
        return pltpu.roll(x, TILE - 1, 1)

    def turn_w(x):
        return pltpu.roll(x, 1, 1)

    def around(c):
        r = pl.multiple_of(8 * c, 8)
        up = pl.multiple_of(8 * jnp.minimum(c + 1, CHUNKS - 1), 8)
        down = pl.multiple_of(8 * jnp.maximum(c - 1, 0), 8)
        return pl.ds(r, 8), pl.ds(up, 8), pl.ds(down, 8)

    @pl.when(level == 0)
    def _():
        def chunk(c, _):
            here, above, _ = around(c)
            east = [(ewid[here, tile(0)], nwid[here, tile(0)])]
            east = [tuple((x, turn_e(x)) for x in east[0])]
            for t in range(TILES):
                (e, re), (n, rn) = east[t]
                u = (t + 1) % TILES
                if u:
                    east.append(tuple((x, turn_e(x)) for x in (ewid[here, tile(u)], nwid[here, tile(u)])))
                else:
                    east.append(east[0])
                ee = jnp.where(last, east[t + 1][0][1], re)
                ne = jnp.where(last, east[t + 1][1][1], rn)
                en = north_of(e, ewid[above, tile(t)])
                nn = north_of(n, nwid[above, tile(t)])
                ratio_e[here, tile(t)] = (n + ne) / (e + ee)
                ratio_n[here, tile(t)] = (e + en) / (n + nn)
                span_e[here, tile(t)] = flux_scale * (n + ne)
                span_n[here, tile(t)] = flux_scale * (e + en)
                inv_area[here, tile(t)] = 1.0 / (e * n)
                half_e[here, tile(t)] = (0.5 * time_step) / e
                half_n[here, tile(t)] = (0.5 * time_step) / n
                over[here, tile(t)] = jnp.zeros((8, TILE), F32)
                over_e[here, tile(t)] = jnp.zeros((8, TILE), F32)
            return 0

        lax.fori_loop(0, CHUNKS, chunk, 0)

    for r in range(0, ROWS, 8):
        deep[r : r + 8, :] = thick[level, r : r + 8, :] * land[level, r : r + 8, :].astype(F32)

    def laps(c, _):
        here, above, below = around(c)

        def turned_at(t):
            cells = [x[level, here, tile(t)] for x in data] + [deep[here, tile(t)]]
            return [(x, turn_e(x)) for x in cells]

        def zonal(t, turned, ahead):
            d, rd = turned[4]
            de = jnp.where(last, ahead[4][1], rd)
            lon_thick = jnp.minimum(d, de)
            ce = lon_thick * ratio_e[here, tile(t)]
            east = [jnp.where(last, ahead[f][1], turned[f][1]) for f in range(4)]
            flux = [ce * (east[f] - turned[f][0]) for f in range(4)]
            te = lon_thick * span_e[here, tile(t)] * (turned[2][0] + east[2])
            be = (beta_salt * east[1] - alpha_temp * east[0]) * de
            before = over_e[here, tile(t)]
            pe = before + 0.5 * be
            over_e[here, tile(t)] = before + be
            return ce, flux, te, east, pe

        end, start = turned_at(TILES - 1), turned_at(0)
        kept = zonal(TILES - 1, end, start)
        behind, behind_pe = [turn_w(x) for x in kept[1]], pltpu.roll(kept[4], 2, 1)
        kept_flux, kept_pe = behind, behind_pe
        turned = start
        for t in range(TILES):
            if t < TILES - 1:
                ahead = turned_at(t + 1) if t < TILES - 2 else end
                ce, flux, te, east, pe = zonal(t, turned, ahead)
                turned_flux, turned_pe = [turn_w(x) for x in flux], pltpu.roll(pe, 2, 1)
            else:
                ce, flux, te, east, pe = kept
                turned_flux, turned_pe = kept_flux, kept_pe
            coef_e[here, tile(t)] = ce
            d = turned[4][0]
            dn, ds = north_of(d, deep[above, tile(t)]), south_of(d, deep[below, tile(t)])
            lat_thick = jnp.minimum(d, dn)
            rn = ratio_n[here, tile(t)]
            cn = lat_thick * rn
            cs = jnp.minimum(ds, d) * south_of(rn, ratio_n[below, tile(t)])
            iv = inv_area[here, tile(t)] / jnp.maximum(d, thin_floor)
            coef_n[here, tile(t)] = cn
            inv_vol[here, tile(t)] = iv
            for f in range(4):
                q = turned[f][0]
                qn, qs = north_of(q, data[f][level, above, tile(t)]), south_of(q, data[f][level, below, tile(t)])
                west = jnp.where(first, behind[f], turned_flux[f])
                lap[f, here, tile(t)] = (flux[f] - west + cn * (qn - q) - cs * (q - qs)) * iv
                if f == 3:
                    move_n[here, tile(t)] = lat_thick * span_n[here, tile(t)] * (q + qn)
            q0, q1 = turned[0][0], turned[1][0]
            flux_t[here, tile(t)] = te * (q0 + east[0])
            flux_s[here, tile(t)] = te * (q1 + east[1])
            b = (beta_salt * q1 - alpha_temp * q0) * d
            before = over[here, tile(t)]
            pres[here, tile(t)] = before + 0.5 * b
            over[here, tile(t)] = before + b
            slope[here, tile(t)] = pe - jnp.where(lane < 2, behind_pe, turned_pe)
            behind, behind_pe, turned = turned_flux, turned_pe, ahead
        return 0

    lax.fori_loop(0, CHUNKS, laps, 0)

    def finish(c, _):
        here, above, below = around(c)

        def turned_at(t):
            return [(x, turn_e(x)) for x in (lap[f, here, tile(t)] for f in range(4))]

        def zonal(t, turned, ahead):
            ce = coef_e[here, tile(t)]
            flux = [ce * (jnp.where(last, ahead[f][1], turned[f][1]) - turned[f][0]) for f in range(4)]
            flux[0] = flux[0] + flux_t[here, tile(t)]
            flux[1] = flux[1] + flux_s[here, tile(t)]
            return flux

        end, start = turned_at(TILES - 1), turned_at(0)
        kept = zonal(TILES - 1, end, start)
        kept_turned = [turn_w(x) for x in kept]
        behind, turned = kept_turned, start
        outs = (temp_out, salt_out, uvel_out, vvel_out)
        for t in range(TILES):
            if t < TILES - 1:
                ahead = turned_at(t + 1) if t < TILES - 2 else end
                flux = zonal(t, turned, ahead)
                turned_flux = [turn_w(x) for x in flux]
            else:
                flux, turned_flux = kept, kept_turned
            cn = coef_n[here, tile(t)]
            cs = south_of(cn, coef_n[below, tile(t)])
            iv = biharm_coef * inv_vol[here, tile(t)]
            gn = move_n[here, tile(t)]
            gs = south_of(gn, move_n[below, tile(t)])
            wet = land[level, here, tile(t)].astype(F32)
            u, v = uvel[level, here, tile(t)], vvel[level, here, tile(t)]
            turning = time_step * cori[here, tile(t)]
            for f in range(4):
                m = turned[f][0]
                mn, ms = north_of(m, lap[f, above, tile(t)]), south_of(m, lap[f, below, tile(t)])
                west = jnp.where(first, behind[f], turned_flux[f])
                total = flux[f] - west + cn * (mn - m) - cs * (m - ms)
                if f < 2:
                    q = data[f][level, here, tile(t)]
                    qn, qs = north_of(q, data[f][level, above, tile(t)]), south_of(q, data[f][level, below, tile(t)])
                    total = total + gn * (q + qn) - gs * (qs + q)
                    change = wet * (q - total * iv)
                elif f == 2:
                    change = wet * (u + turning * v - slope[here, tile(t)] * half_e[here, tile(t)] - total * iv)
                else:
                    p = pres[here, tile(t)]
                    rise = north_of(p, pres[above, tile(t)]) - south_of(p, pres[below, tile(t)])
                    change = wet * (v - turning * u - rise * half_n[here, tile(t)] - total * iv)
                outs[f][level, here, tile(t)] = change
            behind, turned = turned_flux, ahead
        return 0

    lax.fori_loop(0, CHUNKS, finish, 0)


def inner(arrays, coriolis):
    plane = pltpu.VMEM((ROWS, COLS), F32)
    return pl.pallas_call(
        inner_kernel,
        grid=(LEVELS,),
        in_specs=[VMEM] * 9,
        out_specs=[VMEM] * 4,
        out_shape=[pltpu.VMEM((LEVELS, ROWS, COLS), F32)] * 4,
        scratch_shapes=[plane] * 14 + [pltpu.VMEM((4, ROWS, COLS), F32)] + [plane] * 4,
        compiler_params=PARAMS,
        name="inner",
    )(*[onto_chip(x) for x in (*arrays, coriolis)])


def metric(e, n, lanes, rows):
    ee, ne, en, nn = lanes(e, 1), lanes(n, 1), rows(e, 1), rows(n, 1)
    return (
        (n + ne) / (e + ee),
        (e + en) / (n + nn),
        flux_scale * (n + ne),
        flux_scale * (e + en),
        1.0 / (e * n),
        (0.5 * time_step) / e,
        (0.5 * time_step) / n,
    )


def patch(cells, d, wet, cori, known, over, lanes, rows):
    ratio_e, ratio_n, span_e, span_n, inv_area, half_e, half_n = known
    temp, salt, uvel, vvel = cells
    de, dn = lanes(d, 1), rows(d, 1)
    lon_thick, lat_thick = jnp.minimum(d, de), jnp.minimum(d, dn)
    ce, cn = lon_thick * ratio_e, lat_thick * ratio_n
    cs = rows(cn, -1)
    iv = inv_area / jnp.maximum(d, thin_floor)
    b = (beta_salt * salt - alpha_temp * temp) * d
    p = over + 0.5 * b
    ge = (lanes(p, 1) - lanes(p, -1)) * half_e
    gn = (rows(p, 1) - rows(p, -1)) * half_n
    outs = []
    te = tn = None
    for f in (2, 3, 0, 1):
        q = cells[f]
        qe, qn, qs = lanes(q, 1), rows(q, 1), rows(q, -1)
        if f == 2:
            te = lon_thick * span_e * (q + qe)
        if f == 3:
            tn = lat_thick * span_n * (q + qn)
            ts = rows(tn, -1)
        fe = ce * (qe - q)
        m = (fe - lanes(fe, -1) + cn * (qn - q) - cs * (q - qs)) * iv
        fe = ce * (lanes(m, 1) - m)
        if f < 2:
            fe = fe + te * (q + qe)
        total = fe - lanes(fe, -1) + cn * (rows(m, 1) - m) - cs * (m - rows(m, -1))
        if f < 2:
            total = total + tn * (q + qn) - ts * (qs + q)
        change = q - biharm_coef * iv * total
        if f == 2:
            change = change + time_step * cori * vvel - ge
        if f == 3:
            change = change - time_step * cori * uvel - gn
        outs.append(wet * change)
    return (outs[2], outs[3], outs[0], outs[1]), over + b


def rims_kernel(
    temp, salt, uvel, vvel, thick, land, ewid, nwid, cori, ghosts, temp_in, salt_in, uvel_in, vvel_in,
    temp_out, salt_out, uvel_out, vvel_out, known, spin, over,
):
    level = pl.program_id(0)
    sub = lax.broadcasted_iota(jnp.int32, (8, COLS), 0)
    low, high = slice(0, 8), slice(ROWS - 8, ROWS)

    def lanes(x, by):
        return pltpu.roll(x, COLS - 1 if by > 0 else 1, 2)

    def rows(x, by):
        return pltpu.roll(x, 7 if by > 0 else 1, 1)

    def strips(f, south, north):
        g = [ghosts[k, pl.ds(f, 1), :] for k in range(4)]
        s = jnp.where(sub == 0, g[2], jnp.where(sub == 1, g[3], pltpu.roll(south, 2, 0)))
        n = jnp.where(sub == 6, g[0], jnp.where(sub == 7, g[1], pltpu.roll(north, 6, 0)))
        return jnp.stack([s, n])

    def own(south, north):
        return jnp.stack([pltpu.roll(south, 2, 0), pltpu.roll(north, 6, 0)])

    @pl.when(level == 0)
    def _():
        e = strips(20, ewid[low, :], ewid[high, :])
        n = strips(21, nwid[low, :], nwid[high, :])
        for i, x in enumerate(metric(e, n, lanes, rows)):
            known[i] = x
        spin[...] = own(cori[low, :], cori[high, :])
        over[...] = jnp.zeros((2, 8, COLS), F32)

    cells = [
        strips(LEVELS * kind + level, x[level, low, :], x[level, high, :])
        for kind, x in enumerate((temp, salt, uvel, vvel))
    ]
    wet_low, wet_high = land[level, low, :].astype(F32), land[level, high, :].astype(F32)
    d = strips(4 * LEVELS + level, thick[level, low, :] * wet_low, thick[level, high, :] * wet_high)
    new, over[...] = patch(
        cells, d, own(wet_low, wet_high), spin[...], [known[i] for i in range(7)], over[...], lanes, rows
    )
    ins = (temp_in, salt_in, uvel_in, vvel_in)
    for x, old, out in zip(new, ins, (temp_out, salt_out, uvel_out, vvel_out)):
        out[level, low, :] = jnp.where(sub < 2, pltpu.roll(x[0], 6, 0), old[level, low, :])
        out[level, high, :] = jnp.where(sub >= 6, pltpu.roll(x[1], 2, 0), old[level, high, :])


def rims(arrays, coriolis, ghosts, outs):
    return pl.pallas_call(
        rims_kernel,
        grid=(LEVELS,),
        in_specs=[VMEM] * 14,
        out_specs=[VMEM] * 4,
        out_shape=[pltpu.VMEM((LEVELS, ROWS, COLS), F32)] * 4,
        scratch_shapes=[
            pltpu.VMEM((7, 2, 8, COLS), F32),
            pltpu.VMEM((2, 8, COLS), F32),
            pltpu.VMEM((2, 8, COLS), F32),
        ],
        input_output_aliases={10: 0, 11: 1, 12: 2, 13: 3},
        compiler_params=PARAMS,
        name="rims",
    )(*[onto_chip(x) for x in (*arrays, coriolis, ghosts, *outs)])


def sides_kernel(
    win, corner, lon_even, lon_odd, temp_in, salt_in, uvel_in, vvel_in,
    temp_out, salt_out, uvel_out, vvel_out,
    side, known, over, edges, mid_sem, low_sem, high_sem,
):
    level = pl.program_id(0)
    ins, outs = (temp_in, salt_in, uvel_in, vvel_in), (temp_out, salt_out, uvel_out, vvel_out)
    lane = lax.broadcasted_iota(jnp.int32, (TALL, TILE), 1)
    field = packed_field()((TALL, TILE))
    ghost_lane = jnp.logical_or(field == 0, field == 33)
    middle = pl.ds(TILE, COLS - 2 * TILE)

    def mid_copy(i):
        return pltpu.make_async_copy(ins[i].at[:, :, middle], outs[i].at[:, :, middle], mid_sem.at[i])

    def edge_copies(i, at):
        return (
            pltpu.make_async_copy(edges.at[0, i, at], outs[i].at[at, :, pl.ds(0, TILE)], low_sem.at[i, at]),
            pltpu.make_async_copy(edges.at[1, i, at], outs[i].at[at, :, pl.ds(COLS - TILE, TILE)], high_sem.at[i, at]),
        )

    def lanes(x, by):
        return pltpu.roll(x, TILE - 1 if by > 0 else 1, 1)

    def rows(x, by):
        return pltpu.roll(x, TALL - 1 if by > 0 else 1, 0)

    def tall(body, north, south):
        pad = jnp.zeros((6, TILE), F32)
        return jnp.concatenate([pad, south, body, north, pad], axis=0)

    def extended(f):
        shift = (TILE - 2 * f) & (TILE - 1)
        base = tall(
            win[f],
            jnp.concatenate([corner[k, pl.ds(f, 1), :] for k in (0, 1)], axis=0),
            jnp.concatenate([corner[k, pl.ds(f, 1), :] for k in (2, 3)], axis=0),
        )
        return jnp.where(ghost_lane, pltpu.roll(side[...], shift, 1), base)

    @pl.when(level == 0)
    def _():
        for i in range(4):
            mid_copy(i).start()
        odd = lax.axis_index("lon") % 2 == 1
        a, b = lon_even[...], lon_odd[...]
        got = jnp.where(packed_field()((ROWS + 8, TILE)) >= 33, jnp.where(odd, b, a), jnp.where(odd, a, b))
        side[...] = tall(got[0:ROWS], got[ROWS : ROWS + 2], got[ROWS + 2 : ROWS + 4])
        e, n = extended(20), extended(21)
        for i, x in enumerate(metric(e, n, lanes, rows)):
            known[i] = x
        over[...] = jnp.zeros((TALL, TILE), F32)

    cells = [extended(LEVELS * kind + level) for kind in range(4)]
    d = extended(4 * LEVELS + level)
    blank = jnp.zeros((2, TILE), F32)
    wet, spin = tall(win[FIELDS + level], blank, blank), tall(win[FIELDS + LEVELS], blank, blank)
    new, over[...] = patch(cells, d, wet, spin, [known[i] for i in range(7)], over[...], lanes, rows)
    own = lax.broadcasted_iota(jnp.int32, (ROWS, TILE), 1)
    for i, x in enumerate(new):
        x = x[8 : 8 + ROWS]
        edges[0, i, level] = jnp.where(own < 2, x, ins[i][level, :, 0:TILE])
        edges[1, i, level] = jnp.where(own >= TILE - 2, pltpu.roll(x, TILE // 2, 1), ins[i][level, :, COLS - TILE : COLS])
        for copy in edge_copies(i, level):
            copy.start()

    @pl.when(level == LEVELS - 1)
    def _():
        for i in range(4):
            mid_copy(i).wait()
            for at in range(LEVELS):
                for copy in edge_copies(i, at):
                    copy.wait()


def sides(win, corner, lon_even, lon_odd, outs):
    return pl.pallas_call(
        sides_kernel,
        grid=(LEVELS,),
        in_specs=[VMEM] * 8,
        out_specs=[pl.BlockSpec(memory_space=pltpu.HBM)] * 4,
        out_shape=[jax.ShapeDtypeStruct((LEVELS, ROWS, COLS), F32)] * 4,
        scratch_shapes=[
            pltpu.VMEM((TALL, TILE), F32),
            pltpu.VMEM((7, TALL, TILE), F32),
            pltpu.VMEM((TALL, TILE), F32),
            pltpu.VMEM((2, 4, LEVELS, ROWS, TILE), F32),
            pltpu.SemaphoreType.DMA((4,)),
            pltpu.SemaphoreType.DMA((4, LEVELS)),
            pltpu.SemaphoreType.DMA((4, LEVELS)),
        ],
        compiler_params=PARAMS,
        name="sides",
    )(*[onto_chip(x) for x in (win, corner, lon_even, lon_odd, *outs)])


def shards(temp, salt, uvel, vvel, thick, land, east_width, north_width, coriolis):
    lats, lons = lax.axis_size("lat"), lax.axis_size("lon")
    arrays = (temp, salt, uvel, vvel, thick, land, east_width, north_width)
    near, far = pack_rows(arrays)
    near = lax.ppermute(near, AXES, lat_pairs(lats, lons, 0))
    far = lax.ppermute(far, AXES, lat_pairs(lats, lons, 1))
    win, packed = windows(arrays, coriolis)
    outs = inner(arrays, coriolis)
    near, far, packed, *outs = lax.optimization_barrier((near, far, packed, *outs))
    packed, ghosts, corner = pack_columns(packed, near, far)
    lon_even = lax.ppermute(packed, AXES, lon_pairs(lats, lons, 0))
    lon_odd = lax.ppermute(packed, AXES, lon_pairs(lats, lons, 1))
    outs = rims(arrays, coriolis, ghosts, outs)
    return tuple(sides(win, corner, lon_even, lon_odd, outs))


def solution(mesh):
    deep, flat = P(None, "lat", "lon"), P("lat", "lon")
    return jax.shard_map(
        shards,
        mesh=mesh,
        in_specs=(deep,) * 6 + (flat,) * 3,
        out_specs=(deep,) * 4,
        check_vma=False,
    )
```

```python
import jax
import jax.numpy as jnp
from jax import lax
from jax.experimental import pallas as pl
from jax.experimental.pallas import tpu as pltpu
from jax.sharding import PartitionSpec as P

time_step = 0.2
biharm_coef = 0.02
alpha_temp = 0.2
beta_salt = 0.8
thin_floor = 0.25
flux_scale = time_step / 8.0 / biharm_coef

LEVELS = 4
ROWS = 64
COLS = 768
TILE = 128
TILES = COLS // TILE
CHUNKS = ROWS // 8
TALL = ROWS + 16
FIELDS = 22
SHOWN = FIELDS + LEVELS + 1
F32 = jnp.float32
PARAMS = pltpu.CompilerParams(vmem_limit_bytes=12 * 1024 * 1024)
AXES = ("lon", "lat")
VMEM = pl.BlockSpec(memory_space=pltpu.VMEM)


def place(lat, lon, lats, lons):
    return (lon % lons) * lats + lat


def both(pairs):
    return [p for a, b in pairs for p in ((a, b), (b, a))]


def lat_pairs(lats, lons, bit):
    pairs = [
        (place(i, j, lats, lons), place(i + 1, j, lats, lons))
        for i in range(bit, lats - 1, 2)
        for j in range(lons)
    ]
    if bit:
        pairs += [
            (place(lats - 1, j, lats, lons), place(lats - 1, lons - 1 - j, lats, lons))
            for j in range(lons // 2)
        ]
    return both(pairs)


def lon_pairs(lats, lons, bit):
    return both(
        [
            (place(i, j, lats, lons), place(i, j + 1, lats, lons))
            for i in range(lats)
            for j in range(bit, lons, 2)
        ]
    )


def onto_chip(x):
    return pltpu.with_memory_space_constraint(x, pltpu.VMEM)


def off_chip(x):
    return pltpu.with_memory_space_constraint(x, pltpu.HBM)


def rows_kernel(*refs):
    low, high, (near_ref, far_ref), stage = refs[:8], refs[8:16], refs[16:18], refs[18]
    lat = lax.axis_index("lat")
    odd = lat % 2 == 1
    top = lat == lax.axis_size("lat") - 1

    def gather(group, take, dst):
        for kind in range(5):
            for level in range(LEVELS):
                if kind < 4:
                    cells = group[kind][level]
                else:
                    cells = group[4][level] * group[5][level].astype(F32)
                for k, row in enumerate(take):
                    dst[k, kind * LEVELS + level : kind * LEVELS + level + 1, :] = cells[row : row + 1]
        for k, row in enumerate(take):
            dst[k, 20:21, :] = group[6][row : row + 1, :]
            dst[k, 21:22, :] = group[7][row : row + 1, :]

    @pl.when(odd)
    def _():
        gather(low, (0, 1), near_ref)

        @pl.when(jnp.logical_not(top))
        def _():
            gather(high, (6, 7), far_ref)

        @pl.when(top)
        def _():
            gather(high, (6, 5), stage)
            kind_row = lax.broadcasted_iota(jnp.int32, (24, TILE), 0)
            turned = jnp.logical_and(kind_row >= 2 * LEVELS, kind_row < 4 * LEVELS)
            sign = jnp.where(turned, -1.0, 1.0).astype(F32)
            flip = TILE - 1 - lax.broadcasted_iota(jnp.int32, (24, TILE), 1)
            for k in range(2):
                for t in range(COLS // TILE):
                    src = stage[k, :, COLS - TILE * (t + 1) : COLS - TILE * t]
                    rev = jnp.take_along_axis(src, flip, axis=1, mode="promise_in_bounds")
                    far_ref[k, :, TILE * t : TILE * (t + 1)] = rev * sign

    @pl.when(jnp.logical_not(odd))
    def _():
        gather(high, (6, 7), near_ref)
        gather(low, (0, 1), far_ref)


def pack_rows(arrays):
    def spec(a, at):
        if a.ndim == 3:
            return pl.BlockSpec((LEVELS, 8, COLS), lambda i: (0, at, 0))
        return pl.BlockSpec((8, COLS), lambda i: (at, 0))

    whole = pl.BlockSpec((2, 24, COLS), lambda i: (0, 0, 0))
    shape = pltpu.VMEM((2, 24, COLS), F32)
    return pl.pallas_call(
        rows_kernel,
        grid=(1,),
        in_specs=[spec(a, 0) for a in arrays] + [spec(a, ROWS // 8 - 1) for a in arrays],
        out_specs=[pl.BlockSpec(memory_space=pltpu.VMEM)] * 2,
        out_shape=[shape, shape],
        scratch_shapes=[pltpu.VMEM((2, 24, COLS), F32)],
        compiler_params=PARAMS,
        name="pack_rows",
    )(*[off_chip(x) for x in (*arrays, *arrays)])


def packed_field():
    def of(shape):
        lane = lax.broadcasted_iota(jnp.int32, shape, len(shape) - 1)
        return ((lane + 2) & (TILE - 1)) >> 1

    return of


def windows_kernel(temp, salt, uvel, vvel, thick, land, ewid, nwid, cori, win, packed):
    lane = lax.broadcasted_iota(jnp.int32, (ROWS, TILE), 1)
    field = packed_field()((ROWS, TILE))
    total = jnp.zeros((ROWS, TILE), F32)

    def edge(f, cut):
        kind, level = divmod(f, LEVELS)
        if kind < 4:
            return (temp, salt, uvel, vvel)[kind][level, :, cut]
        if kind == 4:
            return thick[level, :, cut] * land[level, :, cut].astype(F32)
        if f < FIELDS:
            return (ewid, nwid)[f - 20][:, cut]
        if f < FIELDS + LEVELS:
            return land[f - FIELDS, :, cut].astype(F32)
        return cori[:, cut]

    for f in range(SHOWN):
        low, high = edge(f, slice(0, TILE)), edge(f, slice(COLS - TILE, COLS))
        cells = jnp.where(lane < TILE // 4, low, pltpu.roll(high, TILE // 2, 1))
        win[f] = cells
        if f < FIELDS:
            mine = jnp.logical_or(field == f, field == f + 33)
            total = jnp.where(mine, pltpu.roll(cells, (TILE // 2 + 2 * f) % TILE, 1), total)
    packed[...] = total


def windows(arrays, coriolis):
    return pl.pallas_call(
        windows_kernel,
        in_specs=[VMEM] * 9,
        out_specs=[VMEM] * 2,
        out_shape=[pltpu.VMEM((SHOWN, ROWS, TILE), F32), pltpu.VMEM((ROWS, TILE), F32)],
        compiler_params=PARAMS,
        name="windows",
    )(*[onto_chip(x) for x in (*arrays, coriolis)])


def columns_kernel(packed, near, far, out, ghosts, corner):
    lat = lax.axis_index("lat")
    odd = lat % 2 == 1
    out[0:ROWS, :] = packed[...]
    row = lax.broadcasted_iota(jnp.int32, (24, COLS), 0)
    fill = jnp.logical_and(lat == 0, row >= 20)
    lane = lax.broadcasted_iota(jnp.int32, (24, TILE), 1)
    field = packed_field()((24, TILE))
    small_row = lax.broadcasted_iota(jnp.int32, (24, TILE), 0)
    mine = jnp.logical_or(field == small_row, field == small_row + 33)
    for k in range(2):
        a, b = near[k], far[k]
        for side in range(2):
            if side == 0:
                cells = jnp.where(odd, b, a)
            else:
                cells = jnp.where(fill, 1.0, jnp.where(odd, a, b))
            at = 2 * side + k
            ghosts[at] = cells
            shown = jnp.where(lane < TILE // 4, cells[:, 0:TILE], pltpu.roll(cells[:, COLS - TILE : COLS], TILE // 2, 1))
            corner[at] = shown
            spread = pltpu.roll(shown, TILE // 2, 1, stride=2, stride_axis=0)
            out[ROWS + at : ROWS + at + 1, :] = jnp.sum(jnp.where(mine, spread, 0.0), axis=0, keepdims=True)
    out[ROWS + 4 : ROWS + 8, :] = jnp.zeros((4, TILE), F32)


def pack_columns(packed, near, far):
    return pl.pallas_call(
        columns_kernel,
        in_specs=[VMEM] * 3,
        out_specs=[VMEM] * 3,
        out_shape=[
            pltpu.VMEM((ROWS + 8, TILE), F32),
            pltpu.VMEM((4, 24, COLS), F32),
            pltpu.VMEM((4, 24, TILE), F32),
        ],
        compiler_params=PARAMS,
        name="pack_columns",
    )(*[onto_chip(x) for x in (packed, near, far)])


def north_of(here, above):
    sub = lax.broadcasted_iota(jnp.int32, here.shape, 0)
    return pltpu.roll(jnp.where(sub == 0, above, here), 7, 0)


def south_of(here, below):
    sub = lax.broadcasted_iota(jnp.int32, here.shape, 0)
    return pltpu.roll(jnp.where(sub == 7, below, here), 1, 0)


def tile(t):
    return slice(TILE * t, TILE * t + TILE)


def turn_e(x):
    return pltpu.roll(x, TILE - 1, 1)


def turn_w(x):
    return pltpu.roll(x, 1, 1)


def around(c):
    r = pl.multiple_of(8 * c, 8)
    up = pl.multiple_of(8 * jnp.minimum(c + 1, CHUNKS - 1), 8)
    down = pl.multiple_of(8 * jnp.maximum(c - 1, 0), 8)
    return pl.ds(r, 8), pl.ds(up, 8), pl.ds(down, 8)


def inner_metric(ewid, nwid, known, over, over_e):
    ratio_e, ratio_n, span_e, span_n, inv_area, half_e, half_n = known
    last = lax.broadcasted_iota(jnp.int32, (8, TILE), 1) == TILE - 1

    def chunk(c, _):
        here, above, _ = around(c)
        east = [(ewid[here, tile(0)], nwid[here, tile(0)])]
        east = [tuple((x, turn_e(x)) for x in east[0])]
        for t in range(TILES):
            (e, re), (n, rn) = east[t]
            u = (t + 1) % TILES
            if u:
                east.append(tuple((x, turn_e(x)) for x in (ewid[here, tile(u)], nwid[here, tile(u)])))
            else:
                east.append(east[0])
            ee = jnp.where(last, east[t + 1][0][1], re)
            ne = jnp.where(last, east[t + 1][1][1], rn)
            en = north_of(e, ewid[above, tile(t)])
            nn = north_of(n, nwid[above, tile(t)])
            ratio_e[here, tile(t)] = (n + ne) / (e + ee)
            ratio_n[here, tile(t)] = (e + en) / (n + nn)
            span_e[here, tile(t)] = flux_scale * (n + ne)
            span_n[here, tile(t)] = flux_scale * (e + en)
            inv_area[here, tile(t)] = 1.0 / (e * n)
            half_e[here, tile(t)] = (0.5 * time_step) / e
            half_n[here, tile(t)] = (0.5 * time_step) / n
            over[here, tile(t)] = jnp.zeros((8, TILE), F32)
            over_e[here, tile(t)] = jnp.zeros((8, TILE), F32)
        return 0

    lax.fori_loop(0, CHUNKS, chunk, 0)


def inner_level(level, fields, outs, known, work, over, over_e, keep):
    temp, salt, uvel, vvel, thick, land, ewid, nwid, cori = fields
    ratio_e, ratio_n, span_e, span_n, inv_area, half_e, half_n = known
    deep, coef_e, coef_n, inv_vol, move_n, flux_t, flux_s, pres, slope, lap = work
    lane = lax.broadcasted_iota(jnp.int32, (8, TILE), 1)
    first, last = lane == 0, lane == TILE - 1
    data = (temp, salt, uvel, vvel)

    for r in range(0, ROWS, 8):
        deep[r : r + 8, :] = thick[level, r : r + 8, :] * land[level, r : r + 8, :].astype(F32)

    def laps(c, _):
        here, above, below = around(c)

        def turned_at(t):
            cells = [x[level, here, tile(t)] for x in data] + [deep[here, tile(t)]]
            return [(x, turn_e(x)) for x in cells]

        def zonal(t, turned, ahead):
            d, rd = turned[4]
            de = jnp.where(last, ahead[4][1], rd)
            lon_thick = jnp.minimum(d, de)
            ce = lon_thick * ratio_e[here, tile(t)]
            east = [jnp.where(last, ahead[f][1], turned[f][1]) for f in range(4)]
            flux = [ce * (east[f] - turned[f][0]) for f in range(4)]
            te = lon_thick * span_e[here, tile(t)] * (turned[2][0] + east[2])
            be = (beta_salt * east[1] - alpha_temp * east[0]) * de
            before = over_e[here, tile(t)]
            pe = before + 0.5 * be
            if keep:
                over_e[here, tile(t)] = before + be
            return ce, flux, te, east, pe

        end, start = turned_at(TILES - 1), turned_at(0)
        kept = zonal(TILES - 1, end, start)
        behind, behind_pe = [turn_w(x) for x in kept[1]], pltpu.roll(kept[4], 2, 1)
        kept_flux, kept_pe = behind, behind_pe
        turned = start
        for t in range(TILES):
            if t < TILES - 1:
                ahead = turned_at(t + 1) if t < TILES - 2 else end
                ce, flux, te, east, pe = zonal(t, turned, ahead)
                turned_flux, turned_pe = [turn_w(x) for x in flux], pltpu.roll(pe, 2, 1)
            else:
                ce, flux, te, east, pe = kept
                turned_flux, turned_pe = kept_flux, kept_pe
            coef_e[here, tile(t)] = ce
            d = turned[4][0]
            dn, ds = north_of(d, deep[above, tile(t)]), south_of(d, deep[below, tile(t)])
            lat_thick = jnp.minimum(d, dn)
            rn = ratio_n[here, tile(t)]
            cn = lat_thick * rn
            cs = jnp.minimum(ds, d) * south_of(rn, ratio_n[below, tile(t)])
            iv = inv_area[here, tile(t)] / jnp.maximum(d, thin_floor)
            coef_n[here, tile(t)] = cn
            inv_vol[here, tile(t)] = iv
            for f in range(4):
                q = turned[f][0]
                qn, qs = north_of(q, data[f][level, above, tile(t)]), south_of(q, data[f][level, below, tile(t)])
                west = jnp.where(first, behind[f], turned_flux[f])
                lap[f, here, tile(t)] = (flux[f] - west + cn * (qn - q) - cs * (q - qs)) * iv
                if f == 3:
                    move_n[here, tile(t)] = lat_thick * span_n[here, tile(t)] * (q + qn)
            q0, q1 = turned[0][0], turned[1][0]
            flux_t[here, tile(t)] = te * (q0 + east[0])
            flux_s[here, tile(t)] = te * (q1 + east[1])
            b = (beta_salt * q1 - alpha_temp * q0) * d
            before = over[here, tile(t)]
            pres[here, tile(t)] = before + 0.5 * b
            if keep:
                over[here, tile(t)] = before + b
            slope[here, tile(t)] = pe - jnp.where(lane < 2, behind_pe, turned_pe)
            behind, behind_pe, turned = turned_flux, turned_pe, ahead
        return 0

    lax.fori_loop(0, CHUNKS, laps, 0, unroll=2)

    def finish(c, _):
        here, above, below = around(c)

        def turned_at(t):
            return [(x, turn_e(x)) for x in (lap[f, here, tile(t)] for f in range(4))]

        def zonal(t, turned, ahead):
            ce = coef_e[here, tile(t)]
            flux = [ce * (jnp.where(last, ahead[f][1], turned[f][1]) - turned[f][0]) for f in range(4)]
            flux[0] = flux[0] + flux_t[here, tile(t)]
            flux[1] = flux[1] + flux_s[here, tile(t)]
            return flux

        end, start = turned_at(TILES - 1), turned_at(0)
        kept = zonal(TILES - 1, end, start)
        kept_turned = [turn_w(x) for x in kept]
        behind, turned = kept_turned, start
        for t in range(TILES):
            if t < TILES - 1:
                ahead = turned_at(t + 1) if t < TILES - 2 else end
                flux = zonal(t, turned, ahead)
                turned_flux = [turn_w(x) for x in flux]
            else:
                flux, turned_flux = kept, kept_turned
            cn = coef_n[here, tile(t)]
            cs = south_of(cn, coef_n[below, tile(t)])
            iv = biharm_coef * inv_vol[here, tile(t)]
            gn = move_n[here, tile(t)]
            gs = south_of(gn, move_n[below, tile(t)])
            wet = land[level, here, tile(t)].astype(F32)
            u, v = uvel[level, here, tile(t)], vvel[level, here, tile(t)]
            turning = time_step * cori[here, tile(t)]
            for f in range(4):
                m = turned[f][0]
                mn, ms = north_of(m, lap[f, above, tile(t)]), south_of(m, lap[f, below, tile(t)])
                west = jnp.where(first, behind[f], turned_flux[f])
                total = flux[f] - west + cn * (mn - m) - cs * (m - ms)
                if f < 2:
                    q = data[f][level, here, tile(t)]
                    qn, qs = north_of(q, data[f][level, above, tile(t)]), south_of(q, data[f][level, below, tile(t)])
                    total = total + gn * (q + qn) - gs * (qs + q)
                    change = wet * (q - total * iv)
                elif f == 2:
                    change = wet * (u + turning * v - slope[here, tile(t)] * half_e[here, tile(t)] - total * iv)
                else:
                    p = pres[here, tile(t)]
                    rise = north_of(p, pres[above, tile(t)]) - south_of(p, pres[below, tile(t)])
                    change = wet * (v - turning * u - rise * half_n[here, tile(t)] - total * iv)
                outs[f][level, here, tile(t)] = change
            behind, turned = turned_flux, ahead
        return 0

    lax.fori_loop(0, CHUNKS, finish, 0, unroll=2)


WORK = [pltpu.VMEM((ROWS, COLS), F32)] * 9 + [pltpu.VMEM((4, ROWS, COLS), F32)]


def inner_kernel(*refs):
    fields, outs, known, over, over_e, work = refs[:9], refs[9:13], refs[13:20], refs[20], refs[21], refs[22:]
    level = pl.program_id(0)

    @pl.when(level == 0)
    def _():
        inner_metric(fields[6], fields[7], known, over, over_e)

    inner_level(level, fields, outs, known, work, over, over_e, True)


def inner(arrays, coriolis):
    out = [pltpu.VMEM((LEVELS, ROWS, COLS), F32)] * 4 + [pltpu.VMEM((ROWS, COLS), F32)] * 9
    done = pl.pallas_call(
        inner_kernel,
        grid=(LEVELS - 1,),
        in_specs=[VMEM] * 9,
        out_specs=[VMEM] * 13,
        out_shape=out,
        scratch_shapes=WORK,
        compiler_params=PARAMS,
        name="inner",
    )(*[onto_chip(x) for x in (*arrays, coriolis)])
    return done[:4], done[4:]


def metric(e, n, lanes, rows):
    ee, ne, en, nn = lanes(e, 1), lanes(n, 1), rows(e, 1), rows(n, 1)
    return (
        (n + ne) / (e + ee),
        (e + en) / (n + nn),
        flux_scale * (n + ne),
        flux_scale * (e + en),
        1.0 / (e * n),
        (0.5 * time_step) / e,
        (0.5 * time_step) / n,
    )


def patch(cells, d, wet, cori, known, over, lanes, rows):
    ratio_e, ratio_n, span_e, span_n, inv_area, half_e, half_n = known
    temp, salt, uvel, vvel = cells
    de, dn = lanes(d, 1), rows(d, 1)
    lon_thick, lat_thick = jnp.minimum(d, de), jnp.minimum(d, dn)
    ce, cn = lon_thick * ratio_e, lat_thick * ratio_n
    cs = rows(cn, -1)
    iv = inv_area / jnp.maximum(d, thin_floor)
    b = (beta_salt * salt - alpha_temp * temp) * d
    p = over + 0.5 * b
    ge = (lanes(p, 1) - lanes(p, -1)) * half_e
    gn = (rows(p, 1) - rows(p, -1)) * half_n
    outs = []
    te = tn = None
    for f in (2, 3, 0, 1):
        q = cells[f]
        qe, qn, qs = lanes(q, 1), rows(q, 1), rows(q, -1)
        if f == 2:
            te = lon_thick * span_e * (q + qe)
        if f == 3:
            tn = lat_thick * span_n * (q + qn)
            ts = rows(tn, -1)
        fe = ce * (qe - q)
        m = (fe - lanes(fe, -1) + cn * (qn - q) - cs * (q - qs)) * iv
        fe = ce * (lanes(m, 1) - m)
        if f < 2:
            fe = fe + te * (q + qe)
        total = fe - lanes(fe, -1) + cn * (rows(m, 1) - m) - cs * (m - rows(m, -1))
        if f < 2:
            total = total + tn * (q + qn) - ts * (qs + q)
        change = q - biharm_coef * iv * total
        if f == 2:
            change = change + time_step * cori * vvel - ge
        if f == 3:
            change = change - time_step * cori * uvel - gn
        outs.append(wet * change)
    return (outs[2], outs[3], outs[0], outs[1]), over + b


def rims_level(level, fields, ghosts, outs, known, spin, over):
    temp, salt, uvel, vvel, thick, land, ewid, nwid, cori = fields
    sub = lax.broadcasted_iota(jnp.int32, (8, COLS), 0)
    low, high = slice(0, 8), slice(ROWS - 8, ROWS)

    def lanes(x, by):
        return pltpu.roll(x, COLS - 1 if by > 0 else 1, 2)

    def rows(x, by):
        return pltpu.roll(x, 7 if by > 0 else 1, 1)

    def strips(f, south, north):
        g = [ghosts[k, pl.ds(f, 1), :] for k in range(4)]
        s = jnp.where(sub == 0, g[2], jnp.where(sub == 1, g[3], pltpu.roll(south, 2, 0)))
        n = jnp.where(sub == 6, g[0], jnp.where(sub == 7, g[1], pltpu.roll(north, 6, 0)))
        return jnp.stack([s, n])

    def own(south, north):
        return jnp.stack([pltpu.roll(south, 2, 0), pltpu.roll(north, 6, 0)])

    @pl.when(level == 0)
    def _():
        e = strips(20, ewid[low, :], ewid[high, :])
        n = strips(21, nwid[low, :], nwid[high, :])
        for i, x in enumerate(metric(e, n, lanes, rows)):
            known[i] = x
        spin[...] = own(cori[low, :], cori[high, :])
        over[...] = jnp.zeros((2, 8, COLS), F32)

    cells = [
        strips(LEVELS * kind + level, x[level, low, :], x[level, high, :])
        for kind, x in enumerate((temp, salt, uvel, vvel))
    ]
    wet_low, wet_high = land[level, low, :].astype(F32), land[level, high, :].astype(F32)
    d = strips(4 * LEVELS + level, thick[level, low, :] * wet_low, thick[level, high, :] * wet_high)
    new, over[...] = patch(
        cells, d, own(wet_low, wet_high), spin[...], [known[i] for i in range(7)], over[...], lanes, rows
    )
    for x, (old, out) in zip(new, outs):
        out[level, low, :] = jnp.where(sub < 2, pltpu.roll(x[0], 6, 0), old[level, low, :])
        out[level, high, :] = jnp.where(sub >= 6, pltpu.roll(x[1], 2, 0), old[level, high, :])


def runs_late():
    lon, lons = lax.axis_index("lon"), lax.axis_size("lon")
    top = lax.axis_index("lat") == lax.axis_size("lat") - 1
    late = jnp.logical_or(lon == lons - 1, lon == lons // 2)
    return jnp.where(top, lon == 0, late)


def last_kernel(*refs):
    fields, known, over, over_e, outs, work = refs[:9], refs[9:16], refs[16], refs[17], refs[22:26], refs[26:]

    @pl.when(jnp.logical_not(runs_late()))
    def _():
        inner_level(LEVELS - 1, fields, outs, known, work, over, over_e, False)


def rims_kernel(*refs):
    fields, known, over, over_e, ghosts = refs[:9], refs[9:16], refs[16], refs[17], refs[18]
    outs, rim_known, spin, rim_over, work = refs[23:27], refs[27], refs[28], refs[29], refs[30:]
    level = pl.program_id(0)

    @pl.when(jnp.logical_and(runs_late(), level == 0))
    def _():
        inner_level(LEVELS - 1, fields, outs, known, work, over, over_e, False)

    rims_level(level, fields, ghosts, list(zip(outs, outs)), rim_known, spin, rim_over)


def last_level(arrays, coriolis, known, outs):
    return pl.pallas_call(
        last_kernel,
        in_specs=[VMEM] * 22,
        out_specs=[VMEM] * 4,
        out_shape=[pltpu.VMEM((LEVELS, ROWS, COLS), F32)] * 4,
        scratch_shapes=WORK,
        input_output_aliases={18: 0, 19: 1, 20: 2, 21: 3},
        compiler_params=PARAMS,
        name="last_level",
    )(*[onto_chip(x) for x in (*arrays, coriolis, *known, *outs)])


def rims(arrays, coriolis, known, ghosts, outs):
    return pl.pallas_call(
        rims_kernel,
        grid=(LEVELS,),
        in_specs=[VMEM] * 23,
        out_specs=[VMEM] * 4,
        out_shape=[pltpu.VMEM((LEVELS, ROWS, COLS), F32)] * 4,
        scratch_shapes=[
            pltpu.VMEM((7, 2, 8, COLS), F32),
            pltpu.VMEM((2, 8, COLS), F32),
            pltpu.VMEM((2, 8, COLS), F32),
        ]
        + WORK,
        input_output_aliases={19: 0, 20: 1, 21: 2, 22: 3},
        compiler_params=PARAMS,
        name="rims",
    )(*[onto_chip(x) for x in (*arrays, coriolis, *known, ghosts, *outs)])


def sides_kernel(
    win, corner, lon_even, lon_odd, temp_in, salt_in, uvel_in, vvel_in,
    temp_out, salt_out, uvel_out, vvel_out,
    side, known, over, edges, mid_sem, low_sem, high_sem,
):
    level = pl.program_id(0)
    ins, outs = (temp_in, salt_in, uvel_in, vvel_in), (temp_out, salt_out, uvel_out, vvel_out)
    lane = lax.broadcasted_iota(jnp.int32, (TALL, TILE), 1)
    field = packed_field()((TALL, TILE))
    ghost_lane = jnp.logical_or(field == 0, field == 33)
    middle = pl.ds(TILE, COLS - 2 * TILE)

    def mid_copy(i):
        return pltpu.make_async_copy(ins[i].at[:, :, middle], outs[i].at[:, :, middle], mid_sem.at[i])

    def edge_copies(i, at):
        return (
            pltpu.make_async_copy(edges.at[0, i, at], outs[i].at[at, :, pl.ds(0, TILE)], low_sem.at[i, at]),
            pltpu.make_async_copy(edges.at[1, i, at], outs[i].at[at, :, pl.ds(COLS - TILE, TILE)], high_sem.at[i, at]),
        )

    def lanes(x, by):
        return pltpu.roll(x, TILE - 1 if by > 0 else 1, 1)

    def rows(x, by):
        return pltpu.roll(x, TALL - 1 if by > 0 else 1, 0)

    def tall(body, north, south):
        pad = jnp.zeros((6, TILE), F32)
        return jnp.concatenate([pad, south, body, north, pad], axis=0)

    def extended(f):
        shift = (TILE - 2 * f) & (TILE - 1)
        base = tall(
            win[f],
            jnp.concatenate([corner[k, pl.ds(f, 1), :] for k in (0, 1)], axis=0),
            jnp.concatenate([corner[k, pl.ds(f, 1), :] for k in (2, 3)], axis=0),
        )
        return jnp.where(ghost_lane, pltpu.roll(side[...], shift, 1), base)

    @pl.when(level == 0)
    def _():
        for i in range(4):
            mid_copy(i).start()
        odd = lax.axis_index("lon") % 2 == 1
        a, b = lon_even[...], lon_odd[...]
        got = jnp.where(packed_field()((ROWS + 8, TILE)) >= 33, jnp.where(odd, b, a), jnp.where(odd, a, b))
        side[...] = tall(got[0:ROWS], got[ROWS : ROWS + 2], got[ROWS + 2 : ROWS + 4])
        e, n = extended(20), extended(21)
        for i, x in enumerate(metric(e, n, lanes, rows)):
            known[i] = x
        over[...] = jnp.zeros((TALL, TILE), F32)

    cells = [extended(LEVELS * kind + level) for kind in range(4)]
    d = extended(4 * LEVELS + level)
    blank = jnp.zeros((2, TILE), F32)
    wet, spin = tall(win[FIELDS + level], blank, blank), tall(win[FIELDS + LEVELS], blank, blank)
    new, over[...] = patch(cells, d, wet, spin, [known[i] for i in range(7)], over[...], lanes, rows)
    own = lax.broadcasted_iota(jnp.int32, (ROWS, TILE), 1)
    for i, x in enumerate(new):
        x = x[8 : 8 + ROWS]
        edges[0, i, level] = jnp.where(own < 2, x, ins[i][level, :, 0:TILE])
        edges[1, i, level] = jnp.where(own >= TILE - 2, pltpu.roll(x, TILE // 2, 1), ins[i][level, :, COLS - TILE : COLS])
        for copy in edge_copies(i, level):
            copy.start()

    @pl.when(level == LEVELS - 1)
    def _():
        for i in range(4):
            mid_copy(i).wait()
            for at in range(LEVELS):
                for copy in edge_copies(i, at):
                    copy.wait()


def sides(win, corner, lon_even, lon_odd, outs):
    return pl.pallas_call(
        sides_kernel,
        grid=(LEVELS,),
        in_specs=[VMEM] * 8,
        out_specs=[pl.BlockSpec(memory_space=pltpu.HBM)] * 4,
        out_shape=[jax.ShapeDtypeStruct((LEVELS, ROWS, COLS), F32)] * 4,
        scratch_shapes=[
            pltpu.VMEM((TALL, TILE), F32),
            pltpu.VMEM((7, TALL, TILE), F32),
            pltpu.VMEM((TALL, TILE), F32),
            pltpu.VMEM((2, 4, LEVELS, ROWS, TILE), F32),
            pltpu.SemaphoreType.DMA((4,)),
            pltpu.SemaphoreType.DMA((4, LEVELS)),
            pltpu.SemaphoreType.DMA((4, LEVELS)),
        ],
        compiler_params=PARAMS,
        name="sides",
    )(*[onto_chip(x) for x in (win, corner, lon_even, lon_odd, *outs)])


def shards(temp, salt, uvel, vvel, thick, land, east_width, north_width, coriolis):
    lats, lons = lax.axis_size("lat"), lax.axis_size("lon")
    arrays = (temp, salt, uvel, vvel, thick, land, east_width, north_width)
    near, far = pack_rows(arrays)
    near = lax.ppermute(near, AXES, lat_pairs(lats, lons, 0))
    far = lax.ppermute(far, AXES, lat_pairs(lats, lons, 1))
    win, packed = windows(arrays, coriolis)
    outs, known = inner(arrays, coriolis)
    outs = last_level(arrays, coriolis, known, outs)
    near, far, packed, *outs = lax.optimization_barrier((near, far, packed, *outs))
    packed, ghosts, corner = pack_columns(packed, near, far)
    lon_odd = lax.ppermute(packed, AXES, lon_pairs(lats, lons, 1))
    lon_even = lax.ppermute(packed, AXES, lon_pairs(lats, lons, 0))
    outs = rims(arrays, coriolis, known, ghosts, outs)
    return tuple(sides(win, corner, lon_even, lon_odd, outs))


def solution(mesh):
    deep, flat = P(None, "lat", "lon"), P("lat", "lon")
    return jax.shard_map(
        shards,
        mesh=mesh,
        in_specs=(deep,) * 6 + (flat,) * 3,
        out_specs=(deep,) * 4,
        check_vma=False,
    )
```

```python
import jax
import jax.numpy as jnp
from jax import lax
from jax.experimental import pallas as pl
from jax.experimental.pallas import tpu as pltpu
from jax.sharding import PartitionSpec as P

time_step = 0.2
biharm_coef = 0.02
alpha_temp = 0.2
beta_salt = 0.8
thin_floor = 0.25
flux_scale = time_step / 8.0 / biharm_coef

LEVELS = 4
ROWS = 64
COLS = 768
TILE = 128
TILES = COLS // TILE
CHUNKS = ROWS // 8
TALL = ROWS + 16
FIELDS = 22
KINDS = 6
GROUP = TILE // LEVELS
F32 = jnp.float32
PARAMS = pltpu.CompilerParams(vmem_limit_bytes=12 * 1024 * 1024)
AXES = ("lon", "lat")
VMEM = pl.BlockSpec(memory_space=pltpu.VMEM)


def place(lat, lon, lats, lons):
    return (lon % lons) * lats + lat


def both(pairs):
    return [p for a, b in pairs for p in ((a, b), (b, a))]


def lat_pairs(lats, lons, bit):
    pairs = [
        (place(i, j, lats, lons), place(i + 1, j, lats, lons))
        for i in range(bit, lats - 1, 2)
        for j in range(lons)
    ]
    if bit:
        pairs += [
            (place(lats - 1, j, lats, lons), place(lats - 1, lons - 1 - j, lats, lons))
            for j in range(lons // 2)
        ]
    return both(pairs)


def lon_pairs(lats, lons, bit):
    return both(
        [
            (place(i, j, lats, lons), place(i, j + 1, lats, lons))
            for i in range(lats)
            for j in range(bit, lons, 2)
        ]
    )


def onto_chip(x):
    return pltpu.with_memory_space_constraint(x, pltpu.VMEM)


def off_chip(x):
    return pltpu.with_memory_space_constraint(x, pltpu.HBM)


def rows_kernel(*refs):
    low, high, (near_ref, far_ref), stage = refs[:8], refs[8:16], refs[16:18], refs[18]
    lat = lax.axis_index("lat")
    odd = lat % 2 == 1
    top = lat == lax.axis_size("lat") - 1

    def gather(group, take, dst):
        for kind in range(5):
            for level in range(LEVELS):
                if kind < 4:
                    cells = group[kind][level]
                else:
                    cells = group[4][level] * group[5][level].astype(F32)
                for k, row in enumerate(take):
                    dst[k, kind * LEVELS + level : kind * LEVELS + level + 1, :] = cells[row : row + 1]
        for k, row in enumerate(take):
            dst[k, 20:21, :] = group[6][row : row + 1, :]
            dst[k, 21:22, :] = group[7][row : row + 1, :]

    @pl.when(odd)
    def _():
        gather(low, (0, 1), near_ref)

        @pl.when(jnp.logical_not(top))
        def _():
            gather(high, (6, 7), far_ref)

        @pl.when(top)
        def _():
            gather(high, (6, 5), stage)
            kind_row = lax.broadcasted_iota(jnp.int32, (24, TILE), 0)
            turned = jnp.logical_and(kind_row >= 2 * LEVELS, kind_row < 4 * LEVELS)
            sign = jnp.where(turned, -1.0, 1.0).astype(F32)
            flip = TILE - 1 - lax.broadcasted_iota(jnp.int32, (24, TILE), 1)
            for k in range(2):
                for t in range(COLS // TILE):
                    src = stage[k, :, COLS - TILE * (t + 1) : COLS - TILE * t]
                    rev = jnp.take_along_axis(src, flip, axis=1, mode="promise_in_bounds")
                    far_ref[k, :, TILE * t : TILE * (t + 1)] = rev * sign

    @pl.when(jnp.logical_not(odd))
    def _():
        gather(high, (6, 7), near_ref)
        gather(low, (0, 1), far_ref)


def pack_rows(arrays):
    def spec(a, at):
        if a.ndim == 3:
            return pl.BlockSpec((LEVELS, 8, COLS), lambda i: (0, at, 0))
        return pl.BlockSpec((8, COLS), lambda i: (at, 0))

    whole = pl.BlockSpec((2, 24, COLS), lambda i: (0, 0, 0))
    shape = pltpu.VMEM((2, 24, COLS), F32)
    return pl.pallas_call(
        rows_kernel,
        grid=(1,),
        in_specs=[spec(a, 0) for a in arrays] + [spec(a, ROWS // 8 - 1) for a in arrays],
        out_specs=[pl.BlockSpec(memory_space=pltpu.VMEM)] * 2,
        out_shape=[shape, shape],
        scratch_shapes=[pltpu.VMEM((2, 24, COLS), F32)],
        compiler_params=PARAMS,
        name="pack_rows",
    )(*[off_chip(x) for x in (*arrays, *arrays)])


def slot_of(shape):
    return ((lax.broadcasted_iota(jnp.int32, shape, len(shape) - 1) + 2) & (GROUP - 1)) >> 1


def level_of(shape):
    return ((lax.broadcasted_iota(jnp.int32, shape, len(shape) - 1) + 8) >> 5) & (LEVELS - 1)


def join_ends(low, high):
    lane = lax.broadcasted_iota(jnp.int32, low.shape, len(low.shape) - 1)
    return jnp.where(lane < 8, low, pltpu.roll(high, 16, len(low.shape) - 1))


def windows_kernel(temp, salt, uvel, vvel, thick, land, ewid, nwid, cori, win, packed):
    shape = (ROWS, TILE)
    lane = lax.broadcasted_iota(jnp.int32, shape, 1)
    slot = slot_of(shape)
    ends = (slice(0, TILE), slice(COLS - TILE, COLS))
    total = jnp.zeros(shape, F32)

    def spread(parts):
        whole = parts[0]
        for level in range(1, len(parts)):
            whole = jnp.where(lane >= GROUP * level, pltpu.roll(parts[level], GROUP * level, 1), whole)
        return whole

    def at(kind, level, cut):
        if kind < 4:
            return (temp, salt, uvel, vvel)[kind][level, :, cut]
        if kind == 4:
            return thick[level, :, cut] * land[level, :, cut].astype(F32)
        if kind == 5:
            return (ewid, nwid)[level][:, cut]
        if kind == 6:
            return land[level, :, cut].astype(F32)
        return cori[:, cut]

    for kind in range(KINDS + 2):
        count = (LEVELS, 2, LEVELS, 1)[max(kind - 4, 0)]
        parts = [join_ends(*[at(kind, level, cut) for cut in ends]) for level in range(count)]
        cells = spread(parts * LEVELS if count == 1 else parts)
        win[kind] = cells
        if kind < KINDS:
            total = jnp.where(slot == 9 + kind, pltpu.roll(cells, 16 + 2 * kind, 1), total)
            total = jnp.where(slot == kind, pltpu.roll(cells, TILE - 16 + 2 * kind, 1), total)
    packed[...] = total


def windows(arrays, coriolis):
    return pl.pallas_call(
        windows_kernel,
        in_specs=[VMEM] * 9,
        out_specs=[VMEM] * 2,
        out_shape=[pltpu.VMEM((KINDS + 2, ROWS, TILE), F32), pltpu.VMEM((ROWS, TILE), F32)],
        compiler_params=PARAMS,
        name="windows",
    )(*[onto_chip(x) for x in (*arrays, coriolis)])


def columns_kernel(packed, near, far, out, ghosts, corner):
    lat = lax.axis_index("lat")
    odd = lat % 2 == 1
    out[0:ROWS, :] = packed[...]
    row = lax.broadcasted_iota(jnp.int32, (24, COLS), 0)
    fill = jnp.logical_and(lat == 0, row >= 20)
    lane = lax.broadcasted_iota(jnp.int32, (24, TILE), 1)
    small_row = lax.broadcasted_iota(jnp.int32, (24, TILE), 0)
    mine = jnp.logical_and(lane >> 5 == small_row & (LEVELS - 1), lane & (GROUP - 1) < 16)
    slot = slot_of((8, TILE))
    kind = lax.broadcasted_iota(jnp.int32, (8, TILE), 0)
    for k in range(2):
        a, b = near[k], far[k]
        for side in range(2):
            if side == 0:
                cells = jnp.where(odd, b, a)
            else:
                cells = jnp.where(fill, 1.0, jnp.where(odd, a, b))
            at = 2 * side + k
            ghosts[at] = cells
            ends = join_ends(cells[:, 0:TILE], cells[:, COLS - TILE : COLS])
            moved = ends
            for level in range(1, LEVELS):
                moved = jnp.where(small_row & (LEVELS - 1) == level, pltpu.roll(ends, GROUP * level, 1), moved)
            ends = jnp.where(mine, moved, 0.0)
            rows = [jnp.sum(ends[LEVELS * i : LEVELS * (i + 1)], axis=0, keepdims=True) for i in range(KINDS)]
            shown = jnp.concatenate(rows + [jnp.zeros((8 - KINDS, TILE), F32)], axis=0)
            corner[at] = shown
            east = pltpu.roll(shown, 16, 1, stride=2, stride_axis=0)
            west = pltpu.roll(shown, TILE - 16, 1, stride=2, stride_axis=0)
            sent = jnp.where(slot == kind + 9, east, jnp.where(slot == kind, west, 0.0))
            out[ROWS + at : ROWS + at + 1, :] = jnp.sum(sent[0:KINDS], axis=0, keepdims=True)
    out[ROWS + 4 : ROWS + 8, :] = jnp.zeros((4, TILE), F32)


def pack_columns(packed, near, far):
    return pl.pallas_call(
        columns_kernel,
        in_specs=[VMEM] * 3,
        out_specs=[VMEM] * 3,
        out_shape=[
            pltpu.VMEM((ROWS + 8, TILE), F32),
            pltpu.VMEM((4, 24, COLS), F32),
            pltpu.VMEM((4, 8, TILE), F32),
        ],
        compiler_params=PARAMS,
        name="pack_columns",
    )(*[onto_chip(x) for x in (packed, near, far)])


def north_of(here, above):
    sub = lax.broadcasted_iota(jnp.int32, here.shape, 0)
    return pltpu.roll(jnp.where(sub == 0, above, here), 7, 0)


def south_of(here, below):
    sub = lax.broadcasted_iota(jnp.int32, here.shape, 0)
    return pltpu.roll(jnp.where(sub == 7, below, here), 1, 0)


def tile(t):
    return slice(TILE * t, TILE * t + TILE)


def turn_e(x):
    return pltpu.roll(x, TILE - 1, 1)


def turn_w(x):
    return pltpu.roll(x, 1, 1)


def around(c):
    r = pl.multiple_of(8 * c, 8)
    up = pl.multiple_of(8 * jnp.minimum(c + 1, CHUNKS - 1), 8)
    down = pl.multiple_of(8 * jnp.maximum(c - 1, 0), 8)
    return pl.ds(r, 8), pl.ds(up, 8), pl.ds(down, 8)


def inner_metric(ewid, nwid, known, over, over_e):
    ratio_e, ratio_n, span_e, span_n, inv_area, half_e, half_n = known
    last = lax.broadcasted_iota(jnp.int32, (8, TILE), 1) == TILE - 1

    def chunk(c, _):
        here, above, _ = around(c)
        east = [(ewid[here, tile(0)], nwid[here, tile(0)])]
        east = [tuple((x, turn_e(x)) for x in east[0])]
        for t in range(TILES):
            (e, re), (n, rn) = east[t]
            u = (t + 1) % TILES
            if u:
                east.append(tuple((x, turn_e(x)) for x in (ewid[here, tile(u)], nwid[here, tile(u)])))
            else:
                east.append(east[0])
            ee = jnp.where(last, east[t + 1][0][1], re)
            ne = jnp.where(last, east[t + 1][1][1], rn)
            en = north_of(e, ewid[above, tile(t)])
            nn = north_of(n, nwid[above, tile(t)])
            ratio_e[here, tile(t)] = (n + ne) / (e + ee)
            ratio_n[here, tile(t)] = (e + en) / (n + nn)
            span_e[here, tile(t)] = flux_scale * (n + ne)
            span_n[here, tile(t)] = flux_scale * (e + en)
            inv_area[here, tile(t)] = 1.0 / (e * n)
            half_e[here, tile(t)] = (0.5 * time_step) / e
            half_n[here, tile(t)] = (0.5 * time_step) / n
            over[here, tile(t)] = jnp.zeros((8, TILE), F32)
            over_e[here, tile(t)] = jnp.zeros((8, TILE), F32)
        return 0

    lax.fori_loop(0, CHUNKS, chunk, 0)


def inner_level(level, fields, outs, known, work, over, over_e, keep):
    temp, salt, uvel, vvel, thick, land, ewid, nwid, cori = fields
    ratio_e, ratio_n, span_e, span_n, inv_area, half_e, half_n = known
    deep, coef_e, coef_n, inv_vol, move_n, flux_t, flux_s, pres, slope, lap = work
    lane = lax.broadcasted_iota(jnp.int32, (8, TILE), 1)
    first, last = lane == 0, lane == TILE - 1
    data = (temp, salt, uvel, vvel)

    for r in range(0, ROWS, 8):
        deep[r : r + 8, :] = thick[level, r : r + 8, :] * land[level, r : r + 8, :].astype(F32)

    def laps(c, _):
        here, above, below = around(c)

        def turned_at(t):
            cells = [x[level, here, tile(t)] for x in data] + [deep[here, tile(t)]]
            return [(x, turn_e(x)) for x in cells]

        def zonal(t, turned, ahead):
            d, rd = turned[4]
            de = jnp.where(last, ahead[4][1], rd)
            lon_thick = jnp.minimum(d, de)
            ce = lon_thick * ratio_e[here, tile(t)]
            east = [jnp.where(last, ahead[f][1], turned[f][1]) for f in range(4)]
            flux = [ce * (east[f] - turned[f][0]) for f in range(4)]
            te = lon_thick * span_e[here, tile(t)] * (turned[2][0] + east[2])
            be = (beta_salt * east[1] - alpha_temp * east[0]) * de
            before = over_e[here, tile(t)]
            pe = before + 0.5 * be
            if keep:
                over_e[here, tile(t)] = before + be
            return ce, flux, te, east, pe

        end, start = turned_at(TILES - 1), turned_at(0)
        kept = zonal(TILES - 1, end, start)
        behind, behind_pe = [turn_w(x) for x in kept[1]], pltpu.roll(kept[4], 2, 1)
        kept_flux, kept_pe = behind, behind_pe
        turned = start
        for t in range(TILES):
            if t < TILES - 1:
                ahead = turned_at(t + 1) if t < TILES - 2 else end
                ce, flux, te, east, pe = zonal(t, turned, ahead)
                turned_flux, turned_pe = [turn_w(x) for x in flux], pltpu.roll(pe, 2, 1)
            else:
                ce, flux, te, east, pe = kept
                turned_flux, turned_pe = kept_flux, kept_pe
            coef_e[here, tile(t)] = ce
            d = turned[4][0]
            dn, ds = north_of(d, deep[above, tile(t)]), south_of(d, deep[below, tile(t)])
            lat_thick = jnp.minimum(d, dn)
            rn = ratio_n[here, tile(t)]
            cn = lat_thick * rn
            cs = jnp.minimum(ds, d) * south_of(rn, ratio_n[below, tile(t)])
            iv = inv_area[here, tile(t)] / jnp.maximum(d, thin_floor)
            coef_n[here, tile(t)] = cn
            inv_vol[here, tile(t)] = iv
            for f in range(4):
                q = turned[f][0]
                qn, qs = north_of(q, data[f][level, above, tile(t)]), south_of(q, data[f][level, below, tile(t)])
                west = jnp.where(first, behind[f], turned_flux[f])
                lap[f, here, tile(t)] = (flux[f] - west + cn * (qn - q) - cs * (q - qs)) * iv
                if f == 3:
                    move_n[here, tile(t)] = lat_thick * span_n[here, tile(t)] * (q + qn)
            q0, q1 = turned[0][0], turned[1][0]
            flux_t[here, tile(t)] = te * (q0 + east[0])
            flux_s[here, tile(t)] = te * (q1 + east[1])
            b = (beta_salt * q1 - alpha_temp * q0) * d
            before = over[here, tile(t)]
            pres[here, tile(t)] = before + 0.5 * b
            if keep:
                over[here, tile(t)] = before + b
            slope[here, tile(t)] = pe - jnp.where(lane < 2, behind_pe, turned_pe)
            behind, behind_pe, turned = turned_flux, turned_pe, ahead
        return 0

    lax.fori_loop(0, CHUNKS, laps, 0, unroll=2)

    def finish(c, _):
        here, above, below = around(c)

        def turned_at(t):
            return [(x, turn_e(x)) for x in (lap[f, here, tile(t)] for f in range(4))]

        def zonal(t, turned, ahead):
            ce = coef_e[here, tile(t)]
            flux = [ce * (jnp.where(last, ahead[f][1], turned[f][1]) - turned[f][0]) for f in range(4)]
            flux[0] = flux[0] + flux_t[here, tile(t)]
            flux[1] = flux[1] + flux_s[here, tile(t)]
            return flux

        end, start = turned_at(TILES - 1), turned_at(0)
        kept = zonal(TILES - 1, end, start)
        kept_turned = [turn_w(x) for x in kept]
        behind, turned = kept_turned, start
        for t in range(TILES):
            if t < TILES - 1:
                ahead = turned_at(t + 1) if t < TILES - 2 else end
                flux = zonal(t, turned, ahead)
                turned_flux = [turn_w(x) for x in flux]
            else:
                flux, turned_flux = kept, kept_turned
            cn = coef_n[here, tile(t)]
            cs = south_of(cn, coef_n[below, tile(t)])
            iv = biharm_coef * inv_vol[here, tile(t)]
            gn = move_n[here, tile(t)]
            gs = south_of(gn, move_n[below, tile(t)])
            wet = land[level, here, tile(t)].astype(F32)
            u, v = uvel[level, here, tile(t)], vvel[level, here, tile(t)]
            turning = time_step * cori[here, tile(t)]
            for f in range(4):
                m = turned[f][0]
                mn, ms = north_of(m, lap[f, above, tile(t)]), south_of(m, lap[f, below, tile(t)])
                west = jnp.where(first, behind[f], turned_flux[f])
                total = flux[f] - west + cn * (mn - m) - cs * (m - ms)
                if f < 2:
                    q = data[f][level, here, tile(t)]
                    qn, qs = north_of(q, data[f][level, above, tile(t)]), south_of(q, data[f][level, below, tile(t)])
                    total = total + gn * (q + qn) - gs * (qs + q)
                    change = wet * (q - total * iv)
                elif f == 2:
                    change = wet * (u + turning * v - slope[here, tile(t)] * half_e[here, tile(t)] - total * iv)
                else:
                    p = pres[here, tile(t)]
                    rise = north_of(p, pres[above, tile(t)]) - south_of(p, pres[below, tile(t)])
                    change = wet * (v - turning * u - rise * half_n[here, tile(t)] - total * iv)
                outs[f][level, here, tile(t)] = change
            behind, turned = turned_flux, ahead
        return 0

    lax.fori_loop(0, CHUNKS, finish, 0, unroll=2)


WORK = [pltpu.VMEM((ROWS, COLS), F32)] * 9 + [pltpu.VMEM((4, ROWS, COLS), F32)]


def inner_kernel(*refs):
    fields, outs, known, over, over_e, work = refs[:9], refs[9:13], refs[13:20], refs[20], refs[21], refs[22:]
    level = pl.program_id(0)

    @pl.when(level == 0)
    def _():
        inner_metric(fields[6], fields[7], known, over, over_e)

    inner_level(level, fields, outs, known, work, over, over_e, True)


def inner(arrays, coriolis):
    out = [pltpu.VMEM((LEVELS, ROWS, COLS), F32)] * 4 + [pltpu.VMEM((ROWS, COLS), F32)] * 9
    done = pl.pallas_call(
        inner_kernel,
        grid=(LEVELS - 1,),
        in_specs=[VMEM] * 9,
        out_specs=[VMEM] * 13,
        out_shape=out,
        scratch_shapes=WORK,
        compiler_params=PARAMS,
        name="inner",
    )(*[onto_chip(x) for x in (*arrays, coriolis)])
    return done[:4], done[4:]


def metric(e, n, lanes, rows):
    ee, ne, en, nn = lanes(e, 1), lanes(n, 1), rows(e, 1), rows(n, 1)
    return (
        (n + ne) / (e + ee),
        (e + en) / (n + nn),
        flux_scale * (n + ne),
        flux_scale * (e + en),
        1.0 / (e * n),
        (0.5 * time_step) / e,
        (0.5 * time_step) / n,
    )


def patch(cells, d, wet, cori, known, overhead, lanes, rows):
    ratio_e, ratio_n, span_e, span_n, inv_area, half_e, half_n = known
    temp, salt, uvel, vvel = cells
    de, dn = lanes(d, 1), rows(d, 1)
    lon_thick, lat_thick = jnp.minimum(d, de), jnp.minimum(d, dn)
    ce, cn = lon_thick * ratio_e, lat_thick * ratio_n
    cs = rows(cn, -1)
    iv = inv_area / jnp.maximum(d, thin_floor)
    b = (beta_salt * salt - alpha_temp * temp) * d
    p = overhead(b) + 0.5 * b
    ge = (lanes(p, 1) - lanes(p, -1)) * half_e
    gn = (rows(p, 1) - rows(p, -1)) * half_n
    outs = []
    te = tn = None
    for f in (2, 3, 0, 1):
        q = cells[f]
        qe, qn, qs = lanes(q, 1), rows(q, 1), rows(q, -1)
        if f == 2:
            te = lon_thick * span_e * (q + qe)
        if f == 3:
            tn = lat_thick * span_n * (q + qn)
            ts = rows(tn, -1)
        fe = ce * (qe - q)
        m = (fe - lanes(fe, -1) + cn * (qn - q) - cs * (q - qs)) * iv
        fe = ce * (lanes(m, 1) - m)
        if f < 2:
            fe = fe + te * (q + qe)
        total = fe - lanes(fe, -1) + cn * (rows(m, 1) - m) - cs * (m - rows(m, -1))
        if f < 2:
            total = total + tn * (q + qn) - ts * (qs + q)
        change = q - biharm_coef * iv * total
        if f == 2:
            change = change + time_step * cori * vvel - ge
        if f == 3:
            change = change - time_step * cori * uvel - gn
        outs.append(wet * change)
    return outs[2], outs[3], outs[0], outs[1]


def rims_level(level, fields, ghosts, outs, known, spin, over):
    temp, salt, uvel, vvel, thick, land, ewid, nwid, cori = fields
    sub = lax.broadcasted_iota(jnp.int32, (8, COLS), 0)
    low, high = slice(0, 8), slice(ROWS - 8, ROWS)

    def lanes(x, by):
        return pltpu.roll(x, COLS - 1 if by > 0 else 1, 2)

    def rows(x, by):
        return pltpu.roll(x, 7 if by > 0 else 1, 1)

    def strips(f, south, north):
        g = [ghosts[k, pl.ds(f, 1), :] for k in range(4)]
        s = jnp.where(sub == 0, g[2], jnp.where(sub == 1, g[3], pltpu.roll(south, 2, 0)))
        n = jnp.where(sub == 6, g[0], jnp.where(sub == 7, g[1], pltpu.roll(north, 6, 0)))
        return jnp.stack([s, n])

    def own(south, north):
        return jnp.stack([pltpu.roll(south, 2, 0), pltpu.roll(north, 6, 0)])

    @pl.when(level == 0)
    def _():
        e = strips(20, ewid[low, :], ewid[high, :])
        n = strips(21, nwid[low, :], nwid[high, :])
        for i, x in enumerate(metric(e, n, lanes, rows)):
            known[i] = x
        spin[...] = own(cori[low, :], cori[high, :])
        over[...] = jnp.zeros((2, 8, COLS), F32)

    cells = [
        strips(LEVELS * kind + level, x[level, low, :], x[level, high, :])
        for kind, x in enumerate((temp, salt, uvel, vvel))
    ]
    wet_low, wet_high = land[level, low, :].astype(F32), land[level, high, :].astype(F32)
    d = strips(4 * LEVELS + level, thick[level, low, :] * wet_low, thick[level, high, :] * wet_high)

    def overhead(b):
        before = over[...]
        over[...] = before + b
        return before

    new = patch(
        cells, d, own(wet_low, wet_high), spin[...], [known[i] for i in range(7)], overhead, lanes, rows
    )
    for x, (old, out) in zip(new, outs):
        out[level, low, :] = jnp.where(sub < 2, pltpu.roll(x[0], 6, 0), old[level, low, :])
        out[level, high, :] = jnp.where(sub >= 6, pltpu.roll(x[1], 2, 0), old[level, high, :])


def runs_late():
    lon, lons = lax.axis_index("lon"), lax.axis_size("lon")
    top = lax.axis_index("lat") == lax.axis_size("lat") - 1
    late = jnp.logical_or(lon == lons - 1, lon == lons // 2)
    return jnp.where(top, lon == 0, late)


def last_kernel(*refs):
    fields, known, over, over_e, outs, work = refs[:9], refs[9:16], refs[16], refs[17], refs[22:26], refs[26:]

    @pl.when(jnp.logical_not(runs_late()))
    def _():
        inner_level(LEVELS - 1, fields, outs, known, work, over, over_e, False)


def rims_kernel(*refs):
    fields, known, over, over_e, ghosts = refs[:9], refs[9:16], refs[16], refs[17], refs[18]
    outs, rim_known, spin, rim_over, work = refs[23:27], refs[27], refs[28], refs[29], refs[30:]
    level = pl.program_id(0)

    @pl.when(jnp.logical_and(runs_late(), level == 0))
    def _():
        inner_level(LEVELS - 1, fields, outs, known, work, over, over_e, False)

    rims_level(level, fields, ghosts, list(zip(outs, outs)), rim_known, spin, rim_over)


def last_level(arrays, coriolis, known, outs):
    return pl.pallas_call(
        last_kernel,
        in_specs=[VMEM] * 22,
        out_specs=[VMEM] * 4,
        out_shape=[pltpu.VMEM((LEVELS, ROWS, COLS), F32)] * 4,
        scratch_shapes=WORK,
        input_output_aliases={18: 0, 19: 1, 20: 2, 21: 3},
        compiler_params=PARAMS,
        name="last_level",
    )(*[onto_chip(x) for x in (*arrays, coriolis, *known, *outs)])


def rims(arrays, coriolis, known, ghosts, outs):
    return pl.pallas_call(
        rims_kernel,
        grid=(LEVELS,),
        in_specs=[VMEM] * 23,
        out_specs=[VMEM] * 4,
        out_shape=[pltpu.VMEM((LEVELS, ROWS, COLS), F32)] * 4,
        scratch_shapes=[
            pltpu.VMEM((7, 2, 8, COLS), F32),
            pltpu.VMEM((2, 8, COLS), F32),
            pltpu.VMEM((2, 8, COLS), F32),
        ]
        + WORK,
        input_output_aliases={19: 0, 20: 1, 21: 2, 22: 3},
        compiler_params=PARAMS,
        name="rims",
    )(*[onto_chip(x) for x in (*arrays, coriolis, *known, ghosts, *outs)])


def sides_kernel(
    win, corner, lon_even, lon_odd, temp_in, salt_in, uvel_in, vvel_in,
    temp_out, salt_out, uvel_out, vvel_out,
    side, edges, mid_sem, low_sem, high_sem,
):
    ins, outs = (temp_in, salt_in, uvel_in, vvel_in), (temp_out, salt_out, uvel_out, vvel_out)
    shape = (TALL, TILE)
    level, slot = level_of(shape), slot_of(shape)
    ghost_lane = jnp.logical_or(slot == 0, slot == 9)
    middle = pl.ds(TILE, COLS - 2 * TILE)

    def middle_copy(i):
        return pltpu.make_async_copy(ins[i].at[:, :, middle], outs[i].at[:, :, middle], mid_sem.at[i])

    def low_copy(i):
        return pltpu.make_async_copy(edges.at[0, i], outs[i].at[:, :, pl.ds(0, TILE)], low_sem.at[i])

    def high_copy(i):
        return pltpu.make_async_copy(edges.at[1, i], outs[i].at[:, :, pl.ds(COLS - TILE, TILE)], high_sem.at[i])

    for i in range(4):
        middle_copy(i).start()

    def lanes(x, by):
        return pltpu.roll(x, TILE - 1 if by > 0 else 1, 1)

    def rows(x, by):
        return pltpu.roll(x, TALL - 1 if by > 0 else 1, 0)

    def tall(body, north, south):
        pad = jnp.zeros((6, TILE), F32)
        return jnp.concatenate([pad, south, body, north, pad], axis=0)

    odd = lax.axis_index("lon") % 2 == 1
    a, b = lon_even[...], lon_odd[...]
    got = jnp.where(slot_of((ROWS + 8, TILE)) >= 9, jnp.where(odd, b, a), jnp.where(odd, a, b))
    side[...] = tall(got[0:ROWS], got[ROWS : ROWS + 2], got[ROWS + 2 : ROWS + 4])

    def extended(kind):
        ends = [jnp.concatenate([corner[k, kind : kind + 1, :] for k in pair], axis=0) for pair in ((0, 1), (2, 3))]
        came = side[...]
        if kind:
            came = pltpu.roll(came, TILE - 2 * kind, 1)
        return jnp.where(ghost_lane, came, tall(win[kind], *ends))

    def everywhere(x):
        return jnp.where(level < 2, x, pltpu.roll(x, 2 * GROUP, 1))

    pair = extended(5)
    e = everywhere(jnp.where(level == 0, pair, pltpu.roll(pair, GROUP, 1)))
    n = everywhere(jnp.where(level == 0, pltpu.roll(pair, TILE - GROUP, 1), pair))

    def overhead(b):
        total = jnp.where(level > 0, pltpu.roll(b, GROUP, 1), 0.0)
        for up in (2, 3):
            total = total + jnp.where(level >= up, pltpu.roll(b, GROUP * up, 1), 0.0)
        return total

    cells = [extended(kind) for kind in range(4)]
    blank = jnp.zeros((2, TILE), F32)
    wet, spin = tall(win[KINDS], blank, blank), tall(win[KINDS + 1], blank, blank)
    new = patch(cells, extended(4), wet, spin, metric(e, n, lanes, rows), overhead, lanes, rows)
    lane = lax.broadcasted_iota(jnp.int32, (ROWS, TILE), 1)
    for i, x in enumerate(new):
        x = x[8 : 8 + ROWS]
        x = jnp.where(lane & (GROUP - 1) < 8, x, pltpu.roll(x, TILE - 16, 1))
        for at in range(LEVELS):
            own = pltpu.roll(x, TILE - GROUP * at, 1) if at else x
            edges[0, i, at] = jnp.where(lane < 2, own, ins[i][at, :, 0:TILE])
            edges[1, i, at] = jnp.where(lane >= TILE - 2, own, ins[i][at, :, COLS - TILE : COLS])
        low_copy(i).start()
        high_copy(i).start()
    for i in range(4):
        middle_copy(i).wait()
        low_copy(i).wait()
        high_copy(i).wait()


def sides(win, corner, lon_even, lon_odd, outs):
    return pl.pallas_call(
        sides_kernel,
        in_specs=[VMEM] * 8,
        out_specs=[pl.BlockSpec(memory_space=pltpu.HBM)] * 4,
        out_shape=[jax.ShapeDtypeStruct((LEVELS, ROWS, COLS), F32)] * 4,
        scratch_shapes=[
            pltpu.VMEM((TALL, TILE), F32),
            pltpu.VMEM((2, 4, LEVELS, ROWS, TILE), F32),
            pltpu.SemaphoreType.DMA((4,)),
            pltpu.SemaphoreType.DMA((4,)),
            pltpu.SemaphoreType.DMA((4,)),
        ],
        compiler_params=PARAMS,
        name="sides",
    )(*[onto_chip(x) for x in (win, corner, lon_even, lon_odd, *outs)])


def shards(temp, salt, uvel, vvel, thick, land, east_width, north_width, coriolis):
    lats, lons = lax.axis_size("lat"), lax.axis_size("lon")
    arrays = (temp, salt, uvel, vvel, thick, land, east_width, north_width)
    near, far = pack_rows(arrays)
    near = lax.ppermute(near, AXES, lat_pairs(lats, lons, 0))
    far = lax.ppermute(far, AXES, lat_pairs(lats, lons, 1))
    win, packed = windows(arrays, coriolis)
    outs, known = inner(arrays, coriolis)
    outs = last_level(arrays, coriolis, known, outs)
    near, far, packed, *outs = lax.optimization_barrier((near, far, packed, *outs))
    packed, ghosts, corner = pack_columns(packed, near, far)
    lon_odd = lax.ppermute(packed, AXES, lon_pairs(lats, lons, 1))
    lon_even = lax.ppermute(packed, AXES, lon_pairs(lats, lons, 0))
    outs = rims(arrays, coriolis, known, ghosts, outs)
    return tuple(sides(win, corner, lon_even, lon_odd, outs))


def solution(mesh):
    deep, flat = P(None, "lat", "lon"), P("lat", "lon")
    return jax.shard_map(
        shards,
        mesh=mesh,
        in_specs=(deep,) * 6 + (flat,) * 3,
        out_specs=(deep,) * 4,
        check_vma=False,
    )
```

```python
import jax
import jax.numpy as jnp
from jax import lax
from jax.experimental import pallas as pl
from jax.experimental.pallas import tpu as pltpu
from jax.sharding import PartitionSpec as P

time_step = 0.2
biharm_coef = 0.02
alpha_temp = 0.2
beta_salt = 0.8
thin_floor = 0.25
flux_scale = time_step / 8.0 / biharm_coef

LEVELS = 4
ROWS = 64
COLS = 768
TILE = 128
TILES = COLS // TILE
CHUNKS = ROWS // 8
TALL = ROWS + 16
FIELDS = 22
AHEAD = 2
KINDS = 6
GROUP = TILE // LEVELS
F32 = jnp.float32
PARAMS = pltpu.CompilerParams(vmem_limit_bytes=12 * 1024 * 1024)
AXES = ("lon", "lat")
VMEM = pl.BlockSpec(memory_space=pltpu.VMEM)


def place(lat, lon, lats, lons):
    return (lon % lons) * lats + lat


def both(pairs):
    return [p for a, b in pairs for p in ((a, b), (b, a))]


def lat_pairs(lats, lons, bit):
    pairs = [
        (place(i, j, lats, lons), place(i + 1, j, lats, lons))
        for i in range(bit, lats - 1, 2)
        for j in range(lons)
    ]
    if bit:
        pairs += [
            (place(lats - 1, j, lats, lons), place(lats - 1, lons - 1 - j, lats, lons))
            for j in range(lons // 2)
        ]
    return both(pairs)


def lon_pairs(lats, lons, bit):
    return both(
        [
            (place(i, j, lats, lons), place(i, j + 1, lats, lons))
            for i in range(lats)
            for j in range(bit, lons, 2)
        ]
    )


def onto_chip(x):
    return pltpu.with_memory_space_constraint(x, pltpu.VMEM)


def off_chip(x):
    return pltpu.with_memory_space_constraint(x, pltpu.HBM)


def rows_kernel(*refs):
    low, high, (near_ref, far_ref), stage = refs[:8], refs[8:16], refs[16:18], refs[18]
    lat = lax.axis_index("lat")
    odd = lat % 2 == 1
    top = lat == lax.axis_size("lat") - 1

    def gather(group, take, dst):
        for kind in range(5):
            for level in range(LEVELS):
                if kind < 4:
                    cells = group[kind][level]
                else:
                    cells = group[4][level] * group[5][level].astype(F32)
                for k, row in enumerate(take):
                    dst[k, kind * LEVELS + level : kind * LEVELS + level + 1, :] = cells[row : row + 1]
        for k, row in enumerate(take):
            dst[k, 20:21, :] = group[6][row : row + 1, :]
            dst[k, 21:22, :] = group[7][row : row + 1, :]

    @pl.when(odd)
    def _():
        gather(low, (0, 1), near_ref)

        @pl.when(jnp.logical_not(top))
        def _():
            gather(high, (6, 7), far_ref)

        @pl.when(top)
        def _():
            gather(high, (6, 5), stage)
            kind_row = lax.broadcasted_iota(jnp.int32, (24, TILE), 0)
            turned = jnp.logical_and(kind_row >= 2 * LEVELS, kind_row < 4 * LEVELS)
            sign = jnp.where(turned, -1.0, 1.0).astype(F32)
            flip = TILE - 1 - lax.broadcasted_iota(jnp.int32, (24, TILE), 1)
            for k in range(2):
                for t in range(COLS // TILE):
                    src = stage[k, :, COLS - TILE * (t + 1) : COLS - TILE * t]
                    rev = jnp.take_along_axis(src, flip, axis=1, mode="promise_in_bounds")
                    far_ref[k, :, TILE * t : TILE * (t + 1)] = rev * sign

    @pl.when(jnp.logical_not(odd))
    def _():
        gather(high, (6, 7), near_ref)
        gather(low, (0, 1), far_ref)


def pack_rows(arrays):
    def spec(a, at):
        if a.ndim == 3:
            return pl.BlockSpec((LEVELS, 8, COLS), lambda i: (0, at, 0))
        return pl.BlockSpec((8, COLS), lambda i: (at, 0))

    whole = pl.BlockSpec((2, 24, COLS), lambda i: (0, 0, 0))
    shape = pltpu.VMEM((2, 24, COLS), F32)
    return pl.pallas_call(
        rows_kernel,
        grid=(1,),
        in_specs=[spec(a, 0) for a in arrays] + [spec(a, ROWS // 8 - 1) for a in arrays],
        out_specs=[pl.BlockSpec(memory_space=pltpu.VMEM)] * 2,
        out_shape=[shape, shape],
        scratch_shapes=[pltpu.VMEM((2, 24, COLS), F32)],
        compiler_params=PARAMS,
        name="pack_rows",
    )(*[off_chip(x) for x in (*arrays, *arrays)])


def slot_of(shape):
    return ((lax.broadcasted_iota(jnp.int32, shape, len(shape) - 1) + 2) & (GROUP - 1)) >> 1


def level_of(shape):
    return ((lax.broadcasted_iota(jnp.int32, shape, len(shape) - 1) + 8) >> 5) & (LEVELS - 1)


def join_ends(low, high):
    lane = lax.broadcasted_iota(jnp.int32, low.shape, len(low.shape) - 1)
    return jnp.where(lane < 8, low, pltpu.roll(high, 16, len(low.shape) - 1))


def windows_kernel(temp, salt, uvel, vvel, thick, land, ewid, nwid, cori, win, packed):
    shape = (ROWS, TILE)
    lane = lax.broadcasted_iota(jnp.int32, shape, 1)
    slot = slot_of(shape)
    ends = (slice(0, TILE), slice(COLS - TILE, COLS))
    total = jnp.zeros(shape, F32)

    def spread(parts):
        whole = parts[0]
        for level in range(1, len(parts)):
            whole = jnp.where(lane >= GROUP * level, pltpu.roll(parts[level], GROUP * level, 1), whole)
        return whole

    def at(kind, level, cut):
        if kind < 4:
            return (temp, salt, uvel, vvel)[kind][level, :, cut]
        if kind == 4:
            return thick[level, :, cut] * land[level, :, cut].astype(F32)
        if kind == 5:
            return (ewid, nwid)[level][:, cut]
        if kind == 6:
            return land[level, :, cut].astype(F32)
        return cori[:, cut]

    for kind in range(KINDS + 2):
        count = (LEVELS, 2, LEVELS, 1)[max(kind - 4, 0)]
        parts = [join_ends(*[at(kind, level, cut) for cut in ends]) for level in range(count)]
        cells = spread(parts * LEVELS if count == 1 else parts)
        win[kind] = cells
        if kind < KINDS:
            total = jnp.where(slot == 9 + kind, pltpu.roll(cells, 16 + 2 * kind, 1), total)
            total = jnp.where(slot == kind, pltpu.roll(cells, TILE - 16 + 2 * kind, 1), total)
    packed[...] = total


def windows(arrays, coriolis):
    return pl.pallas_call(
        windows_kernel,
        in_specs=[VMEM] * 9,
        out_specs=[VMEM] * 2,
        out_shape=[pltpu.VMEM((KINDS + 2, ROWS, TILE), F32), pltpu.VMEM((ROWS, TILE), F32)],
        compiler_params=PARAMS,
        name="windows",
    )(*[onto_chip(x) for x in (*arrays, coriolis)])


def columns_kernel(packed, near, far, out, ghosts, corner):
    lat = lax.axis_index("lat")
    odd = lat % 2 == 1
    out[0:ROWS, :] = packed[...]
    row = lax.broadcasted_iota(jnp.int32, (24, COLS), 0)
    fill = jnp.logical_and(lat == 0, row >= 20)
    lane = lax.broadcasted_iota(jnp.int32, (24, TILE), 1)
    small_row = lax.broadcasted_iota(jnp.int32, (24, TILE), 0)
    mine = jnp.logical_and(lane >> 5 == small_row & (LEVELS - 1), lane & (GROUP - 1) < 16)
    slot = slot_of((8, TILE))
    kind = lax.broadcasted_iota(jnp.int32, (8, TILE), 0)
    for k in range(2):
        a, b = near[k], far[k]
        for side in range(2):
            if side == 0:
                cells = jnp.where(odd, b, a)
            else:
                cells = jnp.where(fill, 1.0, jnp.where(odd, a, b))
            at = 2 * side + k
            ghosts[at] = cells
            ends = join_ends(cells[:, 0:TILE], cells[:, COLS - TILE : COLS])
            moved = ends
            for level in range(1, LEVELS):
                moved = jnp.where(small_row & (LEVELS - 1) == level, pltpu.roll(ends, GROUP * level, 1), moved)
            ends = jnp.where(mine, moved, 0.0)
            rows = [jnp.sum(ends[LEVELS * i : LEVELS * (i + 1)], axis=0, keepdims=True) for i in range(KINDS)]
            shown = jnp.concatenate(rows + [jnp.zeros((8 - KINDS, TILE), F32)], axis=0)
            corner[at] = shown
            east = pltpu.roll(shown, 16, 1, stride=2, stride_axis=0)
            west = pltpu.roll(shown, TILE - 16, 1, stride=2, stride_axis=0)
            sent = jnp.where(slot == kind + 9, east, jnp.where(slot == kind, west, 0.0))
            out[ROWS + at : ROWS + at + 1, :] = jnp.sum(sent[0:KINDS], axis=0, keepdims=True)
    out[ROWS + 4 : ROWS + 8, :] = jnp.zeros((4, TILE), F32)


def pack_columns(packed, near, far):
    return pl.pallas_call(
        columns_kernel,
        in_specs=[VMEM] * 3,
        out_specs=[VMEM] * 3,
        out_shape=[
            pltpu.VMEM((ROWS + 8, TILE), F32),
            pltpu.VMEM((4, 24, COLS), F32),
            pltpu.VMEM((4, 8, TILE), F32),
        ],
        compiler_params=PARAMS,
        name="pack_columns",
    )(*[onto_chip(x) for x in (packed, near, far)])


def north_of(here, above):
    sub = lax.broadcasted_iota(jnp.int32, here.shape, 0)
    return pltpu.roll(jnp.where(sub == 0, above, here), 7, 0)


def south_of(here, below):
    sub = lax.broadcasted_iota(jnp.int32, here.shape, 0)
    return pltpu.roll(jnp.where(sub == 7, below, here), 1, 0)


def tile(t):
    return slice(TILE * t, TILE * t + TILE)


def turn_e(x):
    return pltpu.roll(x, TILE - 1, 1)


def turn_w(x):
    return pltpu.roll(x, 1, 1)


def around(c):
    r = pl.multiple_of(8 * c, 8)
    up = pl.multiple_of(8 * jnp.minimum(c + 1, CHUNKS - 1), 8)
    down = pl.multiple_of(8 * jnp.maximum(c - 1, 0), 8)
    return pl.ds(r, 8), pl.ds(up, 8), pl.ds(down, 8)


def inner_metric(ewid, nwid, known, over, over_e):
    ratio_e, ratio_n, span_e, span_n, inv_area, half_e, half_n = known
    last = lax.broadcasted_iota(jnp.int32, (8, TILE), 1) == TILE - 1

    def chunk(c, _):
        here, above, _ = around(c)
        east = [(ewid[here, tile(0)], nwid[here, tile(0)])]
        east = [tuple((x, turn_e(x)) for x in east[0])]
        for t in range(TILES):
            (e, re), (n, rn) = east[t]
            u = (t + 1) % TILES
            if u:
                east.append(tuple((x, turn_e(x)) for x in (ewid[here, tile(u)], nwid[here, tile(u)])))
            else:
                east.append(east[0])
            ee = jnp.where(last, east[t + 1][0][1], re)
            ne = jnp.where(last, east[t + 1][1][1], rn)
            en = north_of(e, ewid[above, tile(t)])
            nn = north_of(n, nwid[above, tile(t)])
            ratio_e[here, tile(t)] = (n + ne) / (e + ee)
            ratio_n[here, tile(t)] = (e + en) / (n + nn)
            span_e[here, tile(t)] = flux_scale * (n + ne)
            span_n[here, tile(t)] = flux_scale * (e + en)
            inv_area[here, tile(t)] = 1.0 / (e * n)
            half_e[here, tile(t)] = (0.5 * time_step) / e
            half_n[here, tile(t)] = (0.5 * time_step) / n
            over[here, tile(t)] = jnp.zeros((8, TILE), F32)
            over_e[here, tile(t)] = jnp.zeros((8, TILE), F32)
        return 0

    lax.fori_loop(0, CHUNKS, chunk, 0, unroll=2)


def inner_level(level, fields, outs, known, work, over, over_e, keep):
    temp, salt, uvel, vvel, thick, land, ewid, nwid, cori = fields
    ratio_e, ratio_n, span_e, span_n, inv_area, half_e, half_n = known
    deep, coef_e, coef_n, inv_vol, move_n, flux_t, flux_s, pres, slope, lap = work
    lane = lax.broadcasted_iota(jnp.int32, (8, TILE), 1)
    first, last = lane == 0, lane == TILE - 1
    data = (temp, salt, uvel, vvel)

    for r in range(0, ROWS, 8):
        deep[r : r + 8, :] = thick[level, r : r + 8, :] * land[level, r : r + 8, :].astype(F32)

    def laps(c, _):
        here, above, below = around(c)

        def turned_at(t):
            cells = [x[level, here, tile(t)] for x in data] + [deep[here, tile(t)]]
            return [(x, turn_e(x)) for x in cells]

        def zonal(t, turned, ahead):
            d, rd = turned[4]
            de = jnp.where(last, ahead[4][1], rd)
            lon_thick = jnp.minimum(d, de)
            ce = lon_thick * ratio_e[here, tile(t)]
            east = [jnp.where(last, ahead[f][1], turned[f][1]) for f in range(4)]
            flux = [ce * (east[f] - turned[f][0]) for f in range(4)]
            te = lon_thick * span_e[here, tile(t)] * (turned[2][0] + east[2])
            be = (beta_salt * east[1] - alpha_temp * east[0]) * de
            before = over_e[here, tile(t)]
            pe = before + 0.5 * be
            if keep:
                over_e[here, tile(t)] = before + be
            return ce, flux, te, east, pe

        end, start = turned_at(TILES - 1), turned_at(0)
        kept = zonal(TILES - 1, end, start)
        behind, behind_pe = [turn_w(x) for x in kept[1]], pltpu.roll(kept[4], 2, 1)
        kept_flux, kept_pe = behind, behind_pe
        turned = start
        for t in range(TILES):
            if t < TILES - 1:
                ahead = turned_at(t + 1) if t < TILES - 2 else end
                ce, flux, te, east, pe = zonal(t, turned, ahead)
                turned_flux, turned_pe = [turn_w(x) for x in flux], pltpu.roll(pe, 2, 1)
            else:
                ce, flux, te, east, pe = kept
                turned_flux, turned_pe = kept_flux, kept_pe
            coef_e[here, tile(t)] = ce
            d = turned[4][0]
            dn, ds = north_of(d, deep[above, tile(t)]), south_of(d, deep[below, tile(t)])
            lat_thick = jnp.minimum(d, dn)
            rn = ratio_n[here, tile(t)]
            cn = lat_thick * rn
            cs = jnp.minimum(ds, d) * south_of(rn, ratio_n[below, tile(t)])
            iv = inv_area[here, tile(t)] / jnp.maximum(d, thin_floor)
            coef_n[here, tile(t)] = cn
            inv_vol[here, tile(t)] = iv
            for f in range(4):
                q = turned[f][0]
                qn, qs = north_of(q, data[f][level, above, tile(t)]), south_of(q, data[f][level, below, tile(t)])
                west = jnp.where(first, behind[f], turned_flux[f])
                lap[f, here, tile(t)] = (flux[f] - west + cn * (qn - q) - cs * (q - qs)) * iv
                if f == 3:
                    move_n[here, tile(t)] = lat_thick * span_n[here, tile(t)] * (q + qn)
            q0, q1 = turned[0][0], turned[1][0]
            flux_t[here, tile(t)] = te * (q0 + east[0])
            flux_s[here, tile(t)] = te * (q1 + east[1])
            b = (beta_salt * q1 - alpha_temp * q0) * d
            before = over[here, tile(t)]
            pres[here, tile(t)] = before + 0.5 * b
            if keep:
                over[here, tile(t)] = before + b
            slope[here, tile(t)] = pe - jnp.where(lane < 2, behind_pe, turned_pe)
            behind, behind_pe, turned = turned_flux, turned_pe, ahead
        return 0

    lax.fori_loop(0, CHUNKS, laps, 0, unroll=2)

    def finish(c, _):
        here, above, below = around(c)

        def turned_at(t):
            return [(x, turn_e(x)) for x in (lap[f, here, tile(t)] for f in range(4))]

        def zonal(t, turned, ahead):
            ce = coef_e[here, tile(t)]
            flux = [ce * (jnp.where(last, ahead[f][1], turned[f][1]) - turned[f][0]) for f in range(4)]
            flux[0] = flux[0] + flux_t[here, tile(t)]
            flux[1] = flux[1] + flux_s[here, tile(t)]
            return flux

        end, start = turned_at(TILES - 1), turned_at(0)
        kept = zonal(TILES - 1, end, start)
        kept_turned = [turn_w(x) for x in kept]
        behind, turned = kept_turned, start
        for t in range(TILES):
            if t < TILES - 1:
                ahead = turned_at(t + 1) if t < TILES - 2 else end
                flux = zonal(t, turned, ahead)
                turned_flux = [turn_w(x) for x in flux]
            else:
                flux, turned_flux = kept, kept_turned
            cn = coef_n[here, tile(t)]
            cs = south_of(cn, coef_n[below, tile(t)])
            iv = biharm_coef * inv_vol[here, tile(t)]
            gn = move_n[here, tile(t)]
            gs = south_of(gn, move_n[below, tile(t)])
            wet = land[level, here, tile(t)].astype(F32)
            u, v = uvel[level, here, tile(t)], vvel[level, here, tile(t)]
            turning = time_step * cori[here, tile(t)]
            for f in range(4):
                m = turned[f][0]
                mn, ms = north_of(m, lap[f, above, tile(t)]), south_of(m, lap[f, below, tile(t)])
                west = jnp.where(first, behind[f], turned_flux[f])
                total = flux[f] - west + cn * (mn - m) - cs * (m - ms)
                if f < 2:
                    q = data[f][level, here, tile(t)]
                    qn, qs = north_of(q, data[f][level, above, tile(t)]), south_of(q, data[f][level, below, tile(t)])
                    total = total + gn * (q + qn) - gs * (qs + q)
                    change = wet * (q - total * iv)
                elif f == 2:
                    change = wet * (u + turning * v - slope[here, tile(t)] * half_e[here, tile(t)] - total * iv)
                else:
                    p = pres[here, tile(t)]
                    rise = north_of(p, pres[above, tile(t)]) - south_of(p, pres[below, tile(t)])
                    change = wet * (v - turning * u - rise * half_n[here, tile(t)] - total * iv)
                outs[f][level, here, tile(t)] = change
            behind, turned = turned_flux, ahead
        return 0

    lax.fori_loop(0, CHUNKS, finish, 0, unroll=2)


WORK = [pltpu.VMEM((ROWS, COLS), F32)] * 9 + [pltpu.VMEM((4, ROWS, COLS), F32)]


def inner_kernel(*refs):
    fields, outs, known, over, over_e, work = refs[:9], refs[9:13], refs[13:20], refs[20], refs[21], refs[22:]
    level = pl.program_id(0)

    @pl.when(level == 0)
    def _():
        inner_metric(fields[6], fields[7], known, over, over_e)

    @pl.when(jnp.logical_or(level < AHEAD, near_fold()))
    def _():
        inner_level(level, fields, outs, known, work, over, over_e, True)


def inner(arrays, coriolis):
    out = [pltpu.VMEM((LEVELS, ROWS, COLS), F32)] * 4 + [pltpu.VMEM((ROWS, COLS), F32)] * 9
    done = pl.pallas_call(
        inner_kernel,
        grid=(AHEAD + 1,),
        in_specs=[VMEM] * 9,
        out_specs=[VMEM] * 13,
        out_shape=out,
        scratch_shapes=WORK,
        compiler_params=PARAMS,
        name="inner",
    )(*[onto_chip(x) for x in (*arrays, coriolis)])
    return done[:4], done[4:]


def metric(e, n, lanes, rows):
    ee, ne, en, nn = lanes(e, 1), lanes(n, 1), rows(e, 1), rows(n, 1)
    return (
        (n + ne) / (e + ee),
        (e + en) / (n + nn),
        flux_scale * (n + ne),
        flux_scale * (e + en),
        1.0 / (e * n),
        (0.5 * time_step) / e,
        (0.5 * time_step) / n,
    )


def patch(cells, d, wet, cori, known, overhead, lanes, rows):
    ratio_e, ratio_n, span_e, span_n, inv_area, half_e, half_n = known
    temp, salt, uvel, vvel = cells
    de, dn = lanes(d, 1), rows(d, 1)
    lon_thick, lat_thick = jnp.minimum(d, de), jnp.minimum(d, dn)
    ce, cn = lon_thick * ratio_e, lat_thick * ratio_n
    cs = rows(cn, -1)
    iv = inv_area / jnp.maximum(d, thin_floor)
    b = (beta_salt * salt - alpha_temp * temp) * d
    p = overhead(b) + 0.5 * b
    ge = (lanes(p, 1) - lanes(p, -1)) * half_e
    gn = (rows(p, 1) - rows(p, -1)) * half_n
    outs = []
    te = tn = None
    for f in (2, 3, 0, 1):
        q = cells[f]
        qe, qn, qs = lanes(q, 1), rows(q, 1), rows(q, -1)
        if f == 2:
            te = lon_thick * span_e * (q + qe)
        if f == 3:
            tn = lat_thick * span_n * (q + qn)
            ts = rows(tn, -1)
        fe = ce * (qe - q)
        m = (fe - lanes(fe, -1) + cn * (qn - q) - cs * (q - qs)) * iv
        fe = ce * (lanes(m, 1) - m)
        if f < 2:
            fe = fe + te * (q + qe)
        total = fe - lanes(fe, -1) + cn * (rows(m, 1) - m) - cs * (m - rows(m, -1))
        if f < 2:
            total = total + tn * (q + qn) - ts * (qs + q)
        change = q - biharm_coef * iv * total
        if f == 2:
            change = change + time_step * cori * vvel - ge
        if f == 3:
            change = change - time_step * cori * uvel - gn
        outs.append(wet * change)
    return outs[2], outs[3], outs[0], outs[1]


def rims_level(level, fields, ghosts, outs, known, spin, over):
    temp, salt, uvel, vvel, thick, land, ewid, nwid, cori = fields
    sub = lax.broadcasted_iota(jnp.int32, (8, COLS), 0)
    low, high = slice(0, 8), slice(ROWS - 8, ROWS)

    def lanes(x, by):
        return pltpu.roll(x, COLS - 1 if by > 0 else 1, 2)

    def rows(x, by):
        return pltpu.roll(x, 7 if by > 0 else 1, 1)

    def strips(f, south, north):
        g = [ghosts[k, pl.ds(f, 1), :] for k in range(4)]
        s = jnp.where(sub == 0, g[2], jnp.where(sub == 1, g[3], pltpu.roll(south, 2, 0)))
        n = jnp.where(sub == 6, g[0], jnp.where(sub == 7, g[1], pltpu.roll(north, 6, 0)))
        return jnp.stack([s, n])

    def own(south, north):
        return jnp.stack([pltpu.roll(south, 2, 0), pltpu.roll(north, 6, 0)])

    @pl.when(level == 0)
    def _():
        e = strips(20, ewid[low, :], ewid[high, :])
        n = strips(21, nwid[low, :], nwid[high, :])
        for i, x in enumerate(metric(e, n, lanes, rows)):
            known[i] = x
        spin[...] = own(cori[low, :], cori[high, :])
        over[...] = jnp.zeros((2, 8, COLS), F32)

    cells = [
        strips(LEVELS * kind + level, x[level, low, :], x[level, high, :])
        for kind, x in enumerate((temp, salt, uvel, vvel))
    ]
    wet_low, wet_high = land[level, low, :].astype(F32), land[level, high, :].astype(F32)
    d = strips(4 * LEVELS + level, thick[level, low, :] * wet_low, thick[level, high, :] * wet_high)

    def overhead(b):
        before = over[...]
        over[...] = before + b
        return before

    new = patch(
        cells, d, own(wet_low, wet_high), spin[...], [known[i] for i in range(7)], overhead, lanes, rows
    )
    for x, (old, out) in zip(new, outs):
        out[level, low, :] = jnp.where(sub < 2, pltpu.roll(x[0], 6, 0), old[level, low, :])
        out[level, high, :] = jnp.where(sub >= 6, pltpu.roll(x[1], 2, 0), old[level, high, :])


def near_fold():
    return lax.axis_index("lat") >= lax.axis_size("lat") - 2


def runs_early():
    return jnp.logical_and(lax.axis_index("lon") == 0, lax.axis_index("lat") < lax.axis_size("lat") - 1)


def middle_kernel(*refs):
    fields, known, outs, over, over_e, work = refs[:9], refs[9:16], refs[22:26], refs[26], refs[27], refs[28:]

    @pl.when(runs_early())
    def _():
        level = AHEAD + near_fold().astype(jnp.int32)
        inner_level(level, fields, outs, known, work, over, over_e, True)


def rims_kernel(*refs):
    fields, known, ghosts, outs, over, over_e = refs[:9], refs[9:16], refs[18], refs[23:27], refs[27], refs[28]
    rim_known, spin, rim_over, work = refs[29], refs[30], refs[31], refs[32:]
    level = pl.program_id(0)

    @pl.when(level == 0)
    def _():
        def one(at, _):
            inner_level(at, fields, outs, known, work, over, over_e, True)
            return 0

        done = AHEAD + runs_early().astype(jnp.int32) + near_fold().astype(jnp.int32)
        lax.fori_loop(done, LEVELS, one, 0)

    rims_level(level, fields, ghosts, list(zip(outs, outs)), rim_known, spin, rim_over)


WHOLE = [pltpu.VMEM((LEVELS, ROWS, COLS), F32)] * 4 + [pltpu.VMEM((ROWS, COLS), F32)] * 2


def middle(arrays, coriolis, known, outs):
    done = pl.pallas_call(
        middle_kernel,
        in_specs=[VMEM] * 22,
        out_specs=[VMEM] * 6,
        out_shape=WHOLE,
        scratch_shapes=WORK,
        input_output_aliases={16: 4, 17: 5, 18: 0, 19: 1, 20: 2, 21: 3},
        compiler_params=PARAMS,
        name="middle",
    )(*[onto_chip(x) for x in (*arrays, coriolis, *known, *outs)])
    return done[:4], (*known[:7], *done[4:])


def rims(arrays, coriolis, known, ghosts, outs):
    return pl.pallas_call(
        rims_kernel,
        grid=(LEVELS,),
        in_specs=[VMEM] * 23,
        out_specs=[VMEM] * 6,
        out_shape=WHOLE,
        scratch_shapes=[
            pltpu.VMEM((7, 2, 8, COLS), F32),
            pltpu.VMEM((2, 8, COLS), F32),
            pltpu.VMEM((2, 8, COLS), F32),
        ]
        + WORK,
        input_output_aliases={16: 4, 17: 5, 19: 0, 20: 1, 21: 2, 22: 3},
        compiler_params=PARAMS,
        name="rims",
    )(*[onto_chip(x) for x in (*arrays, coriolis, *known, ghosts, *outs)])[:4]


def sides_kernel(
    win, corner, lon_odd, lon_even, temp_in, salt_in, uvel_in, vvel_in,
    temp_out, salt_out, uvel_out, vvel_out,
    side, edges, mid_sem, low_sem, high_sem,
):
    ins, outs = (temp_in, salt_in, uvel_in, vvel_in), (temp_out, salt_out, uvel_out, vvel_out)
    shape = (TALL, TILE)
    level, slot = level_of(shape), slot_of(shape)
    ghost_lane = jnp.logical_or(slot == 0, slot == 9)
    middle = pl.ds(TILE, COLS - 2 * TILE)

    def middle_copy(i):
        return pltpu.make_async_copy(ins[i].at[:, :, middle], outs[i].at[:, :, middle], mid_sem.at[i])

    def low_copy(i):
        return pltpu.make_async_copy(edges.at[0, i], outs[i].at[:, :, pl.ds(0, TILE)], low_sem.at[i])

    def high_copy(i):
        return pltpu.make_async_copy(edges.at[1, i], outs[i].at[:, :, pl.ds(COLS - TILE, TILE)], high_sem.at[i])

    for i in range(4):
        middle_copy(i).start()

    def lanes(x, by):
        return pltpu.roll(x, TILE - 1 if by > 0 else 1, 1)

    def rows(x, by):
        return pltpu.roll(x, TALL - 1 if by > 0 else 1, 0)

    def tall(body, north, south):
        pad = jnp.zeros((6, TILE), F32)
        return jnp.concatenate([pad, south, body, north, pad], axis=0)

    odd = lax.axis_index("lon") % 2 == 1
    a, b = lon_even[...], lon_odd[...]
    got = jnp.where(slot_of((ROWS + 8, TILE)) >= 9, jnp.where(odd, b, a), jnp.where(odd, a, b))
    side[...] = tall(got[0:ROWS], got[ROWS : ROWS + 2], got[ROWS + 2 : ROWS + 4])

    def extended(kind):
        ends = [jnp.concatenate([corner[k, kind : kind + 1, :] for k in pair], axis=0) for pair in ((0, 1), (2, 3))]
        came = side[...]
        if kind:
            came = pltpu.roll(came, TILE - 2 * kind, 1)
        return jnp.where(ghost_lane, came, tall(win[kind], *ends))

    def everywhere(x):
        return jnp.where(level < 2, x, pltpu.roll(x, 2 * GROUP, 1))

    pair = extended(5)
    e = everywhere(jnp.where(level == 0, pair, pltpu.roll(pair, GROUP, 1)))
    n = everywhere(jnp.where(level == 0, pltpu.roll(pair, TILE - GROUP, 1), pair))

    def overhead(b):
        total = jnp.where(level > 0, pltpu.roll(b, GROUP, 1), 0.0)
        for up in (2, 3):
            total = total + jnp.where(level >= up, pltpu.roll(b, GROUP * up, 1), 0.0)
        return total

    cells = [extended(kind) for kind in range(4)]
    blank = jnp.zeros((2, TILE), F32)
    wet, spin = tall(win[KINDS], blank, blank), tall(win[KINDS + 1], blank, blank)
    new = patch(cells, extended(4), wet, spin, metric(e, n, lanes, rows), overhead, lanes, rows)
    lane = lax.broadcasted_iota(jnp.int32, (ROWS, TILE), 1)
    for i, x in enumerate(new):
        x = x[8 : 8 + ROWS]
        x = jnp.where(lane & (GROUP - 1) < 8, x, pltpu.roll(x, TILE - 16, 1))
        for at in range(LEVELS):
            own = pltpu.roll(x, TILE - GROUP * at, 1) if at else x
            edges[0, i, at] = jnp.where(lane < 2, own, ins[i][at, :, 0:TILE])
            edges[1, i, at] = jnp.where(lane >= TILE - 2, own, ins[i][at, :, COLS - TILE : COLS])
        low_copy(i).start()
        high_copy(i).start()
    for i in range(4):
        middle_copy(i).wait()
        low_copy(i).wait()
        high_copy(i).wait()


def sides(win, corner, lon_even, lon_odd, outs):
    return pl.pallas_call(
        sides_kernel,
        in_specs=[VMEM] * 8,
        out_specs=[pl.BlockSpec(memory_space=pltpu.HBM)] * 4,
        out_shape=[jax.ShapeDtypeStruct((LEVELS, ROWS, COLS), F32)] * 4,
        scratch_shapes=[
            pltpu.VMEM((TALL, TILE), F32),
            pltpu.VMEM((2, 4, LEVELS, ROWS, TILE), F32),
            pltpu.SemaphoreType.DMA((4,)),
            pltpu.SemaphoreType.DMA((4,)),
            pltpu.SemaphoreType.DMA((4,)),
        ],
        compiler_params=PARAMS,
        name="sides",
    )(*[onto_chip(x) for x in (win, corner, lon_odd, lon_even, *outs)])


def shards(temp, salt, uvel, vvel, thick, land, east_width, north_width, coriolis):
    lats, lons = lax.axis_size("lat"), lax.axis_size("lon")
    arrays = (temp, salt, uvel, vvel, thick, land, east_width, north_width)
    near, far = pack_rows(arrays)
    near = lax.ppermute(near, AXES, lat_pairs(lats, lons, 0))
    far = lax.ppermute(far, AXES, lat_pairs(lats, lons, 1))
    win, packed = windows(arrays, coriolis)
    outs, known = inner(arrays, coriolis)
    near, far, packed, *outs = lax.optimization_barrier((near, far, packed, *outs))
    packed, ghosts, corner = pack_columns(packed, near, far)
    outs, known = middle(arrays, coriolis, known, outs)
    packed, *outs = lax.optimization_barrier((packed, *outs))
    lon_odd = lax.ppermute(packed, AXES, lon_pairs(lats, lons, 1))
    lon_even = lax.ppermute(packed, AXES, lon_pairs(lats, lons, 0))
    outs = rims(arrays, coriolis, known, ghosts, outs)
    return tuple(sides(win, corner, lon_even, lon_odd, outs))


def solution(mesh):
    deep, flat = P(None, "lat", "lon"), P("lat", "lon")
    return jax.shard_map(
        shards,
        mesh=mesh,
        in_specs=(deep,) * 6 + (flat,) * 3,
        out_specs=(deep,) * 4,
        check_vma=False,
    )
```

```python
import jax
import jax.numpy as jnp
from jax import lax
from jax.experimental import pallas as pl
from jax.experimental.pallas import tpu as pltpu
from jax.sharding import PartitionSpec as P

time_step = 0.2
biharm_coef = 0.02
alpha_temp = 0.2
beta_salt = 0.8
thin_floor = 0.25
flux_scale = time_step / 8.0 / biharm_coef

LEVELS = 4
ROWS = 64
COLS = 768
TILE = 128
TILES = COLS // TILE
CHUNKS = ROWS // 8
TALL = ROWS + 16
FIELDS = 22
AHEAD = 2
KINDS = 6
GROUP = TILE // LEVELS
F32 = jnp.float32
PARAMS = pltpu.CompilerParams(vmem_limit_bytes=12 * 1024 * 1024)
AXES = ("lon", "lat")
VMEM = pl.BlockSpec(memory_space=pltpu.VMEM)


def place(lat, lon, lats, lons):
    return (lon % lons) * lats + lat


def both(pairs):
    return [p for a, b in pairs for p in ((a, b), (b, a))]


def lat_pairs(lats, lons, bit):
    pairs = [
        (place(i, j, lats, lons), place(i + 1, j, lats, lons))
        for i in range(bit, lats - 1, 2)
        for j in range(lons)
    ]
    if bit:
        pairs += [
            (place(lats - 1, j, lats, lons), place(lats - 1, lons - 1 - j, lats, lons))
            for j in range(lons // 2)
        ]
    return both(pairs)


def lon_pairs(lats, lons, bit):
    return both(
        [
            (place(i, j, lats, lons), place(i, j + 1, lats, lons))
            for i in range(lats)
            for j in range(bit, lons, 2)
        ]
    )


def onto_chip(x):
    return pltpu.with_memory_space_constraint(x, pltpu.VMEM)


def off_chip(x):
    return pltpu.with_memory_space_constraint(x, pltpu.HBM)


def rows_kernel(*refs):
    low, high, (near_ref, far_ref), stage = refs[:8], refs[8:16], refs[16:18], refs[18]
    lat = lax.axis_index("lat")
    odd = lat % 2 == 1
    top = lat == lax.axis_size("lat") - 1

    def gather(group, take, dst):
        for kind in range(5):
            for level in range(LEVELS):
                if kind < 4:
                    cells = group[kind][level]
                else:
                    cells = group[4][level] * group[5][level].astype(F32)
                for k, row in enumerate(take):
                    dst[k, kind * LEVELS + level : kind * LEVELS + level + 1, :] = cells[row : row + 1]
        for k, row in enumerate(take):
            dst[k, 20:21, :] = group[6][row : row + 1, :]
            dst[k, 21:22, :] = group[7][row : row + 1, :]

    @pl.when(odd)
    def _():
        gather(low, (0, 1), near_ref)

        @pl.when(jnp.logical_not(top))
        def _():
            gather(high, (6, 7), far_ref)

        @pl.when(top)
        def _():
            gather(high, (6, 5), stage)
            kind_row = lax.broadcasted_iota(jnp.int32, (24, TILE), 0)
            turned = jnp.logical_and(kind_row >= 2 * LEVELS, kind_row < 4 * LEVELS)
            sign = jnp.where(turned, -1.0, 1.0).astype(F32)
            flip = TILE - 1 - lax.broadcasted_iota(jnp.int32, (24, TILE), 1)
            for k in range(2):
                for t in range(COLS // TILE):
                    src = stage[k, :, COLS - TILE * (t + 1) : COLS - TILE * t]
                    rev = jnp.take_along_axis(src, flip, axis=1, mode="promise_in_bounds")
                    far_ref[k, :, TILE * t : TILE * (t + 1)] = rev * sign

    @pl.when(jnp.logical_not(odd))
    def _():
        gather(high, (6, 7), near_ref)
        gather(low, (0, 1), far_ref)


def pack_rows(arrays):
    def spec(a, at):
        if a.ndim == 3:
            return pl.BlockSpec((LEVELS, 8, COLS), lambda i: (0, at, 0))
        return pl.BlockSpec((8, COLS), lambda i: (at, 0))

    whole = pl.BlockSpec((2, 24, COLS), lambda i: (0, 0, 0))
    shape = pltpu.VMEM((2, 24, COLS), F32)
    return pl.pallas_call(
        rows_kernel,
        grid=(1,),
        in_specs=[spec(a, 0) for a in arrays] + [spec(a, ROWS // 8 - 1) for a in arrays],
        out_specs=[pl.BlockSpec(memory_space=pltpu.VMEM)] * 2,
        out_shape=[shape, shape],
        scratch_shapes=[pltpu.VMEM((2, 24, COLS), F32)],
        compiler_params=PARAMS,
        name="pack_rows",
    )(*[off_chip(x) for x in (*arrays, *arrays)])


def slot_of(shape):
    return ((lax.broadcasted_iota(jnp.int32, shape, len(shape) - 1) + 2) & (GROUP - 1)) >> 1


def level_of(shape):
    return ((lax.broadcasted_iota(jnp.int32, shape, len(shape) - 1) + 8) >> 5) & (LEVELS - 1)


def join_ends(low, high):
    lane = lax.broadcasted_iota(jnp.int32, low.shape, len(low.shape) - 1)
    return jnp.where(lane < 8, low, pltpu.roll(high, 16, len(low.shape) - 1))


def windows_kernel(temp, salt, uvel, vvel, thick, land, ewid, nwid, cori, win, packed):
    shape = (ROWS, TILE)
    lane = lax.broadcasted_iota(jnp.int32, shape, 1)
    slot = slot_of(shape)
    ends = (slice(0, TILE), slice(COLS - TILE, COLS))
    total = jnp.zeros(shape, F32)

    def spread(parts):
        whole = parts[0]
        for level in range(1, len(parts)):
            whole = jnp.where(lane >= GROUP * level, pltpu.roll(parts[level], GROUP * level, 1), whole)
        return whole

    def at(kind, level, cut):
        if kind < 4:
            return (temp, salt, uvel, vvel)[kind][level, :, cut]
        if kind == 4:
            return thick[level, :, cut] * land[level, :, cut].astype(F32)
        if kind == 5:
            return (ewid, nwid)[level][:, cut]
        if kind == 6:
            return land[level, :, cut].astype(F32)
        return cori[:, cut]

    for kind in range(KINDS + 2):
        count = (LEVELS, 2, LEVELS, 1)[max(kind - 4, 0)]
        parts = [join_ends(*[at(kind, level, cut) for cut in ends]) for level in range(count)]
        cells = spread(parts * LEVELS if count == 1 else parts)
        win[kind] = cells
        if kind < KINDS:
            total = jnp.where(slot == 9 + kind, pltpu.roll(cells, 16 + 2 * kind, 1), total)
            total = jnp.where(slot == kind, pltpu.roll(cells, TILE - 16 + 2 * kind, 1), total)
    packed[...] = total


def windows(arrays, coriolis):
    return pl.pallas_call(
        windows_kernel,
        in_specs=[VMEM] * 9,
        out_specs=[VMEM] * 2,
        out_shape=[pltpu.VMEM((KINDS + 2, ROWS, TILE), F32), pltpu.VMEM((ROWS, TILE), F32)],
        compiler_params=PARAMS,
        name="windows",
    )(*[onto_chip(x) for x in (*arrays, coriolis)])


def columns_kernel(packed, near, far, out, ghosts, corner):
    lat = lax.axis_index("lat")
    odd = lat % 2 == 1
    out[0:ROWS, :] = packed[...]
    row = lax.broadcasted_iota(jnp.int32, (24, COLS), 0)
    fill = jnp.logical_and(lat == 0, row >= 20)
    lane = lax.broadcasted_iota(jnp.int32, (24, TILE), 1)
    small_row = lax.broadcasted_iota(jnp.int32, (24, TILE), 0)
    mine = jnp.logical_and(lane >> 5 == small_row & (LEVELS - 1), lane & (GROUP - 1) < 16)
    slot = slot_of((8, TILE))
    kind = lax.broadcasted_iota(jnp.int32, (8, TILE), 0)
    for k in range(2):
        a, b = near[k], far[k]
        for side in range(2):
            if side == 0:
                cells = jnp.where(odd, b, a)
            else:
                cells = jnp.where(fill, 1.0, jnp.where(odd, a, b))
            at = 2 * side + k
            ghosts[at] = cells
            ends = join_ends(cells[:, 0:TILE], cells[:, COLS - TILE : COLS])
            moved = ends
            for level in range(1, LEVELS):
                moved = jnp.where(small_row & (LEVELS - 1) == level, pltpu.roll(ends, GROUP * level, 1), moved)
            ends = jnp.where(mine, moved, 0.0)
            rows = [jnp.sum(ends[LEVELS * i : LEVELS * (i + 1)], axis=0, keepdims=True) for i in range(KINDS)]
            shown = jnp.concatenate(rows + [jnp.zeros((8 - KINDS, TILE), F32)], axis=0)
            corner[at] = shown
            east = pltpu.roll(shown, 16, 1, stride=2, stride_axis=0)
            west = pltpu.roll(shown, TILE - 16, 1, stride=2, stride_axis=0)
            sent = jnp.where(slot == kind + 9, east, jnp.where(slot == kind, west, 0.0))
            out[ROWS + at : ROWS + at + 1, :] = jnp.sum(sent[0:KINDS], axis=0, keepdims=True)
    out[ROWS + 4 : ROWS + 8, :] = jnp.zeros((4, TILE), F32)


def pack_columns(packed, near, far):
    return pl.pallas_call(
        columns_kernel,
        in_specs=[VMEM] * 3,
        out_specs=[VMEM] * 3,
        out_shape=[
            pltpu.VMEM((ROWS + 8, TILE), F32),
            pltpu.VMEM((4, 24, COLS), F32),
            pltpu.VMEM((4, 8, TILE), F32),
        ],
        compiler_params=PARAMS,
        name="pack_columns",
    )(*[onto_chip(x) for x in (packed, near, far)])


def north_of(here, above):
    sub = lax.broadcasted_iota(jnp.int32, here.shape, 0)
    return pltpu.roll(jnp.where(sub == 0, above, here), 7, 0)


def south_of(here, below):
    sub = lax.broadcasted_iota(jnp.int32, here.shape, 0)
    return pltpu.roll(jnp.where(sub == 7, below, here), 1, 0)


def tile(t):
    return slice(TILE * t, TILE * t + TILE)


def turn_e(x):
    return pltpu.roll(x, TILE - 1, 1)


def turn_w(x):
    return pltpu.roll(x, 1, 1)


def around(c):
    r = pl.multiple_of(8 * c, 8)
    up = pl.multiple_of(8 * jnp.minimum(c + 1, CHUNKS - 1), 8)
    down = pl.multiple_of(8 * jnp.maximum(c - 1, 0), 8)
    return pl.ds(r, 8), pl.ds(up, 8), pl.ds(down, 8)


def inner_metric(ewid, nwid, known, over, over_e):
    ratio_e, ratio_n, span_e, span_n, inv_area, half_e, half_n = known
    last = lax.broadcasted_iota(jnp.int32, (8, TILE), 1) == TILE - 1

    def chunk(c, _):
        here, above, _ = around(c)
        east = [(ewid[here, tile(0)], nwid[here, tile(0)])]
        east = [tuple((x, turn_e(x)) for x in east[0])]
        for t in range(TILES):
            (e, re), (n, rn) = east[t]
            u = (t + 1) % TILES
            if u:
                east.append(tuple((x, turn_e(x)) for x in (ewid[here, tile(u)], nwid[here, tile(u)])))
            else:
                east.append(east[0])
            ee = jnp.where(last, east[t + 1][0][1], re)
            ne = jnp.where(last, east[t + 1][1][1], rn)
            en = north_of(e, ewid[above, tile(t)])
            nn = north_of(n, nwid[above, tile(t)])
            ratio_e[here, tile(t)] = (n + ne) / (e + ee)
            ratio_n[here, tile(t)] = (e + en) / (n + nn)
            span_e[here, tile(t)] = flux_scale * (n + ne)
            span_n[here, tile(t)] = flux_scale * (e + en)
            inv_area[here, tile(t)] = 1.0 / (e * n)
            half_e[here, tile(t)] = (0.5 * time_step) / e
            half_n[here, tile(t)] = (0.5 * time_step) / n
            over[here, tile(t)] = jnp.zeros((8, TILE), F32)
            over_e[here, tile(t)] = jnp.zeros((8, TILE), F32)
        return 0

    lax.fori_loop(0, CHUNKS, chunk, 0, unroll=2)


def inner_level(level, fields, outs, known, work, over, over_e, keep):
    temp, salt, uvel, vvel, thick, land, ewid, nwid, cori = fields
    ratio_e, ratio_n, span_e, span_n, inv_area, half_e, half_n = known
    deep, coef_e, coef_n, inv_vol, move_n, flux_t, flux_s, pres, slope, lap = work
    lane = lax.broadcasted_iota(jnp.int32, (8, TILE), 1)
    first, last = lane == 0, lane == TILE - 1
    data = (temp, salt, uvel, vvel)

    for r in range(0, ROWS, 8):
        deep[r : r + 8, :] = thick[level, r : r + 8, :] * land[level, r : r + 8, :].astype(F32)

    def laps(c, _):
        here, above, below = around(c)

        def turned_at(t):
            cells = [x[level, here, tile(t)] for x in data] + [deep[here, tile(t)]]
            return [(x, turn_e(x)) for x in cells]

        def zonal(t, turned, ahead):
            d, rd = turned[4]
            de = jnp.where(last, ahead[4][1], rd)
            lon_thick = jnp.minimum(d, de)
            ce = lon_thick * ratio_e[here, tile(t)]
            east = [jnp.where(last, ahead[f][1], turned[f][1]) for f in range(4)]
            flux = [ce * (east[f] - turned[f][0]) for f in range(4)]
            te = lon_thick * span_e[here, tile(t)] * (turned[2][0] + east[2])
            be = (beta_salt * east[1] - alpha_temp * east[0]) * de
            before = over_e[here, tile(t)]
            pe = before + 0.5 * be
            if keep:
                over_e[here, tile(t)] = before + be
            return ce, flux, te, east, pe

        end, start = turned_at(TILES - 1), turned_at(0)
        kept = zonal(TILES - 1, end, start)
        behind, behind_pe = [turn_w(x) for x in kept[1]], pltpu.roll(kept[4], 2, 1)
        kept_flux, kept_pe = behind, behind_pe
        turned = start
        for t in range(TILES):
            if t < TILES - 1:
                ahead = turned_at(t + 1) if t < TILES - 2 else end
                ce, flux, te, east, pe = zonal(t, turned, ahead)
                turned_flux, turned_pe = [turn_w(x) for x in flux], pltpu.roll(pe, 2, 1)
            else:
                ce, flux, te, east, pe = kept
                turned_flux, turned_pe = kept_flux, kept_pe
            coef_e[here, tile(t)] = ce
            d = turned[4][0]
            dn, ds = north_of(d, deep[above, tile(t)]), south_of(d, deep[below, tile(t)])
            lat_thick = jnp.minimum(d, dn)
            rn = ratio_n[here, tile(t)]
            cn = lat_thick * rn
            cs = jnp.minimum(ds, d) * south_of(rn, ratio_n[below, tile(t)])
            iv = inv_area[here, tile(t)] / jnp.maximum(d, thin_floor)
            coef_n[here, tile(t)] = cn
            inv_vol[here, tile(t)] = iv
            for f in range(4):
                q = turned[f][0]
                qn, qs = north_of(q, data[f][level, above, tile(t)]), south_of(q, data[f][level, below, tile(t)])
                west = jnp.where(first, behind[f], turned_flux[f])
                lap[f, here, tile(t)] = (flux[f] - west + cn * (qn - q) - cs * (q - qs)) * iv
                if f == 3:
                    move_n[here, tile(t)] = lat_thick * span_n[here, tile(t)] * (q + qn)
            q0, q1 = turned[0][0], turned[1][0]
            flux_t[here, tile(t)] = te * (q0 + east[0])
            flux_s[here, tile(t)] = te * (q1 + east[1])
            b = (beta_salt * q1 - alpha_temp * q0) * d
            before = over[here, tile(t)]
            pres[here, tile(t)] = before + 0.5 * b
            if keep:
                over[here, tile(t)] = before + b
            slope[here, tile(t)] = pe - jnp.where(lane < 2, behind_pe, turned_pe)
            behind, behind_pe, turned = turned_flux, turned_pe, ahead
        return 0

    lax.fori_loop(0, CHUNKS, laps, 0, unroll=2)

    def finish(c, _):
        here, above, below = around(c)

        def turned_at(t):
            return [(x, turn_e(x)) for x in (lap[f, here, tile(t)] for f in range(4))]

        def zonal(t, turned, ahead):
            ce = coef_e[here, tile(t)]
            flux = [ce * (jnp.where(last, ahead[f][1], turned[f][1]) - turned[f][0]) for f in range(4)]
            flux[0] = flux[0] + flux_t[here, tile(t)]
            flux[1] = flux[1] + flux_s[here, tile(t)]
            return flux

        end, start = turned_at(TILES - 1), turned_at(0)
        kept = zonal(TILES - 1, end, start)
        kept_turned = [turn_w(x) for x in kept]
        behind, turned = kept_turned, start
        for t in range(TILES):
            if t < TILES - 1:
                ahead = turned_at(t + 1) if t < TILES - 2 else end
                flux = zonal(t, turned, ahead)
                turned_flux = [turn_w(x) for x in flux]
            else:
                flux, turned_flux = kept, kept_turned
            cn = coef_n[here, tile(t)]
            cs = south_of(cn, coef_n[below, tile(t)])
            iv = biharm_coef * inv_vol[here, tile(t)]
            gn = move_n[here, tile(t)]
            gs = south_of(gn, move_n[below, tile(t)])
            wet = land[level, here, tile(t)].astype(F32)
            u, v = uvel[level, here, tile(t)], vvel[level, here, tile(t)]
            turning = time_step * cori[here, tile(t)]
            for f in range(4):
                m = turned[f][0]
                mn, ms = north_of(m, lap[f, above, tile(t)]), south_of(m, lap[f, below, tile(t)])
                west = jnp.where(first, behind[f], turned_flux[f])
                total = flux[f] - west + cn * (mn - m) - cs * (m - ms)
                if f < 2:
                    q = data[f][level, here, tile(t)]
                    qn, qs = north_of(q, data[f][level, above, tile(t)]), south_of(q, data[f][level, below, tile(t)])
                    total = total + gn * (q + qn) - gs * (qs + q)
                    change = wet * (q - total * iv)
                elif f == 2:
                    change = wet * (u + turning * v - slope[here, tile(t)] * half_e[here, tile(t)] - total * iv)
                else:
                    p = pres[here, tile(t)]
                    rise = north_of(p, pres[above, tile(t)]) - south_of(p, pres[below, tile(t)])
                    change = wet * (v - turning * u - rise * half_n[here, tile(t)] - total * iv)
                outs[f][level, here, tile(t)] = change
            behind, turned = turned_flux, ahead
        return 0

    lax.fori_loop(0, CHUNKS, finish, 0, unroll=2)


WORK = [pltpu.VMEM((ROWS, COLS), F32)] * 9 + [pltpu.VMEM((4, ROWS, COLS), F32)]


def inner_kernel(*refs):
    fields, outs, known, over, over_e, work = refs[:9], refs[9:13], refs[13:20], refs[20], refs[21], refs[22:]
    level = pl.program_id(0)

    @pl.when(level == 0)
    def _():
        inner_metric(fields[6], fields[7], known, over, over_e)

    @pl.when(jnp.logical_or(level < AHEAD, near_fold()))
    def _():
        inner_level(level, fields, outs, known, work, over, over_e, True)


def inner(arrays, coriolis):
    out = [pltpu.VMEM((LEVELS, ROWS, COLS), F32)] * 4 + [pltpu.VMEM((ROWS, COLS), F32)] * 9
    done = pl.pallas_call(
        inner_kernel,
        grid=(AHEAD + 1,),
        in_specs=[VMEM] * 9,
        out_specs=[VMEM] * 13,
        out_shape=out,
        scratch_shapes=WORK,
        compiler_params=PARAMS,
        name="inner",
    )(*[onto_chip(x) for x in (*arrays, coriolis)])
    return done[:4], done[4:]


def metric(e, n, lanes, rows):
    ee, ne, en, nn = lanes(e, 1), lanes(n, 1), rows(e, 1), rows(n, 1)
    return (
        (n + ne) / (e + ee),
        (e + en) / (n + nn),
        flux_scale * (n + ne),
        flux_scale * (e + en),
        1.0 / (e * n),
        (0.5 * time_step) / e,
        (0.5 * time_step) / n,
    )


def patch(cells, d, wet, cori, known, overhead, lanes, rows):
    ratio_e, ratio_n, span_e, span_n, inv_area, half_e, half_n = known
    temp, salt, uvel, vvel = cells
    de, dn = lanes(d, 1), rows(d, 1)
    lon_thick, lat_thick = jnp.minimum(d, de), jnp.minimum(d, dn)
    ce, cn = lon_thick * ratio_e, lat_thick * ratio_n
    cs = rows(cn, -1)
    iv = inv_area / jnp.maximum(d, thin_floor)
    b = (beta_salt * salt - alpha_temp * temp) * d
    p = overhead(b) + 0.5 * b
    ge = (lanes(p, 1) - lanes(p, -1)) * half_e
    gn = (rows(p, 1) - rows(p, -1)) * half_n
    outs = []
    te = tn = None
    for f in (2, 3, 0, 1):
        q = cells[f]
        qe, qn, qs = lanes(q, 1), rows(q, 1), rows(q, -1)
        if f == 2:
            te = lon_thick * span_e * (q + qe)
        if f == 3:
            tn = lat_thick * span_n * (q + qn)
            ts = rows(tn, -1)
        fe = ce * (qe - q)
        m = (fe - lanes(fe, -1) + cn * (qn - q) - cs * (q - qs)) * iv
        fe = ce * (lanes(m, 1) - m)
        if f < 2:
            fe = fe + te * (q + qe)
        total = fe - lanes(fe, -1) + cn * (rows(m, 1) - m) - cs * (m - rows(m, -1))
        if f < 2:
            total = total + tn * (q + qn) - ts * (qs + q)
        change = q - biharm_coef * iv * total
        if f == 2:
            change = change + time_step * cori * vvel - ge
        if f == 3:
            change = change - time_step * cori * uvel - gn
        outs.append(wet * change)
    return outs[2], outs[3], outs[0], outs[1]


def rims_level(level, fields, ghosts, outs, known, spin, over):
    temp, salt, uvel, vvel, thick, land, ewid, nwid, cori = fields
    sub = lax.broadcasted_iota(jnp.int32, (8, COLS), 0)
    low, high = slice(0, 8), slice(ROWS - 8, ROWS)

    def lanes(x, by):
        return pltpu.roll(x, COLS - 1 if by > 0 else 1, 2)

    def rows(x, by):
        return pltpu.roll(x, 7 if by > 0 else 1, 1)

    def strips(f, south, north):
        g = [ghosts[k, pl.ds(f, 1), :] for k in range(4)]
        s = jnp.where(sub == 0, g[2], jnp.where(sub == 1, g[3], pltpu.roll(south, 2, 0)))
        n = jnp.where(sub == 6, g[0], jnp.where(sub == 7, g[1], pltpu.roll(north, 6, 0)))
        return jnp.stack([s, n])

    def own(south, north):
        return jnp.stack([pltpu.roll(south, 2, 0), pltpu.roll(north, 6, 0)])

    @pl.when(level == 0)
    def _():
        e = strips(20, ewid[low, :], ewid[high, :])
        n = strips(21, nwid[low, :], nwid[high, :])
        for i, x in enumerate(metric(e, n, lanes, rows)):
            known[i] = x
        spin[...] = own(cori[low, :], cori[high, :])
        over[...] = jnp.zeros((2, 8, COLS), F32)

    cells = [
        strips(LEVELS * kind + level, x[level, low, :], x[level, high, :])
        for kind, x in enumerate((temp, salt, uvel, vvel))
    ]
    wet_low, wet_high = land[level, low, :].astype(F32), land[level, high, :].astype(F32)
    d = strips(4 * LEVELS + level, thick[level, low, :] * wet_low, thick[level, high, :] * wet_high)

    def overhead(b):
        before = over[...]
        over[...] = before + b
        return before

    new = patch(
        cells, d, own(wet_low, wet_high), spin[...], [known[i] for i in range(7)], overhead, lanes, rows
    )
    for x, (old, out) in zip(new, outs):
        out[level, low, :] = jnp.where(sub < 2, pltpu.roll(x[0], 6, 0), old[level, low, :])
        out[level, high, :] = jnp.where(sub >= 6, pltpu.roll(x[1], 2, 0), old[level, high, :])


def near_fold():
    return lax.axis_index("lat") >= lax.axis_size("lat") - 2


def runs_early():
    return jnp.logical_and(lax.axis_index("lon") < 2, lax.axis_index("lat") < lax.axis_size("lat") - 1)


def middle_kernel(*refs):
    fields, known, outs, over, over_e, work = refs[:9], refs[9:16], refs[22:26], refs[26], refs[27], refs[28:]

    @pl.when(runs_early())
    def _():
        level = AHEAD + near_fold().astype(jnp.int32)
        inner_level(level, fields, outs, known, work, over, over_e, True)


def rims_kernel(*refs):
    fields, known, ghosts, outs, over, over_e = refs[:9], refs[9:16], refs[18], refs[23:27], refs[27], refs[28]
    rim_known, spin, rim_over, work = refs[29], refs[30], refs[31], refs[32:]
    level = pl.program_id(0)

    @pl.when(level == 0)
    def _():
        def one(at, _):
            inner_level(at, fields, outs, known, work, over, over_e, True)
            return 0

        done = AHEAD + runs_early().astype(jnp.int32) + near_fold().astype(jnp.int32)
        lax.fori_loop(done, LEVELS, one, 0)

    rims_level(level, fields, ghosts, list(zip(outs, outs)), rim_known, spin, rim_over)


WHOLE = [pltpu.VMEM((LEVELS, ROWS, COLS), F32)] * 4 + [pltpu.VMEM((ROWS, COLS), F32)] * 2


def middle(arrays, coriolis, known, outs):
    done = pl.pallas_call(
        middle_kernel,
        in_specs=[VMEM] * 22,
        out_specs=[VMEM] * 6,
        out_shape=WHOLE,
        scratch_shapes=WORK,
        input_output_aliases={16: 4, 17: 5, 18: 0, 19: 1, 20: 2, 21: 3},
        compiler_params=PARAMS,
        name="middle",
    )(*[onto_chip(x) for x in (*arrays, coriolis, *known, *outs)])
    return done[:4], (*known[:7], *done[4:])


def rims(arrays, coriolis, known, ghosts, outs):
    return pl.pallas_call(
        rims_kernel,
        grid=(LEVELS,),
        in_specs=[VMEM] * 23,
        out_specs=[VMEM] * 6,
        out_shape=WHOLE,
        scratch_shapes=[
            pltpu.VMEM((7, 2, 8, COLS), F32),
            pltpu.VMEM((2, 8, COLS), F32),
            pltpu.VMEM((2, 8, COLS), F32),
        ]
        + WORK,
        input_output_aliases={16: 4, 17: 5, 19: 0, 20: 1, 21: 2, 22: 3},
        compiler_params=PARAMS,
        name="rims",
    )(*[onto_chip(x) for x in (*arrays, coriolis, *known, ghosts, *outs)])[:4]


def sides_kernel(
    win, corner, lon_even, lon_odd, temp_in, salt_in, uvel_in, vvel_in,
    temp_out, salt_out, uvel_out, vvel_out,
    side, edges, mid_sem, low_sem, high_sem,
):
    ins, outs = (temp_in, salt_in, uvel_in, vvel_in), (temp_out, salt_out, uvel_out, vvel_out)
    shape = (TALL, TILE)
    level, slot = level_of(shape), slot_of(shape)
    ghost_lane = jnp.logical_or(slot == 0, slot == 9)
    middle = pl.ds(TILE, COLS - 2 * TILE)

    def middle_copy(i):
        return pltpu.make_async_copy(ins[i].at[:, :, middle], outs[i].at[:, :, middle], mid_sem.at[i])

    def low_copy(i):
        return pltpu.make_async_copy(edges.at[0, i], outs[i].at[:, :, pl.ds(0, TILE)], low_sem.at[i])

    def high_copy(i):
        return pltpu.make_async_copy(edges.at[1, i], outs[i].at[:, :, pl.ds(COLS - TILE, TILE)], high_sem.at[i])

    for i in range(4):
        middle_copy(i).start()

    def lanes(x, by):
        return pltpu.roll(x, TILE - 1 if by > 0 else 1, 1)

    def rows(x, by):
        return pltpu.roll(x, TALL - 1 if by > 0 else 1, 0)

    def tall(body, north, south):
        pad = jnp.zeros((6, TILE), F32)
        return jnp.concatenate([pad, south, body, north, pad], axis=0)

    odd = lax.axis_index("lon") % 2 == 1
    a, b = lon_even[...], lon_odd[...]
    got = jnp.where(slot_of((ROWS + 8, TILE)) >= 9, jnp.where(odd, b, a), jnp.where(odd, a, b))
    side[...] = tall(got[0:ROWS], got[ROWS : ROWS + 2], got[ROWS + 2 : ROWS + 4])

    def extended(kind):
        ends = [jnp.concatenate([corner[k, kind : kind + 1, :] for k in pair], axis=0) for pair in ((0, 1), (2, 3))]
        came = side[...]
        if kind:
            came = pltpu.roll(came, TILE - 2 * kind, 1)
        return jnp.where(ghost_lane, came, tall(win[kind], *ends))

    def everywhere(x):
        return jnp.where(level < 2, x, pltpu.roll(x, 2 * GROUP, 1))

    pair = extended(5)
    e = everywhere(jnp.where(level == 0, pair, pltpu.roll(pair, GROUP, 1)))
    n = everywhere(jnp.where(level == 0, pltpu.roll(pair, TILE - GROUP, 1), pair))

    def overhead(b):
        total = jnp.where(level > 0, pltpu.roll(b, GROUP, 1), 0.0)
        for up in (2, 3):
            total = total + jnp.where(level >= up, pltpu.roll(b, GROUP * up, 1), 0.0)
        return total

    cells = [extended(kind) for kind in range(4)]
    blank = jnp.zeros((2, TILE), F32)
    wet, spin = tall(win[KINDS], blank, blank), tall(win[KINDS + 1], blank, blank)
    new = patch(cells, extended(4), wet, spin, metric(e, n, lanes, rows), overhead, lanes, rows)
    lane = lax.broadcasted_iota(jnp.int32, (ROWS, TILE), 1)
    for i, x in enumerate(new):
        x = x[8 : 8 + ROWS]
        x = jnp.where(lane & (GROUP - 1) < 8, x, pltpu.roll(x, TILE - 16, 1))
        for at in range(LEVELS):
            own = pltpu.roll(x, TILE - GROUP * at, 1) if at else x
            edges[0, i, at] = jnp.where(lane < 2, own, ins[i][at, :, 0:TILE])
            edges[1, i, at] = jnp.where(lane >= TILE - 2, own, ins[i][at, :, COLS - TILE : COLS])
        low_copy(i).start()
        high_copy(i).start()
    for i in range(4):
        middle_copy(i).wait()
        low_copy(i).wait()
        high_copy(i).wait()


def sides(win, corner, lon_even, lon_odd, outs):
    return pl.pallas_call(
        sides_kernel,
        in_specs=[VMEM] * 8,
        out_specs=[pl.BlockSpec(memory_space=pltpu.HBM)] * 4,
        out_shape=[jax.ShapeDtypeStruct((LEVELS, ROWS, COLS), F32)] * 4,
        scratch_shapes=[
            pltpu.VMEM((TALL, TILE), F32),
            pltpu.VMEM((2, 4, LEVELS, ROWS, TILE), F32),
            pltpu.SemaphoreType.DMA((4,)),
            pltpu.SemaphoreType.DMA((4,)),
            pltpu.SemaphoreType.DMA((4,)),
        ],
        compiler_params=PARAMS,
        name="sides",
    )(*[onto_chip(x) for x in (win, corner, lon_even, lon_odd, *outs)])


def shards(temp, salt, uvel, vvel, thick, land, east_width, north_width, coriolis):
    lats, lons = lax.axis_size("lat"), lax.axis_size("lon")
    arrays = (temp, salt, uvel, vvel, thick, land, east_width, north_width)
    near, far = pack_rows(arrays)
    near = lax.ppermute(near, AXES, lat_pairs(lats, lons, 0))
    far = lax.ppermute(far, AXES, lat_pairs(lats, lons, 1))
    win, packed = windows(arrays, coriolis)
    outs, known = inner(arrays, coriolis)
    near, far, packed, *outs = lax.optimization_barrier((near, far, packed, *outs))
    packed, ghosts, corner = pack_columns(packed, near, far)
    outs, known = middle(arrays, coriolis, known, outs)
    packed, *outs = lax.optimization_barrier((packed, *outs))
    lon_odd = lax.ppermute(packed, AXES, lon_pairs(lats, lons, 1))
    lon_even = lax.ppermute(packed, AXES, lon_pairs(lats, lons, 0))
    outs = rims(arrays, coriolis, known, ghosts, outs)
    return tuple(sides(win, corner, lon_even, lon_odd, outs))


def solution(mesh):
    deep, flat = P(None, "lat", "lon"), P("lat", "lon")
    return jax.shard_map(
        shards,
        mesh=mesh,
        in_specs=(deep,) * 6 + (flat,) * 3,
        out_specs=(deep,) * 4,
        check_vma=False,
    )
```

```python
import jax
import jax.numpy as jnp
from jax import lax
from jax.experimental import pallas as pl
from jax.experimental.pallas import tpu as pltpu
from jax.sharding import PartitionSpec as P

time_step = 0.2
biharm_coef = 0.02
alpha_temp = 0.2
beta_salt = 0.8
thin_floor = 0.25
flux_scale = time_step / 8.0 / biharm_coef

LEVELS = 4
ROWS = 64
COLS = 768
TILE = 128
TILES = COLS // TILE
CHUNKS = ROWS // 8
TALL = ROWS + 16
FIELDS = 22
AHEAD = 2
KINDS = 6
GROUP = TILE // LEVELS
F32 = jnp.float32
PARAMS = pltpu.CompilerParams(vmem_limit_bytes=12 * 1024 * 1024)
AXES = ("lon", "lat")
VMEM = pl.BlockSpec(memory_space=pltpu.VMEM)


def place(lat, lon, lats, lons):
    return (lon % lons) * lats + lat


def both(pairs):
    return [p for a, b in pairs for p in ((a, b), (b, a))]


def lat_pairs(lats, lons, bit):
    pairs = [
        (place(i, j, lats, lons), place(i + 1, j, lats, lons))
        for i in range(bit, lats - 1, 2)
        for j in range(lons)
    ]
    if bit:
        pairs += [
            (place(lats - 1, j, lats, lons), place(lats - 1, lons - 1 - j, lats, lons))
            for j in range(lons // 2)
        ]
    return both(pairs)


def lon_pairs(lats, lons, bit):
    return both(
        [
            (place(i, j, lats, lons), place(i, j + 1, lats, lons))
            for i in range(lats)
            for j in range(bit, lons, 2)
        ]
    )


def onto_chip(x):
    return pltpu.with_memory_space_constraint(x, pltpu.VMEM)


def off_chip(x):
    return pltpu.with_memory_space_constraint(x, pltpu.HBM)


def rows_kernel(*refs):
    low, high, (near_ref, far_ref), stage = refs[:8], refs[8:16], refs[16:18], refs[18]
    lat = lax.axis_index("lat")
    odd = lat % 2 == 1
    top = lat == lax.axis_size("lat") - 1

    def gather(group, take, dst):
        for kind in range(5):
            for level in range(LEVELS):
                if kind < 4:
                    cells = group[kind][level]
                else:
                    cells = group[4][level] * group[5][level].astype(F32)
                for k, row in enumerate(take):
                    dst[k, kind * LEVELS + level : kind * LEVELS + level + 1, :] = cells[row : row + 1]
        for k, row in enumerate(take):
            dst[k, 20:21, :] = group[6][row : row + 1, :]
            dst[k, 21:22, :] = group[7][row : row + 1, :]

    @pl.when(odd)
    def _():
        gather(low, (0, 1), near_ref)

        @pl.when(jnp.logical_not(top))
        def _():
            gather(high, (6, 7), far_ref)

        @pl.when(top)
        def _():
            gather(high, (6, 5), stage)
            kind_row = lax.broadcasted_iota(jnp.int32, (24, TILE), 0)
            turned = jnp.logical_and(kind_row >= 2 * LEVELS, kind_row < 4 * LEVELS)
            sign = jnp.where(turned, -1.0, 1.0).astype(F32)
            flip = TILE - 1 - lax.broadcasted_iota(jnp.int32, (24, TILE), 1)
            for k in range(2):
                for t in range(COLS // TILE):
                    src = stage[k, :, COLS - TILE * (t + 1) : COLS - TILE * t]
                    rev = jnp.take_along_axis(src, flip, axis=1, mode="promise_in_bounds")
                    far_ref[k, :, TILE * t : TILE * (t + 1)] = rev * sign

    @pl.when(jnp.logical_not(odd))
    def _():
        gather(high, (6, 7), near_ref)
        gather(low, (0, 1), far_ref)


def pack_rows(arrays):
    def spec(a, at):
        if a.ndim == 3:
            return pl.BlockSpec((LEVELS, 8, COLS), lambda i: (0, at, 0))
        return pl.BlockSpec((8, COLS), lambda i: (at, 0))

    whole = pl.BlockSpec((2, 24, COLS), lambda i: (0, 0, 0))
    shape = pltpu.VMEM((2, 24, COLS), F32)
    return pl.pallas_call(
        rows_kernel,
        grid=(1,),
        in_specs=[spec(a, 0) for a in arrays] + [spec(a, ROWS // 8 - 1) for a in arrays],
        out_specs=[pl.BlockSpec(memory_space=pltpu.VMEM)] * 2,
        out_shape=[shape, shape],
        scratch_shapes=[pltpu.VMEM((2, 24, COLS), F32)],
        compiler_params=PARAMS,
        name="pack_rows",
    )(*[off_chip(x) for x in (*arrays, *arrays)])


def slot_of(shape):
    return ((lax.broadcasted_iota(jnp.int32, shape, len(shape) - 1) + 2) & (GROUP - 1)) >> 1


def level_of(shape):
    return ((lax.broadcasted_iota(jnp.int32, shape, len(shape) - 1) + 8) >> 5) & (LEVELS - 1)


def join_ends(low, high):
    lane = lax.broadcasted_iota(jnp.int32, low.shape, len(low.shape) - 1)
    return jnp.where(lane < 8, low, pltpu.roll(high, 16, len(low.shape) - 1))


def spread(parts):
    lane = lax.broadcasted_iota(jnp.int32, (ROWS, TILE), 1)
    whole = parts[0]
    for level in range(1, len(parts)):
        whole = jnp.where(lane >= GROUP * level, pltpu.roll(parts[level], GROUP * level, 1), whole)
    return whole


def windows_kernel(temp, salt, uvel, vvel, thick, land, ewid, nwid, cori, win, packed):
    shape = (ROWS, TILE)
    slot = slot_of(shape)
    ends = (slice(0, TILE), slice(COLS - TILE, COLS))
    total = jnp.zeros(shape, F32)

    def at(kind, level, cut):
        if kind < 4:
            return (temp, salt, uvel, vvel)[kind][level, :, cut]
        if kind == 4:
            return thick[level, :, cut] * land[level, :, cut].astype(F32)
        return (ewid, nwid)[level][:, cut]

    for kind in range(KINDS):
        count = 2 if kind == 5 else LEVELS
        parts = [join_ends(*[at(kind, level, cut) for cut in ends]) for level in range(count)]
        cells = spread(parts)
        win[kind] = cells
        total = jnp.where(slot == 9 + kind, pltpu.roll(cells, 16 + 2 * kind, 1), total)
        total = jnp.where(slot == kind, pltpu.roll(cells, TILE - 16 + 2 * kind, 1), total)
    packed[...] = total


def windows(arrays, coriolis):
    return pl.pallas_call(
        windows_kernel,
        in_specs=[VMEM] * 9,
        out_specs=[VMEM] * 2,
        out_shape=[pltpu.VMEM((KINDS, ROWS, TILE), F32), pltpu.VMEM((ROWS, TILE), F32)],
        compiler_params=PARAMS,
        name="windows",
    )(*[onto_chip(x) for x in (*arrays, coriolis)])


def columns_kernel(packed, near, far, out, ghosts, corner):
    lat = lax.axis_index("lat")
    odd = lat % 2 == 1
    out[0:ROWS, :] = packed[...]
    row = lax.broadcasted_iota(jnp.int32, (24, COLS), 0)
    fill = jnp.logical_and(lat == 0, row >= 20)
    lane = lax.broadcasted_iota(jnp.int32, (24, TILE), 1)
    small_row = lax.broadcasted_iota(jnp.int32, (24, TILE), 0)
    mine = jnp.logical_and(lane >> 5 == small_row & (LEVELS - 1), lane & (GROUP - 1) < 16)
    slot = slot_of((8, TILE))
    kind = lax.broadcasted_iota(jnp.int32, (8, TILE), 0)
    for k in range(2):
        a, b = near[k], far[k]
        for side in range(2):
            if side == 0:
                cells = jnp.where(odd, b, a)
            else:
                cells = jnp.where(fill, 1.0, jnp.where(odd, a, b))
            at = 2 * side + k
            ghosts[at] = cells
            ends = join_ends(cells[:, 0:TILE], cells[:, COLS - TILE : COLS])
            moved = ends
            for level in range(1, LEVELS):
                moved = jnp.where(small_row & (LEVELS - 1) == level, pltpu.roll(ends, GROUP * level, 1), moved)
            ends = jnp.where(mine, moved, 0.0)
            rows = [jnp.sum(ends[LEVELS * i : LEVELS * (i + 1)], axis=0, keepdims=True) for i in range(KINDS)]
            shown = jnp.concatenate(rows + [jnp.zeros((8 - KINDS, TILE), F32)], axis=0)
            corner[at] = shown
            east = pltpu.roll(shown, 16, 1, stride=2, stride_axis=0)
            west = pltpu.roll(shown, TILE - 16, 1, stride=2, stride_axis=0)
            sent = jnp.where(slot == kind + 9, east, jnp.where(slot == kind, west, 0.0))
            out[ROWS + at : ROWS + at + 1, :] = jnp.sum(sent[0:KINDS], axis=0, keepdims=True)
    out[ROWS + 4 : ROWS + 8, :] = jnp.zeros((4, TILE), F32)


def pack_columns(packed, near, far):
    return pl.pallas_call(
        columns_kernel,
        in_specs=[VMEM] * 3,
        out_specs=[VMEM] * 3,
        out_shape=[
            pltpu.VMEM((ROWS + 8, TILE), F32),
            pltpu.VMEM((4, 24, COLS), F32),
            pltpu.VMEM((4, 8, TILE), F32),
        ],
        compiler_params=PARAMS,
        name="pack_columns",
    )(*[onto_chip(x) for x in (packed, near, far)])


def north_of(here, above):
    sub = lax.broadcasted_iota(jnp.int32, here.shape, 0)
    return pltpu.roll(jnp.where(sub == 0, above, here), 7, 0)


def south_of(here, below):
    sub = lax.broadcasted_iota(jnp.int32, here.shape, 0)
    return pltpu.roll(jnp.where(sub == 7, below, here), 1, 0)


def tile(t):
    return slice(TILE * t, TILE * t + TILE)


def turn_e(x):
    return pltpu.roll(x, TILE - 1, 1)


def turn_w(x):
    return pltpu.roll(x, 1, 1)


def around(c):
    r = pl.multiple_of(8 * c, 8)
    up = pl.multiple_of(8 * jnp.minimum(c + 1, CHUNKS - 1), 8)
    down = pl.multiple_of(8 * jnp.maximum(c - 1, 0), 8)
    return pl.ds(r, 8), pl.ds(up, 8), pl.ds(down, 8)


def inner_metric(ewid, nwid, known, over, over_e):
    ratio_e, ratio_n, span_e, span_n, inv_area, half_e, half_n = known
    last = lax.broadcasted_iota(jnp.int32, (8, TILE), 1) == TILE - 1

    def chunk(c, _):
        here, above, _ = around(c)
        east = [(ewid[here, tile(0)], nwid[here, tile(0)])]
        east = [tuple((x, turn_e(x)) for x in east[0])]
        for t in range(TILES):
            (e, re), (n, rn) = east[t]
            u = (t + 1) % TILES
            if u:
                east.append(tuple((x, turn_e(x)) for x in (ewid[here, tile(u)], nwid[here, tile(u)])))
            else:
                east.append(east[0])
            ee = jnp.where(last, east[t + 1][0][1], re)
            ne = jnp.where(last, east[t + 1][1][1], rn)
            en = north_of(e, ewid[above, tile(t)])
            nn = north_of(n, nwid[above, tile(t)])
            ratio_e[here, tile(t)] = (n + ne) / (e + ee)
            ratio_n[here, tile(t)] = (e + en) / (n + nn)
            span_e[here, tile(t)] = flux_scale * (n + ne)
            span_n[here, tile(t)] = flux_scale * (e + en)
            inv_area[here, tile(t)] = 1.0 / (e * n)
            half_e[here, tile(t)] = (0.5 * time_step) / e
            half_n[here, tile(t)] = (0.5 * time_step) / n
            over[here, tile(t)] = jnp.zeros((8, TILE), F32)
            over_e[here, tile(t)] = jnp.zeros((8, TILE), F32)
        return 0

    lax.fori_loop(0, CHUNKS, chunk, 0, unroll=2)


def inner_level(level, fields, outs, known, work, over, over_e, keep):
    temp, salt, uvel, vvel, thick, land, ewid, nwid, cori = fields
    ratio_e, ratio_n, span_e, span_n, inv_area, half_e, half_n = known
    deep, coef_e, coef_n, inv_vol, move_n, flux_t, flux_s, pres, slope, lap = work
    lane = lax.broadcasted_iota(jnp.int32, (8, TILE), 1)
    first, last = lane == 0, lane == TILE - 1
    data = (temp, salt, uvel, vvel)

    for r in range(0, ROWS, 8):
        deep[r : r + 8, :] = thick[level, r : r + 8, :] * land[level, r : r + 8, :].astype(F32)

    def laps(c, _):
        here, above, below = around(c)

        def turned_at(t):
            cells = [x[level, here, tile(t)] for x in data] + [deep[here, tile(t)]]
            return [(x, turn_e(x)) for x in cells]

        def zonal(t, turned, ahead):
            d, rd = turned[4]
            de = jnp.where(last, ahead[4][1], rd)
            lon_thick = jnp.minimum(d, de)
            ce = lon_thick * ratio_e[here, tile(t)]
            east = [jnp.where(last, ahead[f][1], turned[f][1]) for f in range(4)]
            flux = [ce * (east[f] - turned[f][0]) for f in range(4)]
            te = lon_thick * span_e[here, tile(t)] * (turned[2][0] + east[2])
            be = (beta_salt * east[1] - alpha_temp * east[0]) * de
            before = over_e[here, tile(t)]
            pe = before + 0.5 * be
            if keep:
                over_e[here, tile(t)] = before + be
            return ce, flux, te, east, pe

        end, start = turned_at(TILES - 1), turned_at(0)
        kept = zonal(TILES - 1, end, start)
        behind, behind_pe = [turn_w(x) for x in kept[1]], pltpu.roll(kept[4], 2, 1)
        kept_flux, kept_pe = behind, behind_pe
        turned = start
        for t in range(TILES):
            if t < TILES - 1:
                ahead = turned_at(t + 1) if t < TILES - 2 else end
                ce, flux, te, east, pe = zonal(t, turned, ahead)
                turned_flux, turned_pe = [turn_w(x) for x in flux], pltpu.roll(pe, 2, 1)
            else:
                ce, flux, te, east, pe = kept
                turned_flux, turned_pe = kept_flux, kept_pe
            coef_e[here, tile(t)] = ce
            d = turned[4][0]
            dn, ds = north_of(d, deep[above, tile(t)]), south_of(d, deep[below, tile(t)])
            lat_thick = jnp.minimum(d, dn)
            rn = ratio_n[here, tile(t)]
            cn = lat_thick * rn
            cs = jnp.minimum(ds, d) * south_of(rn, ratio_n[below, tile(t)])
            iv = inv_area[here, tile(t)] / jnp.maximum(d, thin_floor)
            coef_n[here, tile(t)] = cn
            inv_vol[here, tile(t)] = iv
            for f in range(4):
                q = turned[f][0]
                qn, qs = north_of(q, data[f][level, above, tile(t)]), south_of(q, data[f][level, below, tile(t)])
                west = jnp.where(first, behind[f], turned_flux[f])
                lap[f, here, tile(t)] = (flux[f] - west + cn * (qn - q) - cs * (q - qs)) * iv
                if f == 3:
                    move_n[here, tile(t)] = lat_thick * span_n[here, tile(t)] * (q + qn)
            q0, q1 = turned[0][0], turned[1][0]
            flux_t[here, tile(t)] = te * (q0 + east[0])
            flux_s[here, tile(t)] = te * (q1 + east[1])
            b = (beta_salt * q1 - alpha_temp * q0) * d
            before = over[here, tile(t)]
            pres[here, tile(t)] = before + 0.5 * b
            if keep:
                over[here, tile(t)] = before + b
            slope[here, tile(t)] = pe - jnp.where(lane < 2, behind_pe, turned_pe)
            behind, behind_pe, turned = turned_flux, turned_pe, ahead
        return 0

    lax.fori_loop(0, CHUNKS, laps, 0, unroll=2)

    def finish(c, _):
        here, above, below = around(c)

        def turned_at(t):
            return [(x, turn_e(x)) for x in (lap[f, here, tile(t)] for f in range(4))]

        def zonal(t, turned, ahead):
            ce = coef_e[here, tile(t)]
            flux = [ce * (jnp.where(last, ahead[f][1], turned[f][1]) - turned[f][0]) for f in range(4)]
            flux[0] = flux[0] + flux_t[here, tile(t)]
            flux[1] = flux[1] + flux_s[here, tile(t)]
            return flux

        end, start = turned_at(TILES - 1), turned_at(0)
        kept = zonal(TILES - 1, end, start)
        kept_turned = [turn_w(x) for x in kept]
        behind, turned = kept_turned, start
        for t in range(TILES):
            if t < TILES - 1:
                ahead = turned_at(t + 1) if t < TILES - 2 else end
                flux = zonal(t, turned, ahead)
                turned_flux = [turn_w(x) for x in flux]
            else:
                flux, turned_flux = kept, kept_turned
            cn = coef_n[here, tile(t)]
            cs = south_of(cn, coef_n[below, tile(t)])
            iv = biharm_coef * inv_vol[here, tile(t)]
            gn = move_n[here, tile(t)]
            gs = south_of(gn, move_n[below, tile(t)])
            wet = land[level, here, tile(t)].astype(F32)
            u, v = uvel[level, here, tile(t)], vvel[level, here, tile(t)]
            turning = time_step * cori[here, tile(t)]
            for f in range(4):
                m = turned[f][0]
                mn, ms = north_of(m, lap[f, above, tile(t)]), south_of(m, lap[f, below, tile(t)])
                west = jnp.where(first, behind[f], turned_flux[f])
                total = flux[f] - west + cn * (mn - m) - cs * (m - ms)
                if f < 2:
                    q = data[f][level, here, tile(t)]
                    qn, qs = north_of(q, data[f][level, above, tile(t)]), south_of(q, data[f][level, below, tile(t)])
                    total = total + gn * (q + qn) - gs * (qs + q)
                    change = wet * (q - total * iv)
                elif f == 2:
                    change = wet * (u + turning * v - slope[here, tile(t)] * half_e[here, tile(t)] - total * iv)
                else:
                    p = pres[here, tile(t)]
                    rise = north_of(p, pres[above, tile(t)]) - south_of(p, pres[below, tile(t)])
                    change = wet * (v - turning * u - rise * half_n[here, tile(t)] - total * iv)
                outs[f][level, here, tile(t)] = change
            behind, turned = turned_flux, ahead
        return 0

    lax.fori_loop(0, CHUNKS, finish, 0, unroll=2)


WORK = [pltpu.VMEM((ROWS, COLS), F32)] * 9 + [pltpu.VMEM((4, ROWS, COLS), F32)]


def inner_kernel(*refs):
    fields, outs, known, over, over_e, work = refs[:9], refs[9:13], refs[13:20], refs[20], refs[21], refs[22:]
    level = pl.program_id(0)

    @pl.when(level == 0)
    def _():
        inner_metric(fields[6], fields[7], known, over, over_e)

    @pl.when(jnp.logical_or(level < AHEAD, near_fold()))
    def _():
        inner_level(level, fields, outs, known, work, over, over_e, True)


def inner(arrays, coriolis):
    out = [pltpu.VMEM((LEVELS, ROWS, COLS), F32)] * 4 + [pltpu.VMEM((ROWS, COLS), F32)] * 9
    done = pl.pallas_call(
        inner_kernel,
        grid=(AHEAD + 1,),
        in_specs=[VMEM] * 9,
        out_specs=[VMEM] * 13,
        out_shape=out,
        scratch_shapes=WORK,
        compiler_params=PARAMS,
        name="inner",
    )(*[onto_chip(x) for x in (*arrays, coriolis)])
    return done[:4], done[4:]


def metric(e, n, lanes, rows):
    ee, ne, en, nn = lanes(e, 1), lanes(n, 1), rows(e, 1), rows(n, 1)
    return (
        (n + ne) / (e + ee),
        (e + en) / (n + nn),
        flux_scale * (n + ne),
        flux_scale * (e + en),
        1.0 / (e * n),
        (0.5 * time_step) / e,
        (0.5 * time_step) / n,
    )


def patch(cells, d, wet, cori, known, overhead, lanes, rows):
    ratio_e, ratio_n, span_e, span_n, inv_area, half_e, half_n = known
    temp, salt, uvel, vvel = cells
    de, dn = lanes(d, 1), rows(d, 1)
    lon_thick, lat_thick = jnp.minimum(d, de), jnp.minimum(d, dn)
    ce, cn = lon_thick * ratio_e, lat_thick * ratio_n
    cs = rows(cn, -1)
    iv = inv_area / jnp.maximum(d, thin_floor)
    b = (beta_salt * salt - alpha_temp * temp) * d
    p = overhead(b) + 0.5 * b
    ge = (lanes(p, 1) - lanes(p, -1)) * half_e
    gn = (rows(p, 1) - rows(p, -1)) * half_n
    outs = []
    te = tn = None
    for f in (2, 3, 0, 1):
        q = cells[f]
        qe, qn, qs = lanes(q, 1), rows(q, 1), rows(q, -1)
        if f == 2:
            te = lon_thick * span_e * (q + qe)
        if f == 3:
            tn = lat_thick * span_n * (q + qn)
            ts = rows(tn, -1)
        fe = ce * (qe - q)
        m = (fe - lanes(fe, -1) + cn * (qn - q) - cs * (q - qs)) * iv
        fe = ce * (lanes(m, 1) - m)
        if f < 2:
            fe = fe + te * (q + qe)
        total = fe - lanes(fe, -1) + cn * (rows(m, 1) - m) - cs * (m - rows(m, -1))
        if f < 2:
            total = total + tn * (q + qn) - ts * (qs + q)
        change = q - biharm_coef * iv * total
        if f == 2:
            change = change + time_step * cori * vvel - ge
        if f == 3:
            change = change - time_step * cori * uvel - gn
        outs.append(wet * change)
    return outs[2], outs[3], outs[0], outs[1]


def rims_level(level, fields, ghosts, outs, known, spin, over):
    temp, salt, uvel, vvel, thick, land, ewid, nwid, cori = fields
    sub = lax.broadcasted_iota(jnp.int32, (8, COLS), 0)
    low, high = slice(0, 8), slice(ROWS - 8, ROWS)

    def lanes(x, by):
        return pltpu.roll(x, COLS - 1 if by > 0 else 1, 2)

    def rows(x, by):
        return pltpu.roll(x, 7 if by > 0 else 1, 1)

    def strips(f, south, north):
        g = [ghosts[k, pl.ds(f, 1), :] for k in range(4)]
        s = jnp.where(sub == 0, g[2], jnp.where(sub == 1, g[3], pltpu.roll(south, 2, 0)))
        n = jnp.where(sub == 6, g[0], jnp.where(sub == 7, g[1], pltpu.roll(north, 6, 0)))
        return jnp.stack([s, n])

    def own(south, north):
        return jnp.stack([pltpu.roll(south, 2, 0), pltpu.roll(north, 6, 0)])

    @pl.when(level == 0)
    def _():
        e = strips(20, ewid[low, :], ewid[high, :])
        n = strips(21, nwid[low, :], nwid[high, :])
        for i, x in enumerate(metric(e, n, lanes, rows)):
            known[i] = x
        spin[...] = own(cori[low, :], cori[high, :])
        over[...] = jnp.zeros((2, 8, COLS), F32)

    cells = [
        strips(LEVELS * kind + level, x[level, low, :], x[level, high, :])
        for kind, x in enumerate((temp, salt, uvel, vvel))
    ]
    wet_low, wet_high = land[level, low, :].astype(F32), land[level, high, :].astype(F32)
    d = strips(4 * LEVELS + level, thick[level, low, :] * wet_low, thick[level, high, :] * wet_high)

    def overhead(b):
        before = over[...]
        over[...] = before + b
        return before

    new = patch(
        cells, d, own(wet_low, wet_high), spin[...], [known[i] for i in range(7)], overhead, lanes, rows
    )
    for x, (old, out) in zip(new, outs):
        out[level, low, :] = jnp.where(sub < 2, pltpu.roll(x[0], 6, 0), old[level, low, :])
        out[level, high, :] = jnp.where(sub >= 6, pltpu.roll(x[1], 2, 0), old[level, high, :])


def near_fold():
    return lax.axis_index("lat") >= lax.axis_size("lat") - 2


def runs_early():
    return jnp.logical_and(lax.axis_index("lon") < 2, lax.axis_index("lat") < lax.axis_size("lat") - 1)


def middle_kernel(*refs):
    fields, known, outs, over, over_e, work = refs[:9], refs[9:16], refs[22:26], refs[26], refs[27], refs[28:]

    @pl.when(runs_early())
    def _():
        level = AHEAD + near_fold().astype(jnp.int32)
        inner_level(level, fields, outs, known, work, over, over_e, True)


def rims_kernel(*refs):
    fields, known, ghosts, outs, over, over_e = refs[:9], refs[9:16], refs[18], refs[23:27], refs[27], refs[28]
    still, rim_known, spin, rim_over, work = refs[29], refs[30], refs[31], refs[32], refs[33:]
    level = pl.program_id(0)

    @pl.when(level == 0)
    def _():
        ends = (slice(0, TILE), slice(COLS - TILE, COLS))
        still[0] = spread([join_ends(*[fields[5][at, :, cut].astype(F32) for cut in ends]) for at in range(LEVELS)])
        still[1] = spread([join_ends(*[fields[8][:, cut] for cut in ends])] * LEVELS)

        def one(at, _):
            inner_level(at, fields, outs, known, work, over, over_e, True)
            return 0

        done = AHEAD + runs_early().astype(jnp.int32) + near_fold().astype(jnp.int32)
        lax.fori_loop(done, LEVELS, one, 0)

    rims_level(level, fields, ghosts, list(zip(outs, outs)), rim_known, spin, rim_over)


WHOLE = [pltpu.VMEM((LEVELS, ROWS, COLS), F32)] * 4 + [pltpu.VMEM((ROWS, COLS), F32)] * 2


def middle(arrays, coriolis, known, outs):
    done = pl.pallas_call(
        middle_kernel,
        in_specs=[VMEM] * 22,
        out_specs=[VMEM] * 6,
        out_shape=WHOLE,
        scratch_shapes=WORK,
        input_output_aliases={16: 4, 17: 5, 18: 0, 19: 1, 20: 2, 21: 3},
        compiler_params=PARAMS,
        name="middle",
    )(*[onto_chip(x) for x in (*arrays, coriolis, *known, *outs)])
    return done[:4], (*known[:7], *done[4:])


def rims(arrays, coriolis, known, ghosts, outs):
    done = pl.pallas_call(
        rims_kernel,
        grid=(LEVELS,),
        in_specs=[VMEM] * 23,
        out_specs=[VMEM] * 7,
        out_shape=WHOLE + [pltpu.VMEM((2, ROWS, TILE), F32)],
        scratch_shapes=[
            pltpu.VMEM((7, 2, 8, COLS), F32),
            pltpu.VMEM((2, 8, COLS), F32),
            pltpu.VMEM((2, 8, COLS), F32),
        ]
        + WORK,
        input_output_aliases={16: 4, 17: 5, 19: 0, 20: 1, 21: 2, 22: 3},
        compiler_params=PARAMS,
        name="rims",
    )(*[onto_chip(x) for x in (*arrays, coriolis, *known, ghosts, *outs)])
    return done[:4], done[6]


def sides_kernel(
    win, still, corner, lon_even, lon_odd, temp_in, salt_in, uvel_in, vvel_in,
    temp_out, salt_out, uvel_out, vvel_out,
    side, edges, mid_sem, low_sem, high_sem,
):
    ins, outs = (temp_in, salt_in, uvel_in, vvel_in), (temp_out, salt_out, uvel_out, vvel_out)
    shape = (TALL, TILE)
    level, slot = level_of(shape), slot_of(shape)
    ghost_lane = jnp.logical_or(slot == 0, slot == 9)
    middle = pl.ds(TILE, COLS - 2 * TILE)

    def middle_copy(i):
        return pltpu.make_async_copy(ins[i].at[:, :, middle], outs[i].at[:, :, middle], mid_sem.at[i])

    def low_copy(i):
        return pltpu.make_async_copy(edges.at[0, i], outs[i].at[:, :, pl.ds(0, TILE)], low_sem.at[i])

    def high_copy(i):
        return pltpu.make_async_copy(edges.at[1, i], outs[i].at[:, :, pl.ds(COLS - TILE, TILE)], high_sem.at[i])

    for i in range(4):
        middle_copy(i).start()

    def lanes(x, by):
        return pltpu.roll(x, TILE - 1 if by > 0 else 1, 1)

    def rows(x, by):
        return pltpu.roll(x, TALL - 1 if by > 0 else 1, 0)

    def tall(body, north, south):
        pad = jnp.zeros((6, TILE), F32)
        return jnp.concatenate([pad, south, body, north, pad], axis=0)

    odd = lax.axis_index("lon") % 2 == 1
    a, b = lon_even[...], lon_odd[...]
    got = jnp.where(slot_of((ROWS + 8, TILE)) >= 9, jnp.where(odd, b, a), jnp.where(odd, a, b))
    side[...] = tall(got[0:ROWS], got[ROWS : ROWS + 2], got[ROWS + 2 : ROWS + 4])

    def extended(kind):
        ends = [jnp.concatenate([corner[k, kind : kind + 1, :] for k in pair], axis=0) for pair in ((0, 1), (2, 3))]
        came = side[...]
        if kind:
            came = pltpu.roll(came, TILE - 2 * kind, 1)
        return jnp.where(ghost_lane, came, tall(win[kind], *ends))

    def everywhere(x):
        return jnp.where(level < 2, x, pltpu.roll(x, 2 * GROUP, 1))

    pair = extended(5)
    e = everywhere(jnp.where(level == 0, pair, pltpu.roll(pair, GROUP, 1)))
    n = everywhere(jnp.where(level == 0, pltpu.roll(pair, TILE - GROUP, 1), pair))

    def overhead(b):
        total = jnp.where(level > 0, pltpu.roll(b, GROUP, 1), 0.0)
        for up in (2, 3):
            total = total + jnp.where(level >= up, pltpu.roll(b, GROUP * up, 1), 0.0)
        return total

    cells = [extended(kind) for kind in range(4)]
    blank = jnp.zeros((2, TILE), F32)
    wet, spin = tall(still[0], blank, blank), tall(still[1], blank, blank)
    new = patch(cells, extended(4), wet, spin, metric(e, n, lanes, rows), overhead, lanes, rows)
    lane = lax.broadcasted_iota(jnp.int32, (ROWS, TILE), 1)
    for i, x in enumerate(new):
        x = x[8 : 8 + ROWS]
        x = jnp.where(lane & (GROUP - 1) < 8, x, pltpu.roll(x, TILE - 16, 1))
        for at in range(LEVELS):
            own = pltpu.roll(x, TILE - GROUP * at, 1) if at else x
            edges[0, i, at] = jnp.where(lane < 2, own, ins[i][at, :, 0:TILE])
            edges[1, i, at] = jnp.where(lane >= TILE - 2, own, ins[i][at, :, COLS - TILE : COLS])
        low_copy(i).start()
        high_copy(i).start()
    for i in range(4):
        middle_copy(i).wait()
        low_copy(i).wait()
        high_copy(i).wait()


def sides(win, still, corner, lon_even, lon_odd, outs):
    return pl.pallas_call(
        sides_kernel,
        in_specs=[VMEM] * 9,
        out_specs=[pl.BlockSpec(memory_space=pltpu.HBM)] * 4,
        out_shape=[jax.ShapeDtypeStruct((LEVELS, ROWS, COLS), F32)] * 4,
        scratch_shapes=[
            pltpu.VMEM((TALL, TILE), F32),
            pltpu.VMEM((2, 4, LEVELS, ROWS, TILE), F32),
            pltpu.SemaphoreType.DMA((4,)),
            pltpu.SemaphoreType.DMA((4,)),
            pltpu.SemaphoreType.DMA((4,)),
        ],
        compiler_params=PARAMS,
        name="sides",
    )(*[onto_chip(x) for x in (win, still, corner, lon_even, lon_odd, *outs)])


def shards(temp, salt, uvel, vvel, thick, land, east_width, north_width, coriolis):
    lats, lons = lax.axis_size("lat"), lax.axis_size("lon")
    arrays = (temp, salt, uvel, vvel, thick, land, east_width, north_width)
    near, far = pack_rows(arrays)
    near = lax.ppermute(near, AXES, lat_pairs(lats, lons, 0))
    far = lax.ppermute(far, AXES, lat_pairs(lats, lons, 1))
    win, packed = windows(arrays, coriolis)
    outs, known = inner(arrays, coriolis)
    near, far, packed, *outs = lax.optimization_barrier((near, far, packed, *outs))
    packed, ghosts, corner = pack_columns(packed, near, far)
    outs, known = middle(arrays, coriolis, known, outs)
    packed, *outs = lax.optimization_barrier((packed, *outs))
    lon_odd = lax.ppermute(packed, AXES, lon_pairs(lats, lons, 1))
    lon_even = lax.ppermute(packed, AXES, lon_pairs(lats, lons, 0))
    outs, still = rims(arrays, coriolis, known, ghosts, outs)
    return tuple(sides(win, still, corner, lon_even, lon_odd, outs))


def solution(mesh):
    deep, flat = P(None, "lat", "lon"), P("lat", "lon")
    return jax.shard_map(
        shards,
        mesh=mesh,
        in_specs=(deep,) * 6 + (flat,) * 3,
        out_specs=(deep,) * 4,
        check_vma=False,
    )
```
